32 devices in a mesh: dp: 4 (over x, core), seq: 8 (over z, y).
Axes of the slice: x: 2, y: 2, z: 4, core: 2. Of those that a mesh axis runs over, the one named last changes fastest.
Arguments:
- tokens: bfloat16 [8, 1024, 2048], P('dp', 'seq'), may hold values from -6 to 6
- segments: int32 [8, 1024], P('dp'), may hold values from 0 to 5, never falling along the last dimension, each value on 1 to 256 neighbouring positions
- routes: int32 [8, 1024, 8], P('dp', 'seq'), may hold values from 0 to 31, as said below
- cotangent: bfloat16 [8, 1024, 2048], P('dp', 'seq'), may hold values from -6 to 6
- attn_weight: bfloat16 [2048, 4, 2048], P(('dp', 'seq')), may hold values from -0.5 to 0.5
- router_weight: bfloat16 [2048, 32], P(('dp', 'seq')), may hold values from -0.0625 to 0.0625
- norm_gains: bfloat16 [4, 2048], P(None, ('dp', 'seq')), may hold values from 0.5 to 1.5
- expert_in: bfloat16 [32, 2048, 2, 1024], P('seq', 'dp'), may hold values from -0.125 to 0.125
- expert_out: bfloat16 [32, 1024, 2048], P('seq', None, 'dp'), may hold values from -6 to 6
Outputs:
- block_out: bfloat16 [8, 1024, 2048], P('dp', 'seq')
- input_grad: float32 [8, 1024, 2048], P('dp', 'seq')
- attn_grad: float32 [2048, 4, 2048], P(('dp', 'seq'))
- router_grad: float32 [2048, 32], P(('dp', 'seq'))
- gain_grad: float32 [4, 2048], P(None, ('dp', 'seq'))
- expert_in_grad: float32 [32, 2048, 2, 1024], P('seq', 'dp')
- expert_out_grad: float32 [32, 1024, 2048], P('seq', None, 'dp')
The draws below stay inside these ranges and needn't reach their ends.
Inputs may be any that keep to these rules, and one draw needn't show every extreme that they name: `segments`: block numbers never fall along a sequence; each block has at most 256 positions. `routes`: each token names 8 different experts.
All inputs are finite; a program needn't handle non-finite values.
Results may differ from the reference program's by a relative error of at most 0.02.
Values may be sent and summed in bfloat16 or wider, within the bound.
A program may use at most 384 MiB of HBM per device.

```python
import math
import jax
import jax.numpy as jnp
import numpy as np
from jax import lax

D = 2048
HEADS = 16
HEAD_DIM = 128
FF = 1024
TOP = 8
LEN = 1024
SEQS = 2
SEG_MOST = 256
SEG_COUNT = 6
EXPERTS = 32
SEQUENCES = 8
CAP = 72
N_DP = 4
N_SEQ = 8


def draw_routes(key, part):
    pop_key = jax.random.fold_in(key, 11)
    tok_key = jax.random.fold_in(key, 23)
    popular = jax.random.randint(pop_key, (EXPERTS,), 0, 2048)
    fresh = jax.random.randint(tok_key, (SEQUENCES, LEN, EXPERTS), 0, 4096)
    scores = (fresh + popular[None, None, :]) * EXPERTS + jnp.arange(EXPERTS, dtype=jnp.int32)[None, None, :]
    picked = jax.lax.top_k(scores, TOP)[0]
    return (picked % EXPERTS).astype(jnp.int32)


def block_levels(key, dims, shards, low, largest):
    def one(axis_at, shards_of):
        steps = jax.random.uniform(jax.random.fold_in(jax.random.fold_in(key, 6), axis_at), (shards_of,), jnp.float32, low / len(shards), largest / len(shards))
        return jnp.repeat(jnp.exp(steps), dims[axis_at] // shards_of).reshape((-1,) + (1,) * (len(dims) - axis_at - 1))

    loudness = one(*shards[0])
    for cut in shards[1:]:
        loudness = loudness * one(*cut)
    return loudness


def profile(count, total, reach, slope):
    portions = [(1 << 20) // math.isqrt(rank ** slope) + 1 for rank in range(2, count + 1)]
    spare, holding = total - reach - (count - 1), [1] * (count - 1)
    while spare > 0:
        movable = [i for i in range(count - 1) if holding[i] < reach]
        mass, remaining = sum([portions[i] for i in movable]), spare
        for i in movable:
            more = min(reach - holding[i], max(1, remaining * portions[i] // mass), spare)
            holding[i] = holding[i] + more
            spare = spare - more
    return np.array([reach] + holding)


def uneven_parts(rng, amount, total, most, slope):
    if amount == 2:
        one = jax.random.randint(rng, (), max(1, total - most), min(most, total - 1) + 1)
        return jnp.stack([one, total - one])
    lengths = jnp.asarray(profile(amount, total, most, slope), jnp.int32)
    couples = (amount - 1) // 2
    source_of, taker = lengths[1:1 + 2 * couples:2], lengths[2:2 + 2 * couples:2]
    room = jnp.minimum(source_of - 1, most - taker)
    moved = jax.random.randint(jax.random.fold_in(rng, 1), (couples,), 0, 1 << 20) % (room + 1)
    lengths = lengths.at[1:1 + 2 * couples:2].set(source_of - moved).at[2:2 + 2 * couples:2].set(taker + moved)
    return lengths[jax.random.permutation(jax.random.fold_in(rng, 2), amount)]


def bell_draw(own_key, extent, deviation, bound, cuts=(), kind=jnp.bfloat16):
    entries = jax.random.normal(own_key, extent, jnp.float32) * deviation
    if len(cuts) > 0:
        entries = block_levels(own_key, extent, cuts, -0.22, 0.18) * entries
    return jnp.clip(entries, min=-bound, max=bound).astype(kind)


def setup_inputs(seed: int = 0) -> dict:
    key_list = jax.random.split(jax.random.key(seed), 10)
    return {
        "tokens": bell_draw(key_list[0], (SEQUENCES, LEN, D), 1.0, 6.0, ((0, 4), (1, 8))),
        "segments": jax.vmap(lambda own: jnp.searchsorted(jnp.cumsum(uneven_parts(own, SEG_COUNT, LEN, SEG_MOST, 1)), jnp.arange(LEN), side="right"))(jax.random.split(key_list[1], SEQUENCES)).reshape((SEQUENCES, LEN)).astype(jnp.int32),
        "routes": draw_routes(jax.random.fold_in(key_list[9], 71), 0),
        "cotangent": bell_draw(key_list[3], (SEQUENCES, LEN, D), 1.0, 6.0, ((0, 4), (1, 8))),
        "attn_weight": bell_draw(key_list[4], (D, 4, D), (D // 16) ** -0.5, 0.5, ((0, 32),)),
        "router_weight": bell_draw(key_list[5], (D, EXPERTS), (4 * D) ** -0.5, 0.0625, ((0, 32),)),
        "norm_gains": jnp.clip(1.0 + 0.1 * jax.random.normal(key_list[6], (4, D), jnp.float32), 0.5, 1.5).astype(jnp.bfloat16),
        "expert_in": bell_draw(key_list[7], (EXPERTS, D, 2, FF), D ** -0.5, 0.125, ((0, 8), (1, 4))),
        "expert_out": bell_draw(key_list[8], (EXPERTS, FF, D), 1 ** -0.5, 6.0, ((0, 8), (2, 4))),
    }


NORM_EPS = 1e-05
ROPE_BASE = 10000.0
MASKED_SCORE = -1e+30

@jax.custom_vjp
def low(v):
    return lax.optimization_barrier(v.astype(jnp.bfloat16)).astype(jnp.float32)

@jax.custom_vjp
def low_back(v):
    return v

def low_keep(v):
    return (low(v), None)

def low_pass(kept, grad):
    return (grad,)

def back_keep(v):
    return (v, None)

def back_low(kept, grad):
    return (low(grad),)
low.defvjp(low_keep, low_pass)
low_back.defvjp(back_keep, back_low)

def rms_scale(values, gain_row):
    return values * lax.rsqrt(lax.optimization_barrier(jnp.mean(values * values, axis=-1, keepdims=True)) + NORM_EPS) * gain_row

def rotary(positions):
    half_dim = HEAD_DIM // 2
    freqs = jnp.exp(-math.log(ROPE_BASE) * (2.0 * jnp.arange(half_dim, dtype=jnp.float32) / HEAD_DIM))
    angles = positions.astype(jnp.float32)[:, None] * freqs[None, :]
    return (jnp.cos(angles)[:, None, :], jnp.sin(angles)[:, None, :])

def rotate(values, cosine, sine):
    half_dim = values.shape[-1] // 2
    first = values[..., :half_dim]
    second = values[..., half_dim:]
    return jnp.concatenate([first * cosine - second * sine, second * cosine + first * sine], axis=-1)

def attend_ref(pieces):
    queries, key_rows, value_rows, seg_ids = pieces
    score_scale = HEAD_DIM ** (-0.5)
    scores = low_back(jnp.einsum('qhd,khd->hqk', queries, key_rows, precision=lax.Precision.HIGHEST) * score_scale)
    allowed = seg_ids[None, :] <= seg_ids[:, None]
    attn_probs = jax.nn.softmax(jnp.where(allowed[None], scores, MASKED_SCORE), axis=-1)
    return jnp.einsum('hqk,khd->qhd', low(attn_probs), value_rows, precision=lax.Precision.HIGHEST)

def expert_ref(pieces):
    expert_rows, weight_in, weight_out = pieces
    gate_up = low_back(jnp.einsum('rd,djf->rjf', expert_rows, weight_in, precision=lax.Precision.HIGHEST))
    hidden = low(jax.nn.silu(gate_up[:, 0]) * gate_up[:, 1])
    return low(low_back(jnp.dot(hidden, weight_out, precision=lax.Precision.HIGHEST)))

def block_forward(resid_in, attention_matrix, router_matrix, gain_rows, exp_in, exp_out, seg_ids, route_ids):
    num_seqs = resid_in.shape[0]
    local_len = LEN // N_SEQ
    normalized_rows = low(rms_scale(resid_in, gain_rows[0]))
    projected_rows = jnp.einsum('gco,okt->kgct', normalized_rows, attention_matrix[:, :3], precision=lax.Precision.HIGHEST)
    query_raw = low_back(projected_rows[0])
    key_raw = low_back(projected_rows[1])
    value_raw = projected_rows[2]
    cosine, sine = rotary(jnp.arange(LEN))

    def to_heads(values):
        return values.reshape(num_seqs, LEN, HEADS, HEAD_DIM)
    queries = low(low_back(rotate(to_heads(rms_scale(query_raw, gain_rows[1])), cosine, sine)))
    key_rows = low(low_back(rotate(to_heads(rms_scale(key_raw, gain_rows[2])), cosine, sine)))
    value_rows = low(low_back(to_heads(value_raw)))
    attended = lax.map(jax.checkpoint(attend_ref), (queries, key_rows, value_rows, seg_ids))
    attention_result = low(low_back(attended.reshape(num_seqs, LEN, D)))
    residual_branch = low_back(jnp.einsum('tav,vm->tam', attention_result, attention_matrix[:, 3], precision=lax.Precision.HIGHEST))
    middle = resid_in + residual_branch
    feedforward_input = low(rms_scale(middle, gain_rows[3]))
    router_scores = low_back(jnp.einsum('tav,vm->tam', feedforward_input, router_matrix, precision=lax.Precision.HIGHEST))
    route_probs = jax.nn.softmax(router_scores, axis=-1)

    def by_source(values):
        last_dim = values.shape[-1]
        split = values.reshape(num_seqs, N_SEQ, local_len, last_dim)
        return jnp.swapaxes(split, 0, 1).reshape(N_SEQ, num_seqs * local_len, last_dim)
    source_in = by_source(feedforward_input)
    source_probs = by_source(route_probs)
    source_routes = by_source(route_ids).astype(jnp.int32)
    pair_gate = jnp.take_along_axis(source_probs, source_routes, axis=-1)
    route_hit = (source_routes[..., None] == jnp.arange(EXPERTS, dtype=jnp.int32)).astype(jnp.int32)
    expert_hits = lax.optimization_barrier(jnp.sum(route_hit, axis=2))
    earlier_hits = jnp.cumsum(expert_hits, axis=1) - expert_hits
    pair_slot = jnp.take_along_axis(earlier_hits, source_routes, axis=-1)
    slot_index = jnp.where(pair_slot < CAP, pair_slot, CAP).astype(jnp.int32)
    source_index = jnp.broadcast_to(jnp.arange(N_SEQ, dtype=jnp.int32)[:, None, None], source_routes.shape)
    pair_rows = low_back(jnp.broadcast_to(source_in[:, :, None, :], source_routes.shape + (D,)))
    buffer = jnp.zeros((EXPERTS, N_SEQ, CAP + 1, D), jnp.float32).at[source_routes, source_index, slot_index].add(pair_rows)
    expert_rows = buffer[:, :, :CAP].reshape(EXPERTS, N_SEQ * CAP, D)
    expert_outs = lax.map(jax.checkpoint(expert_ref), (expert_rows, exp_in, exp_out))
    padded = jnp.concatenate([expert_outs.reshape(EXPERTS, N_SEQ, CAP, D), jnp.zeros((EXPERTS, N_SEQ, 1, D), jnp.float32)], axis=2)
    pair_out = padded[source_routes, source_index, slot_index]
    mixed = lax.optimization_barrier(jnp.sum(pair_gate[..., None] * pair_out, axis=2))
    mixed = jnp.swapaxes(mixed.reshape(N_SEQ, num_seqs, local_len, D), 0, 1).reshape(num_seqs, LEN, D)
    return middle + mixed

def reference(tokens, segments, routes, cotangent, attn_weight, router_weight, norm_gains, expert_in, expert_out):
    weights = tuple((param.astype(jnp.float32) for param in (attn_weight, router_weight, norm_gains, expert_in, expert_out)))
    group_in = tokens.astype(jnp.float32).reshape(N_DP, SEQS, LEN, D)
    group_cot = cotangent.astype(jnp.float32).reshape(N_DP, SEQS, LEN, D)
    group_seg = segments.reshape(N_DP, SEQS, LEN)
    group_route = routes.reshape(N_DP, SEQS, LEN, TOP)

    def one_group(totals, pieces):
        resid_in, cot_in, seg_ids, route_ids = pieces

        def forward(values, *params):
            return block_forward(values, *params, seg_ids, route_ids)
        layer_out, pull_back = jax.vjp(forward, resid_in, *weights)
        grad_list = pull_back(cot_in)
        new_totals = tuple((total_sum + grad_part for total_sum, grad_part in zip(totals, grad_list[1:])))
        return (new_totals, (layer_out.astype(jnp.bfloat16), grad_list[0]))
    zeros_init = tuple((jnp.zeros_like(param) for param in weights))
    totals, (layer_out, input_grad) = lax.scan(one_group, zeros_init, (group_in, group_cot, group_seg, group_route))
    return (layer_out.reshape(SEQUENCES, LEN, D), input_grad.reshape(SEQUENCES, LEN, D), totals[0], totals[1], totals[2], totals[3], totals[4])
```

```python
import math

import jax
import jax.numpy as jnp
from jax import lax
from jax.experimental import pallas as pl
from jax.experimental.pallas import tpu as pltpu
from jax.sharding import PartitionSpec as P

HEADS = 16
HEAD_DIM = 128
NORM_EPS = 1e-05
ROPE_BASE = 10000.0
MASKED_SCORE = -1e30
BF = jnp.bfloat16
F32 = jnp.float32
MESH = pl.DeviceIdType.MESH
VMEM_MOST = 60 << 20


def grid_of(seq_size):
    lines = 4 if seq_size % 4 == 0 else 1
    return lines, seq_size // lines


def greet(targets):
    barrier = pltpu.get_barrier_semaphore()
    count = 0
    for cond, device in targets:

        @pl.when(cond)
        def _(device=device):
            pl.semaphore_signal(barrier, 1, device_id=device, device_id_type=MESH)

        count = count + cond.astype(jnp.int32)
    pl.semaphore_wait(barrier, count)


def neighbours(dp, z, y, nz, ny):
    return {
        ("z", 1): (z < nz - 1, (dp, (z + 1) * ny + y)),
        ("z", -1): (z > 0, (dp, (z - 1) * ny + y)),
        ("y", 1): (y < ny - 1, (dp, z * ny + y + 1)),
        ("y", -1): (y > 0, (dp, z * ny + y - 1)),
    }


def seq_gather(block, collective_id, pieces=2):
    rows, width = block.shape
    seq = lax.axis_size("seq")
    nz, ny = grid_of(seq)
    part = rows // pieces

    def kernel(x_ref, o_ref, send_sem, recv_sem, local_sem):
        dp, me = lax.axis_index("dp"), lax.axis_index("seq")
        z, y = lax.div(me, ny), lax.rem(me, ny)
        near = neighbours(dp, z, y, nz, ny)
        greet(list(near.values()))
        own = pltpu.make_async_copy(x_ref, o_ref.at[me], local_sem)
        own.start()
        sent = []
        names = list(near)

        def cut(h):
            return pl.ds(h * part, part)

        def copy(src, origin, h, name):
            return pltpu.make_async_remote_copy(
                src_ref=src,
                dst_ref=o_ref.at[origin, cut(h)],
                send_sem=send_sem.at[origin, h, names.index(name)],
                recv_sem=recv_sem.at[origin, h],
                device_id=near[name][1],
                device_id_type=MESH,
            )

        def send(src, origin, h, name, cond):
            ok = jnp.logical_and(cond, near[name][0])
            pl.when(ok)(lambda: copy(src, origin, h, name).start())
            sent.append((ok, src, origin, h, name))

        def arrive(origin, h, cond):
            @pl.when(cond)
            def _():
                copy(o_ref.at[origin, cut(h)], origin, h, names[0]).wait_recv()

        always = z >= 0
        for h in range(pieces):
            for name in names:
                send(x_ref.at[cut(h)], me, h, name, always)
        for far in range(1, nz):
            for h in range(pieces):
                for sign in (1, -1):
                    zz = z - sign * far
                    cond = jnp.logical_and(zz >= 0, zz < nz)
                    origin = lax.select(cond, zz * ny + y, me)
                    arrive(origin, h, cond)
                    for name in (("z", sign), ("y", 1), ("y", -1)):
                        send(o_ref.at[origin, cut(h)], origin, h, name, cond)
        for side in range(1, ny):
            for far in range(nz):
                for h in range(pieces):
                    for sign in (1, -1) if far else (1,):
                        zz = z - sign * far
                        for turn in (1, -1):
                            yy = y - turn * side
                            cond = (zz >= 0) & (zz < nz) & (yy >= 0) & (yy < ny)
                            origin = lax.select(cond, zz * ny + yy, me)
                            arrive(origin, h, cond)
                            if side < ny - 1:
                                send(o_ref.at[origin, cut(h)], origin, h, ("y", turn), cond)
        for ok, src, origin, h, name in sent:
            pl.when(ok)(lambda: copy(src, origin, h, name).wait_send())
        own.wait()

    return pl.pallas_call(
        kernel,
        out_shape=jax.ShapeDtypeStruct((seq, rows, width), block.dtype),
        in_specs=[pl.BlockSpec(memory_space=pl.ANY)],
        out_specs=pl.BlockSpec(memory_space=pl.ANY),
        scratch_shapes=[
            pltpu.SemaphoreType.DMA((seq, pieces, 4)),
            pltpu.SemaphoreType.DMA((seq, pieces)),
            pltpu.SemaphoreType.DMA,
        ],
        compiler_params=pltpu.CompilerParams(collective_id=collective_id, has_side_effects=True),
        name="seq_gather",
    )(block)


def seq_reduce(terms, collective_id, pieces=2):
    seq, rows, width = terms.shape
    nz, ny = grid_of(seq)
    part = rows // pieces
    sides = 1 if ny == 2 else 2
    strip = 16

    def kernel(p_ref, o_ref, acc, from_y, from_z, send_sem, ysem, zsem):
        dp, me = lax.axis_index("dp"), lax.axis_index("seq")
        z, y = lax.div(me, ny), lax.rem(me, ny)
        near = neighbours(dp, z, y, nz, ny)
        names = list(near)
        greet(list(near.values()))
        sent = []

        def cut(h):
            return pl.ds(h * part, part)

        def lane(turn):
            return 0 if sides == 1 else (0 if turn == 1 else 1)

        def copy(src, dest, h, name):
            if name[0] == "y":
                dst, sem = from_y.at[lane(name[1]), dest, cut(h)], ysem.at[lane(name[1]), dest, h]
            else:
                side = 0 if name[1] == 1 else 1
                zz = lax.div(dest, ny)
                dst, sem = from_z.at[side, zz, cut(h)], zsem.at[side, zz, h]
            return pltpu.make_async_remote_copy(
                src_ref=src,
                dst_ref=dst,
                send_sem=send_sem.at[dest, h],
                recv_sem=sem,
                device_id=near[name][1],
                device_id_type=MESH,
            )

        def send(src, dest, h, name, ok):
            pl.when(ok)(lambda: copy(src, dest, h, name).start())
            sent.append((ok, src, dest, h, name))

        def add_up(refs, out, h):
            def body(i, carry):
                at = pl.ds(h * part + i * strip, strip)
                total = refs[0][at, :].astype(F32)
                for ref in refs[1:]:
                    total = total + ref[at, :].astype(F32)
                out[at, :] = total.astype(out.dtype)
                return carry

            lax.fori_loop(0, part // strip, body, 0)

        def order():
            for far in range(nz - 1, -1, -1):
                for sign in (1, -1) if far else (1,):
                    zz = z + sign * far
                    yield far, sign, zz, (zz >= 0) & (zz < nz)

        for side in range(ny - 1, 0, -1):
            for far, sign, zz, ok in order():
                for h in range(pieces):
                    for turn in (1, -1):
                        yy = y + turn * side
                        go = ok & (yy >= 0) & (yy < ny)
                        dest = lax.select(go, zz * ny + yy, me)
                        behind = near[("y", -turn)][0]
                        if ny == 2:
                            send(p_ref.at[dest, cut(h)], dest, h, ("y", turn), go)
                        else:

                            @pl.when(go & behind)
                            def _():
                                copy(p_ref.at[dest, cut(h)], dest, h, ("y", turn)).wait_recv()
                                add_up([p_ref.at[dest], from_y.at[lane(turn), dest]], acc.at[dest], h)

                            @pl.when(go & jnp.logical_not(behind))
                            def _():
                                add_up([p_ref.at[dest]], acc.at[dest], h)

                            send(acc.at[dest, cut(h)], dest, h, ("y", turn), go)
        for far, sign, zz, ok in order():
            dest = lax.select(ok, zz * ny + y, me)
            for h in range(pieces):
                for turn in (1, -1):

                    @pl.when(ok & near[("y", -turn)][0])
                    def _():
                        copy(p_ref.at[dest, cut(h)], dest, h, ("y", turn)).wait_recv()

                if ny == 2:

                    @pl.when(ok)
                    def _():
                        add_up([p_ref.at[dest], from_y.at[0, dest]], acc.at[dest], h)

                else:

                    @pl.when(ok)
                    def _():
                        add_up([p_ref.at[dest]], acc.at[dest], h)

                    for turn in (1, -1):

                        @pl.when(ok & near[("y", -turn)][0])
                        def _():
                            add_up([acc.at[dest], from_y.at[lane(turn), dest]], acc.at[dest], h)

                if far:
                    name = ("z", sign)
                    behind = near[("z", -sign)][0]
                    side = 0 if sign == 1 else 1

                    @pl.when(ok & behind)
                    def _():
                        copy(acc.at[dest, cut(h)], dest, h, name).wait_recv()
                        add_up([acc.at[dest], from_z.at[side, zz]], acc.at[dest], h)

                    send(acc.at[dest, cut(h)], dest, h, name, ok)
                else:
                    below, above = near[("z", -1)][0], near[("z", 1)][0]
                    for sign2, cond in ((1, below), (-1, above)):

                        @pl.when(cond)
                        def _():
                            copy(acc.at[me, cut(h)], me, h, ("z", sign2)).wait_recv()

                    lower, upper = from_z.at[0, z], from_z.at[1, z]

                    @pl.when(below & above)
                    def _():
                        add_up([acc.at[me], lower, upper], o_ref, h)

                    @pl.when(below & jnp.logical_not(above))
                    def _():
                        add_up([acc.at[me], lower], o_ref, h)

                    @pl.when(jnp.logical_not(below) & above)
                    def _():
                        add_up([acc.at[me], upper], o_ref, h)

        for ok, src, dest, h, name in sent:
            pl.when(ok)(lambda: copy(src, dest, h, name).wait_send())

    return pl.pallas_call(
        kernel,
        out_shape=jax.ShapeDtypeStruct((rows, width), F32),
        in_specs=[pl.BlockSpec(memory_space=pltpu.VMEM)],
        out_specs=pl.BlockSpec(memory_space=pltpu.VMEM),
        scratch_shapes=[
            pltpu.VMEM((seq, rows, width), BF),
            pltpu.VMEM((sides, seq, rows, width), BF),
            pltpu.VMEM((2, nz, rows, width), BF),
            pltpu.SemaphoreType.DMA((seq, pieces)),
            pltpu.SemaphoreType.DMA((sides, seq, pieces)),
            pltpu.SemaphoreType.DMA((2, nz, pieces)),
        ],
        compiler_params=pltpu.CompilerParams(
            collective_id=collective_id, has_side_effects=True, vmem_limit_bytes=VMEM_MOST
        ),
        name="seq_reduce",
    )(terms)


def small_exchange(arrays, axes, collective_id):
    sizes = [lax.axis_size(axis) for axis in axes]
    peers = math.prod(sizes)
    seq = lax.axis_size("seq")
    count = len(arrays)

    def kernel(*refs):
        ins, outs, (send_sem, recv_sem) = refs[:count], refs[count : 2 * count], refs[2 * count :]
        dp, sq = lax.axis_index("dp"), lax.axis_index("seq")
        me = sq if len(axes) == 1 else dp * seq + sq

        def device(peer):
            return (dp, peer) if len(axes) == 1 else (lax.div(peer, seq), lax.rem(peer, seq))

        barrier = pltpu.get_barrier_semaphore()
        for step in range(1, peers):
            pl.semaphore_signal(
                barrier, 1, device_id=device(lax.rem(me + step, peers)), device_id_type=MESH
            )
        pl.semaphore_wait(barrier, peers - 1)

        def copy(i, peer, src_slot):
            src = ins[i].at[0] if arrays[i].shape[0] == 1 else ins[i].at[peer]
            return pltpu.make_async_remote_copy(
                src_ref=src,
                dst_ref=outs[i].at[src_slot],
                send_sem=send_sem.at[i, peer],
                recv_sem=recv_sem.at[i, src_slot],
                device_id=device(peer),
                device_id_type=MESH,
            )

        for step in range(1, peers):
            for i in range(count):
                copy(i, lax.rem(me + step, peers), me).start()
        for i in range(count):
            outs[i][me] = ins[i][0] if arrays[i].shape[0] == 1 else ins[i][me]
        for step in range(1, peers):
            for i in range(count):
                copy(i, lax.rem(me + step, peers), me).wait_send()
                source = lax.rem(me + peers - step, peers)
                copy(i, source, source).wait_recv()

    return pl.pallas_call(
        kernel,
        out_shape=[jax.ShapeDtypeStruct((peers,) + a.shape[1:], a.dtype) for a in arrays],
        in_specs=[pl.BlockSpec(memory_space=pltpu.VMEM)] * count,
        out_specs=[pl.BlockSpec(memory_space=pltpu.VMEM)] * count,
        scratch_shapes=[
            pltpu.SemaphoreType.DMA((count, peers)),
            pltpu.SemaphoreType.DMA((count, peers)),
        ],
        compiler_params=pltpu.CompilerParams(collective_id=collective_id, has_side_effects=True),
        name="small_exchange",
    )(*arrays)


def packed_rows(parts, sublanes):
    flat = jnp.concatenate(parts, axis=1)
    fill = -flat.shape[1] % (sublanes * 128)
    return jnp.pad(flat, ((0, 0), (0, fill))).reshape(flat.shape[0], -1, 128)


def rms_factor(values):
    return lax.rsqrt(jnp.mean(values * values, axis=-1, keepdims=True) + NORM_EPS)


def norm_back(values, factor, gain_row, incoming):
    scaled = incoming * gain_row
    gain_part = jnp.sum(incoming * values * factor, axis=0)
    inner = jnp.mean(scaled * values, axis=-1, keepdims=True)
    return (factor * (scaled - values * factor * factor * inner), gain_part)


def rotary(positions):
    half_dim = HEAD_DIM // 2
    freqs = jnp.exp(
        -math.log(ROPE_BASE) * (2.0 * jnp.arange(half_dim, dtype=F32) / HEAD_DIM)
    )
    angles = positions.astype(F32)[:, None] * freqs[None, :]
    return (jnp.cos(angles)[:, None, :], jnp.sin(angles)[:, None, :])


def rotate(values, cosine, sine):
    half_dim = values.shape[-1] // 2
    first = values[..., :half_dim]
    second = values[..., half_dim:]
    return jnp.concatenate(
        [first * cosine - second * sine, second * cosine + first * sine], axis=-1
    )


def attend_forward(pieces):
    queries, key_rows, value_rows, seg_ids = pieces
    score_scale = HEAD_DIM ** (-0.5)
    scores = jnp.einsum("qhd,khd->hqk", queries, key_rows, preferred_element_type=F32) * score_scale
    allowed = seg_ids[None, :] <= seg_ids[:, None]
    scores = jnp.where(allowed[None], scores, MASKED_SCORE)
    row_max = jnp.max(scores, axis=-1, keepdims=True)
    exp_scores = jnp.exp(scores - row_max)
    row_sum = jnp.sum(exp_scores, axis=-1, keepdims=True)
    attn_probs = exp_scores / row_sum
    attended = jnp.einsum(
        "hqk,khd->qhd", attn_probs.astype(BF), value_rows, preferred_element_type=F32
    )
    return (attended.astype(BF), (row_max + jnp.log(row_sum))[..., 0])


def attend_backward(pieces):
    queries, key_rows, value_rows, grad_out, log_norm, seg_ids = pieces
    score_scale = HEAD_DIM ** (-0.5)
    scores = jnp.einsum("qhd,khd->hqk", queries, key_rows, preferred_element_type=F32) * score_scale
    allowed = seg_ids[None, :] <= seg_ids[:, None]
    attn_probs = jnp.where(allowed[None], jnp.exp(scores - log_norm[..., None]), 0.0)
    grad_probs = jnp.einsum("qhd,khd->hqk", grad_out, value_rows, preferred_element_type=F32)
    inner = jnp.sum(attn_probs * grad_probs, axis=-1, keepdims=True)
    grad_scores = (attn_probs * (grad_probs - inner)).astype(BF)
    grad_query = (
        jnp.einsum("hqk,khd->qhd", grad_scores, key_rows, preferred_element_type=F32) * score_scale
    )
    grad_key = (
        jnp.einsum("hqk,qhd->khd", grad_scores, queries, preferred_element_type=F32) * score_scale
    )
    grad_value = jnp.einsum(
        "hqk,qhd->khd", attn_probs.astype(BF), grad_out, preferred_element_type=F32
    )
    return (grad_query.astype(BF), grad_key.astype(BF), grad_value.astype(BF))


def swiglu(gate_vals, up_vals):
    return jax.nn.silu(gate_vals) * up_vals


def local(
    tokens,
    segments,
    routes,
    cotangent,
    attn_weight,
    router_weight,
    norm_gains,
    expert_in,
    expert_out,
):
    num_seqs, local_len, width = tokens.shape
    seq_length = segments.shape[1]
    seq, ndp = lax.axis_size("seq"), lax.axis_size("dp")
    me = lax.axis_index("seq")
    devices = seq * ndp
    heads_here = HEADS // seq
    cols = heads_here * HEAD_DIM
    tok = num_seqs * local_len
    group = tok * seq
    own_rows = attn_weight.shape[0]
    experts_all = router_weight.shape[1]
    experts = experts_all // seq
    top = routes.shape[-1]
    capacity = (9 * tok * top + 8 * experts_all - 1) // (8 * experts_all)

    in_full = lax.all_gather(expert_in, "dp", axis=1, tiled=True)
    out_full = lax.all_gather(expert_out, "dp", axis=2, tiled=True)

    n_router, n_gain = own_rows * experts_all, 4 * own_rows
    (small_all,) = small_exchange(
        [packed_rows([router_weight.reshape(1, -1), norm_gains.reshape(1, -1)], 16)], ("dp", "seq"), 1
    )
    small_all = small_all.reshape(devices, -1)
    router_full = small_all[:, :n_router].reshape(width, experts_all)
    gain_rows = (
        small_all[:, n_router : n_router + n_gain]
        .reshape(devices, 4, own_rows)
        .transpose(1, 0, 2)
        .reshape(4, width)
        .astype(F32)
    )
    (routes_all,) = small_exchange([routes.reshape(1, -1, 128)], ("seq",), 2)
    routes_all = routes_all.reshape(seq, tok, top)

    qkv_send = (
        attn_weight[:, :3].reshape(own_rows, 3, seq, cols).transpose(2, 1, 0, 3)
    )
    qkv_got = lax.all_to_all(qkv_send, "seq", split_axis=0, concat_axis=0, tiled=True)
    qkv_full = lax.all_gather(qkv_got, "dp", axis=0, tiled=True)
    qkv_weight = qkv_full.transpose(1, 0, 2, 3).reshape(3, width, cols)
    spread = seq // ndp
    out_rows = lax.all_gather(attn_weight[:, 3], "dp", axis=0, tiled=False)
    out_send = jnp.repeat(out_rows, spread, axis=0)
    out_got = lax.all_to_all(out_send, "seq", split_axis=0, concat_axis=0, tiled=True)
    proj_weight = lax.dynamic_slice_in_dim(
        out_got, lax.rem(me, spread) * ndp, ndp, axis=0
    ).reshape(cols, width)

    resid_in = tokens.astype(F32).reshape(tok, width)
    factor_attn = rms_factor(resid_in)
    normed_low = (resid_in * factor_attn * gain_rows[0]).astype(BF)
    normed_all = seq_gather(normed_low, 3).reshape(group, width)
    raw = jnp.einsum("td,jde->jte", normed_all, qkv_weight, preferred_element_type=F32)
    squares = jnp.sum(raw[:2] * raw[:2], axis=-1).reshape(1, -1, 128)
    (sums,) = small_exchange([squares], ("seq",), 4)
    factors = lax.rsqrt(jnp.sum(sums, axis=0).reshape(2, group, 1) / width + NORM_EPS)
    head_gains = lax.dynamic_slice_in_dim(gain_rows, me * cols, cols, axis=1)

    position = (
        jnp.arange(seq, dtype=jnp.int32)[:, None, None] * local_len
        + jnp.zeros((1, num_seqs, 1), jnp.int32)
        + jnp.arange(local_len, dtype=jnp.int32)[None, None, :]
    ).reshape(group)
    cosine, sine = rotary(position)

    def to_heads(values):
        return values.reshape(group, heads_here, HEAD_DIM)

    def by_sequence(values):
        return (
            values.reshape(seq, num_seqs, local_len, heads_here, HEAD_DIM)
            .transpose(1, 0, 2, 3, 4)
            .reshape(num_seqs, seq_length, heads_here, HEAD_DIM)
        )

    def by_source(values):
        return (
            values.reshape(num_seqs, seq, local_len, cols).transpose(1, 0, 2, 3).reshape(group, cols)
        )

    qn = raw[0] * factors[0] * head_gains[1]
    kn = raw[1] * factors[1] * head_gains[2]
    query_head = by_sequence(rotate(to_heads(qn), cosine, sine).astype(BF))
    key_head = by_sequence(rotate(to_heads(kn), cosine, sine).astype(BF))
    value_head = by_sequence(raw[2].astype(BF))
    attended, log_norm = lax.map(attend_forward, (query_head, key_head, value_head, segments))
    o_head = by_source(attended.reshape(num_seqs, seq_length, cols))
    z_terms = jnp.dot(o_head, proj_weight, preferred_element_type=F32).astype(BF)
    z = seq_reduce(z_terms.reshape(seq, tok, width), 5)

    middle = resid_in + z
    factor_ffn = rms_factor(middle)
    ffn_low = (middle * factor_ffn * gain_rows[3]).astype(BF)
    ffn_all = seq_gather(ffn_low, 6)
    cot_low = cotangent.reshape(tok, width)
    cot_all = seq_gather(cot_low, 7)

    logits_all = jnp.einsum("std,de->ste", ffn_all, router_full, preferred_element_type=F32)
    probs_all = jax.nn.softmax(logits_all, axis=-1)
    here = me * experts + jnp.arange(experts, dtype=jnp.int32)
    hits = jnp.any(routes_all[:, :, :, None] == here, axis=2)
    token_ids = jnp.arange(tok, dtype=jnp.int32)
    earlier = (token_ids[:, None] > token_ids[None, :]).astype(BF)
    slot = jnp.einsum("tu,sue->ste", earlier, hits.astype(BF), preferred_element_type=F32)
    slot = jnp.where(hits, slot, float(tok + 1)).astype(jnp.int32)
    place = slot.transpose(2, 0, 1)[:, :, None, :] == jnp.arange(capacity, dtype=jnp.int32)[
        None, None, :, None
    ]
    place_low = place.astype(BF)
    probs_here = lax.dynamic_slice_in_dim(probs_all, me * experts, experts, axis=2).transpose(2, 0, 1)
    place_gate = jnp.where(place, probs_here[:, :, None, :], 0.0)
    slot_gate = jnp.sum(place_gate, axis=-1)
    slots = seq * capacity
    rows = (
        jnp.einsum("esjt,std->esjd", place_low, ffn_all, preferred_element_type=F32)
        .astype(BF)
        .reshape(experts, slots, width)
    )
    cot_rows = jnp.einsum("esjt,std->esjd", place_low, cot_all, preferred_element_type=F32).reshape(
        experts, slots, width
    )

    gate_up = jnp.einsum("erd,edjf->erjf", rows, in_full, preferred_element_type=F32)
    hidden_f, swiglu_pull = jax.vjp(swiglu, gate_up[:, :, 0], gate_up[:, :, 1])
    hidden = hidden_f.astype(BF)
    expert_res = jnp.einsum("erf,efd->erd", hidden, out_full, preferred_element_type=F32).astype(BF)
    mixed_terms = jnp.einsum(
        "esjt,esjd->std",
        place_gate.astype(BF),
        expert_res.reshape(experts, seq, capacity, width),
        preferred_element_type=F32,
    ).astype(BF)
    mixed = seq_reduce(mixed_terms, 8)
    block_out = (middle + mixed).astype(BF).reshape(num_seqs, local_len, width)

    slot_dgate = jnp.sum(cot_rows * expert_res.astype(F32), axis=-1).reshape(experts, seq, capacity)
    grad_prob_here = jnp.sum(jnp.where(place, slot_dgate[..., None], 0.0), axis=2)
    grad_res = (cot_rows * slot_gate.reshape(experts, slots, 1)).astype(BF)
    grad_hidden = jnp.einsum("erd,efd->erf", grad_res, out_full, preferred_element_type=F32)
    grad_gatev, grad_upv = swiglu_pull(grad_hidden)
    grad_gu = jnp.stack([grad_gatev, grad_upv], axis=2).astype(BF)
    grad_rows = jnp.einsum("erjf,edjf->erd", grad_gu, in_full, preferred_element_type=F32).astype(BF)
    out_term = jnp.einsum("erf,erd->efd", hidden, grad_res, preferred_element_type=F32).astype(BF)
    in_term = jnp.einsum("erd,erjf->edjf", rows, grad_gu, preferred_element_type=F32).astype(BF)
    expert_out_grad = lax.psum_scatter(out_term, "dp", scatter_dimension=2, tiled=True).astype(F32)
    expert_in_grad = lax.psum_scatter(in_term, "dp", scatter_dimension=1, tiled=True).astype(F32)
    dffn_terms = jnp.einsum(
        "esjt,esjd->std",
        place_low,
        grad_rows.reshape(experts, seq, capacity, width),
        preferred_element_type=F32,
    ).astype(BF)
    grad_ffn = seq_reduce(dffn_terms, 9)
    (grad_prob,) = small_exchange(
        [grad_prob_here.transpose(1, 0, 2).reshape(seq, -1, 128)], ("seq",), 10
    )
    grad_prob = grad_prob.reshape(experts_all, tok).T

    route_probs = jax.nn.softmax(
        jnp.dot(ffn_low, router_full, preferred_element_type=F32), axis=-1
    )
    grad_logits = (
        route_probs * (grad_prob - jnp.sum(route_probs * grad_prob, axis=-1, keepdims=True))
    ).astype(BF)
    router_term = jnp.einsum("td,te->de", ffn_low, grad_logits, preferred_element_type=F32)
    grad_ffn = grad_ffn + jnp.einsum(
        "te,de->td", grad_logits, router_full, preferred_element_type=F32
    )
    grad_middle, gain_ffn = norm_back(middle, factor_ffn, gain_rows[3], grad_ffn)
    grad_middle = grad_middle + cot_low.astype(F32)

    dz_all = seq_gather(grad_middle.astype(BF), 11).reshape(group, width)
    grad_o = jnp.einsum("te,de->td", dz_all, proj_weight, preferred_element_type=F32).astype(BF)
    proj_term = jnp.einsum("td,te->de", o_head, dz_all, preferred_element_type=F32).astype(BF)
    grad_q, grad_k, grad_v = lax.map(
        attend_backward,
        (query_head, key_head, value_head, by_sequence(grad_o), log_norm, segments),
    )
    flat = (num_seqs, seq_length, cols)
    grad_qn = rotate(to_heads(by_source(grad_q.reshape(flat)).astype(F32)), cosine, -sine).reshape(
        group, cols
    )
    grad_kn = rotate(to_heads(by_source(grad_k.reshape(flat)).astype(F32)), cosine, -sine).reshape(
        group, cols
    )
    grad_n = jnp.stack([grad_qn, grad_kn])
    scaled = grad_n * head_gains[1:3, None, :]
    inner = jnp.sum(scaled * raw[:2], axis=-1).reshape(1, -1, 128)
    (inners,) = small_exchange([inner], ("seq",), 12)
    inner = jnp.sum(inners, axis=0).reshape(2, group, 1) / width
    gain_heads = jnp.sum(grad_n * raw[:2] * factors, axis=1)
    grad_raw = factors * (scaled - raw[:2] * factors * factors * inner)
    grad_stack = jnp.concatenate(
        [grad_raw.astype(BF), by_source(grad_v.reshape(flat))[None]], axis=0
    )
    dn_terms = jnp.einsum("jte,jde->td", grad_stack, qkv_weight, preferred_element_type=F32).astype(BF)
    grad_normed = seq_reduce(dn_terms.reshape(seq, tok, width), 13)
    qkv_term = jnp.einsum("td,jte->jde", normed_all, grad_stack, preferred_element_type=F32).astype(BF)
    grad_resid, gain_attn = norm_back(resid_in, factor_attn, gain_rows[0], grad_normed)
    input_grad = (grad_resid + grad_middle).reshape(num_seqs, local_len, width)

    qkv_part = lax.psum_scatter(qkv_term, "dp", scatter_dimension=1, tiled=True)
    qkv_out = lax.all_to_all(
        qkv_part.reshape(3, seq, own_rows, cols).transpose(1, 0, 2, 3),
        "seq",
        split_axis=0,
        concat_axis=0,
        tiled=True,
    )
    qkv_grad = qkv_out.transpose(2, 1, 0, 3).reshape(own_rows, 3, width)
    proj_part = lax.psum_scatter(proj_term, "dp", scatter_dimension=0, tiled=True)
    proj_grad = lax.ppermute(
        proj_part,
        ("dp", "seq"),
        [(i * seq + s, s * ndp + i) for i in range(ndp) for s in range(seq)],
    )
    attn_grad = jnp.concatenate([qkv_grad, proj_grad[:, None, :]], axis=1).astype(F32)
    zero_heads = jnp.zeros((2, width), F32)
    gain_heads = lax.dynamic_update_slice_in_dim(zero_heads, gain_heads, me * cols, axis=1)
    gain_term = jnp.concatenate([gain_attn[None], gain_heads, gain_ffn[None]], axis=0)
    gain_send = gain_term.reshape(4, devices, own_rows).transpose(1, 0, 2)
    (terms,) = small_exchange(
        [packed_rows([router_term.reshape(devices, -1), gain_send.reshape(devices, -1)], 8)],
        ("dp", "seq"),
        14,
    )
    total = jnp.sum(terms, axis=0).reshape(-1)
    router_grad = total[:n_router].reshape(own_rows, experts_all)
    gain_grad = total[n_router : n_router + n_gain].reshape(4, own_rows)
    return (
        block_out,
        input_grad,
        attn_grad,
        router_grad,
        gain_grad,
        expert_in_grad,
        expert_out_grad,
    )


def solution(mesh):
    in_specs = (
        P("dp", "seq", None),
        P("dp", None),
        P("dp", "seq", None),
        P("dp", "seq", None),
        P(("dp", "seq"), None, None),
        P(("dp", "seq"), None),
        P(None, ("dp", "seq")),
        P("seq", "dp", None, None),
        P("seq", None, "dp"),
    )
    out_specs = (
        P("dp", "seq", None),
        P("dp", "seq", None),
        P(("dp", "seq"), None, None),
        P(("dp", "seq"), None),
        P(None, ("dp", "seq")),
        P("seq", "dp", None, None),
        P("seq", None, "dp"),
    )
    return jax.shard_map(local, mesh=mesh, in_specs=in_specs, out_specs=out_specs, check_vma=False)
```

```python
import math

import jax
import jax.numpy as jnp
from jax import lax
from jax.experimental import pallas as pl
from jax.experimental.pallas import tpu as pltpu
from jax.sharding import PartitionSpec as P

HEADS = 16
HEAD_DIM = 128
NORM_EPS = 1e-05
ROPE_BASE = 10000.0
MASKED_SCORE = -1e30
BF = jnp.bfloat16
F32 = jnp.float32
MESH = pl.DeviceIdType.MESH
VMEM_MOST = 60 << 20


class Line:
    def __init__(self, size, place, device):
        self.size, self.place, self.device = size, place, device

    def has(self, turn):
        return self.place < self.size - 1 if turn > 0 else self.place > 0

    def inside(self, place):
        return (place >= 0) & (place < self.size)


def grid_of(seq_size):
    lines = 4 if seq_size % 4 == 0 else 1
    return lines, seq_size // lines


def seq_lines():
    dp, me = lax.axis_index("dp"), lax.axis_index("seq")
    nz, ny = grid_of(lax.axis_size("seq"))
    along = Line(nz, lax.div(me, ny), lambda turn: (dp, me + turn * ny))
    across = Line(ny, lax.rem(me, ny), lambda turn: (dp, me + turn))
    return along, across, me, lambda z, y: z * ny + y


def dp_lines():
    dp, me = lax.axis_index("dp"), lax.axis_index("seq")
    along = Line(lax.axis_size("dp") // 2, lax.div(dp, 2), lambda turn: (dp + 2 * turn, me))
    across = Line(2, lax.rem(dp, 2), lambda turn: (dp + turn, me))
    return along, across, dp, lambda x, core: 2 * x + core


def cost_of(microseconds):
    return pl.CostEstimate(flops=0, bytes_accessed=microseconds * 3_600_000, transcendentals=0)


def send_to(src, dst, send_sem, recv_sem, device):
    return pltpu.make_async_remote_copy(
        src_ref=src,
        dst_ref=dst,
        send_sem=send_sem,
        recv_sem=recv_sem,
        device_id=device,
        device_id_type=MESH,
    )


def greet(targets):
    barrier = pltpu.get_barrier_semaphore()
    count = 0
    for cond, device in targets:

        @pl.when(cond)
        def _(device=device):
            pl.semaphore_signal(barrier, 1, device_id=device, device_id_type=MESH)

        count = count + cond.astype(jnp.int32)
    pl.semaphore_wait(barrier, count)


def greet_lines(*lines):
    greet([(line.has(turn), line.device(turn)) for line in lines for turn in (1, -1)])


def cuts_of(rows, ny):
    unit = rows // 16
    late = max(1, unit * 3 // 16) if ny == 2 else unit // 2
    early = unit - late
    half = (early + 1) // 2
    firsts = [(0, half * 16)] + ([(half * 16, (early - half) * 16)] if early > half else [])
    return firsts, [(early * 16, late * 16)]


class Gather:
    def __init__(self, first, second, me, flat, pieces, own, slot, send_sem, recv_sem, ready=None):
        self.first, self.second, self.me, self.flat = first, second, me, flat
        self.pieces, self.own, self.slot = pieces, own, slot
        self.send_sem, self.recv_sem, self.ready = send_sem, recv_sem, ready
        self.sent = []

    def _copy(self, src, origin, h, line, turn):
        way = (0 if line is self.first else 2) + (turn > 0)
        return send_to(
            src,
            self.slot(origin, h),
            self.send_sem.at[origin, h, way],
            self.recv_sem.at[origin, h],
            line.device(turn),
        )

    def _send(self, src, origin, h, line, turn, cond):
        ok = cond & line.has(turn)
        pl.when(ok)(lambda: self._copy(src, origin, h, line, turn).start())
        self.sent.append((ok, src, origin, h, line, turn))

    def start(self):
        for h in range(self.pieces):
            if self.ready is not None:
                self.ready(h)
            for line in (self.first, self.second):
                for turn in (1, -1):
                    self._send(self.own(h), self.me, h, line, turn, self.me >= 0)

    def _arrive(self, place, side, h, sends):
        first, second = self.first, self.second
        cond = first.inside(place) & second.inside(side)
        origin = lax.select(cond, self.flat(place, side), self.me)

        @pl.when(cond)
        def _():
            self._copy(self.slot(origin, h), origin, h, first, 1).wait_recv()

        for line, turn in sends:
            self._send(self.slot(origin, h), origin, h, line, turn, cond)

    def steps(self):
        first, second = self.first, self.second
        listed = []
        for far in range(1, first.size):
            for h in range(self.pieces):
                for sign in (1, -1):
                    listed.append(
                        (
                            far,
                            lambda far=far, h=h, sign=sign: self._arrive(
                                first.place - sign * far,
                                second.place,
                                h,
                                [(first, sign), (second, 1), (second, -1)],
                            ),
                        )
                    )
        for step in range(1, second.size):
            for far in range(first.size):
                for h in range(self.pieces):
                    for sign in (1, -1) if far else (1,):
                        for turn in (1, -1):
                            listed.append(
                                (
                                    far + step + 0.5,
                                    lambda far=far, step=step, h=h, sign=sign, turn=turn: self._arrive(
                                        first.place - sign * far,
                                        second.place - turn * step,
                                        h,
                                        [(second, turn)] if step < second.size - 1 else [],
                                    ),
                                )
                            )
        return listed

    def finish(self):
        for ok, src, origin, h, line, turn in self.sent:
            pl.when(ok)(lambda: self._copy(src, origin, h, line, turn).wait_send())


def run_steps(*programs):
    for _, step in sorted((s for p in programs for s in p.steps()), key=lambda s: s[0]):
        step()


def seq_gathers(block_ref, out_ref, sems):
    along, across, me, flat = seq_lines()
    early, late = cuts_of(block_ref.shape[0], across.size)
    made = []
    for cuts, first, second, index, (send_sem, recv_sem) in (
        (early, along, across, flat, sems[0:2]),
        (late, across, along, lambda y, z: flat(z, y), sems[2:4]),
    ):
        made.append(
            Gather(
                first,
                second,
                me,
                index,
                len(cuts),
                lambda h, cuts=cuts: block_ref.at[pl.ds(*cuts[h])],
                lambda origin, h, cuts=cuts: out_ref.at[origin, pl.ds(*cuts[h])],
                send_sem,
                recv_sem,
            )
        )
    return made


def gather_sems(seq, rows):
    early, late = cuts_of(rows, grid_of(seq)[1])
    return [
        pltpu.SemaphoreType.DMA((seq, len(early), 4)),
        pltpu.SemaphoreType.DMA((seq, len(early))),
        pltpu.SemaphoreType.DMA((seq, len(late), 4)),
        pltpu.SemaphoreType.DMA((seq, len(late))),
    ]


def seq_gather(block, collective_id):
    rows, width = block.shape
    seq = lax.axis_size("seq")

    def kernel(x_ref, o_ref, local_sem, *sems):
        along, across, me, _ = seq_lines()
        greet_lines(along, across)
        own = pltpu.make_async_copy(x_ref, o_ref.at[me], local_sem)
        own.start()
        programs = seq_gathers(x_ref, o_ref, sems)
        for program in programs:
            program.start()
        run_steps(*programs)
        for program in programs:
            program.finish()
        own.wait()

    return pl.pallas_call(
        kernel,
        out_shape=jax.ShapeDtypeStruct((seq, rows, width), block.dtype),
        in_specs=[pl.BlockSpec(memory_space=pl.ANY)],
        out_specs=pl.BlockSpec(memory_space=pl.ANY),
        scratch_shapes=[pltpu.SemaphoreType.DMA] + gather_sems(seq, rows),
        compiler_params=pltpu.CompilerParams(collective_id=collective_id, has_side_effects=True),
        name="seq_gather",
        cost_estimate=cost_of(80),
    )(block)


class Reduce:
    def __init__(self, first, second, me, flat, cuts, terms, acc, out, from_first, from_second, sems):
        self.first, self.second, self.me, self.flat, self.cuts = first, second, me, flat, cuts
        self.terms, self.acc, self.out = terms, acc, out
        self.from_first, self.from_second = from_first, from_second
        self.send_sem, self.first_sem, self.second_sem = sems
        self.base = cuts[0][0]
        self.sent = []

    @staticmethod
    def scratch(rows_of, first_size, second_size, width):
        seq, rows, pieces = first_size * second_size, sum(r for _, r in rows_of), len(rows_of)
        lanes = 1 if first_size == 2 else 2
        return [
            pltpu.VMEM((lanes, seq, rows, width), BF),
            pltpu.VMEM((2, second_size, rows, width), BF),
            pltpu.SemaphoreType.DMA((seq, pieces)),
            pltpu.SemaphoreType.DMA((lanes, seq, pieces)),
            pltpu.SemaphoreType.DMA((2, second_size, pieces)),
        ]

    def _lane(self, turn):
        return 0 if self.first.size == 2 or turn > 0 else 1

    def _cut(self, h):
        return pl.ds(*self.cuts[h])

    def _inner(self, h):
        return pl.ds(self.cuts[h][0] - self.base, self.cuts[h][1])

    def _copy(self, src, dest, spot, h, line, turn):
        if line is self.first:
            lane = self._lane(turn)
            dst, sem = self.from_first.at[lane, dest, self._inner(h)], self.first_sem.at[lane, dest, h]
        else:
            side = 0 if turn > 0 else 1
            dst, sem = self.from_second.at[side, spot, self._inner(h)], self.second_sem.at[side, spot, h]
        return send_to(src, dst, self.send_sem.at[dest, h], sem, line.device(turn))

    def _send(self, src, dest, spot, h, line, turn, ok):
        pl.when(ok)(lambda: self._copy(src, dest, spot, h, line, turn).start())
        self.sent.append((ok, src, dest, spot, h, line, turn))

    def _add(self, cond, whole, parts, out, h):
        first, count = self.cuts[h]

        @pl.when(cond)
        def _():
            def body(i, carry):
                at = pl.ds(pl.multiple_of(first + i * 16, 16), 16)
                inner = pl.ds(pl.multiple_of(first - self.base + i * 16, 16), 16)
                total = None
                for ref in whole:
                    total = ref[at, :].astype(F32) if total is None else total + ref[at, :].astype(F32)
                for ref in parts:
                    total = total + ref[inner, :].astype(F32)
                out[at, :] = total.astype(out.dtype)
                return carry

            lax.fori_loop(0, count // 16, body, 0)

    def _spread(self):
        for far in range(self.second.size - 1, -1, -1):
            for sign in (1, -1) if far else (1,):
                spot = self.second.place + sign * far
                yield far, sign, spot, self.second.inside(spot)

    def outward(self):
        first = self.first
        for step in range(first.size - 1, 0, -1):
            for far, sign, spot, ok in self._spread():
                for h in range(len(self.cuts)):
                    for turn in (1, -1):
                        yield lambda a=(step, spot, ok, h, turn): self._pass_on(*a)

    def _pass_on(self, step, spot, ok, h, turn):
        first = self.first
        goal = first.place + turn * step
        go = ok & first.inside(goal)
        dest = lax.select(go, self.flat(goal, spot), self.me)
        if first.size == 2:
            self._send(self.terms.at[dest, self._cut(h)], dest, spot, h, first, turn, go)
            return
        behind = first.has(-turn)
        self._await(go & behind, dest, spot, h, first, turn)
        self._add(go & behind, [self.terms.at[dest]], [self.from_first.at[self._lane(turn), dest]], self.acc.at[dest], h)
        self._add(go & jnp.logical_not(behind), [self.terms.at[dest]], [], self.acc.at[dest], h)
        self._send(self.acc.at[dest, self._cut(h)], dest, spot, h, first, turn, go)

    def _await(self, cond, dest, spot, h, line, turn):
        @pl.when(cond)
        def _():
            self._copy(self.acc.at[dest, self._cut(h)], dest, spot, h, line, turn).wait_recv()

    def inward(self):
        for far, sign, spot, ok in self._spread():
            for h in range(len(self.cuts)):
                yield lambda a=(far, sign, spot, ok, h): self._collect(*a)

    def _collect(self, far, sign, spot, ok, h):
        first, second, acc = self.first, self.second, self.acc
        dest = lax.select(ok, self.flat(first.place, spot), self.me)
        for turn in (1, -1):
            self._await(ok & first.has(-turn), dest, spot, h, first, turn)
        if first.size == 2:
            self._add(ok, [self.terms.at[dest]], [self.from_first.at[0, dest]], acc.at[dest], h)
        else:
            low, high = first.has(-1), first.has(1)
            lows, highs = self.from_first.at[self._lane(1), dest], self.from_first.at[self._lane(-1), dest]
            self._add(ok & low & high, [self.terms.at[dest]], [lows, highs], acc.at[dest], h)
            self._add(ok & low & jnp.logical_not(high), [self.terms.at[dest]], [lows], acc.at[dest], h)
            self._add(ok & high & jnp.logical_not(low), [self.terms.at[dest]], [highs], acc.at[dest], h)
        if far:
            behind = second.has(-sign)
            side = 0 if sign > 0 else 1
            self._await(ok & behind, dest, spot, h, second, sign)
            self._add(ok & behind, [acc.at[dest]], [self.from_second.at[side, spot]], acc.at[dest], h)
            self._send(acc.at[dest, self._cut(h)], dest, spot, h, second, sign, ok)
            return
        low, high = second.has(-1), second.has(1)
        self._await(low, dest, spot, h, second, 1)
        self._await(high, dest, spot, h, second, -1)
        lows, highs = self.from_second.at[0, spot], self.from_second.at[1, spot]
        self._add(low & high, [acc.at[dest]], [lows, highs], self.out, h)
        self._add(low & jnp.logical_not(high), [acc.at[dest]], [lows], self.out, h)
        self._add(high & jnp.logical_not(low), [acc.at[dest]], [highs], self.out, h)

    def finish(self):
        for ok, src, dest, spot, h, line, turn in self.sent:
            pl.when(ok)(lambda: self._copy(src, dest, spot, h, line, turn).wait_send())


def woven(*lists):
    keyed = [((i + 1) / len(entries), n, entry) for n, entries in enumerate(map(list, lists)) for i, entry in enumerate(entries)]
    return [entry for _, _, entry in sorted(keyed, key=lambda k: k[:2])]


def seq_reduces(terms, acc, out, scratch):
    along, across, me, flat = seq_lines()
    early, late = cuts_of(terms.shape[1], across.size)
    return [
        Reduce(across, along, me, lambda y, z: flat(z, y), early, terms, acc, out, *scratch[0:2], scratch[2:5]),
        Reduce(along, across, me, flat, late, terms, acc, out, *scratch[5:7], scratch[7:10]),
    ]


def reduce_scratch(seq, rows, width):
    nz, ny = grid_of(seq)
    early, late = cuts_of(rows, ny)
    return (
        [pltpu.VMEM((seq, rows, width), BF)]
        + Reduce.scratch(early, ny, nz, width)
        + Reduce.scratch(late, nz, ny, width)
    )


def seq_reduce(terms, collective_id):
    seq, rows, width = terms.shape

    def kernel(p_ref, o_ref, acc, *scratch):
        along, across, _, _ = seq_lines()
        greet_lines(along, across)
        programs = seq_reduces(p_ref, acc, o_ref, scratch)
        for step in woven(*[p.outward() for p in programs]):
            step()
        for step in woven(*[p.inward() for p in programs]):
            step()
        for program in programs:
            program.finish()

    return pl.pallas_call(
        kernel,
        out_shape=jax.ShapeDtypeStruct((rows, width), F32),
        in_specs=[pl.BlockSpec(memory_space=pltpu.VMEM)],
        out_specs=pl.BlockSpec(memory_space=pltpu.VMEM),
        scratch_shapes=reduce_scratch(seq, rows, width),
        compiler_params=pltpu.CompilerParams(
            collective_id=collective_id, has_side_effects=True, vmem_limit_bytes=VMEM_MOST
        ),
        name="seq_reduce",
        cost_estimate=cost_of(80),
    )(terms)


def first_transfers(tokens, qkv_rows, proj_rows, packed, routes, collective_id):
    seq, ndp = lax.axis_size("seq"), lax.axis_size("dp")
    devices = seq * ndp
    rows, width = tokens.shape

    def kernel(x_ref, qkv_ref, proj_ref, packed_ref, routes_ref, x_out, qkv_out, proj_out, packed_out, routes_out, *sems):
        (local_sem, part_send, part_recv, own_sem, qkv_send, qkv_recv, proj_send, proj_recv, proj_fwd) = sems[:9]
        (small_send, small_recv, routes_send, routes_recv) = sems[9:13]
        along, across, me, _ = seq_lines()
        x_line, core_line, dp, dp_flat = dp_lines()
        rank = dp * seq + me
        barrier = pltpu.get_barrier_semaphore()

        def device(peer):
            return (lax.div(peer, seq), lax.rem(peer, seq))

        def meet(step, carry):
            pl.semaphore_signal(
                barrier, 1, device_id=device(lax.rem(rank + step, devices)), device_id_type=MESH
            )
            return carry

        lax.fori_loop(1, devices, meet, 0)
        pl.semaphore_wait(barrier, devices - 1)

        own_x = pltpu.make_async_copy(x_ref, x_out.at[me], local_sem.at[0])
        own_qkv = pltpu.make_async_copy(qkv_ref.at[me], qkv_out.at[dp, me], own_sem)
        own_x.start()
        own_qkv.start()

        def part(peer, origin):
            return send_to(
                qkv_ref.at[peer], qkv_out.at[dp, origin], part_send.at[peer], part_recv.at[origin], (dp, peer)
            )

        for step in range(1, seq):
            part(lax.rem(me + step, seq), me).start()

        goal = lax.div(rank, ndp)
        place = lax.rem(rank, ndp)

        def proj_first(slot):
            return send_to(proj_ref, proj_out.at[slot], proj_send, proj_recv.at[slot], (dp, goal))

        stays = goal == me
        own_proj = pltpu.make_async_copy(proj_ref, proj_out.at[place], local_sem.at[1])
        pl.when(stays)(own_proj.start)
        pl.when(jnp.logical_not(stays))(lambda: proj_first(place).start())

        def small(peer, origin):
            return send_to(
                packed_ref, packed_out.at[origin], small_send.at[peer], small_recv.at[origin], device(peer)
            )

        def small_start(step, carry):
            small(lax.rem(rank + step, devices), rank).start()
            return carry

        lax.fori_loop(1, devices, small_start, 0)

        def route(peer, origin):
            return send_to(
                routes_ref, routes_out.at[origin], routes_send.at[peer], routes_recv.at[origin], (dp, peer)
            )

        for step in range(1, seq):
            route(lax.rem(me + step, seq), me).start()
        packed_out[rank] = packed_ref[...]
        routes_out[me] = routes_ref[...]

        gathers = seq_gathers(x_ref, x_out, sems[13:])
        for program in gathers:
            program.start()

        def ready(h):
            @pl.when(h == me)
            def _():
                own_qkv.wait()

            @pl.when(h != me)
            def _():
                part(h, h).wait_recv()

        spread = Gather(
            x_line,
            core_line,
            dp,
            dp_flat,
            seq,
            lambda h: qkv_out.at[dp, h],
            lambda origin, h: qkv_out.at[origin, h],
            qkv_send,
            qkv_recv,
            ready,
        )
        spread.start()
        root = lax.div(me * ndp, seq)
        root_x, root_core = lax.div(root, 2), lax.rem(root, 2)
        on_line = core_line.place == root_core
        ways = [
            (on_line & (x_line.place >= root_x) & x_line.has(1), x_line.device(1), 0),
            (on_line & (x_line.place <= root_x) & x_line.has(-1), x_line.device(-1), 1),
            (on_line & core_line.has(1), core_line.device(1), 2),
            (on_line & core_line.has(-1), core_line.device(-1), 3),
        ]

        def onward(slot, way, target):
            return send_to(
                proj_out.at[slot], proj_out.at[slot], proj_fwd.at[slot, way], proj_recv.at[slot], target
            )

        for slot in range(ndp):
            held = (dp == root) & (lax.rem(me * ndp + slot, seq) == me)

            @pl.when(held)
            def _():
                own_proj.wait()

            @pl.when(jnp.logical_not(held))
            def _():
                onward(slot, 0, x_line.device(1)).wait_recv()

            for cond, target, way in ways:
                pl.when(cond)(lambda: onward(slot, way, target).start())
        run_steps(*gathers, spread)

        for program in (*gathers, spread):
            program.finish()
        for slot in range(ndp):
            for cond, target, way in ways:
                pl.when(cond)(lambda: onward(slot, way, target).wait_send())
        pl.when(jnp.logical_not(stays))(lambda: proj_first(place).wait_send())
        for step in range(1, seq):
            part(lax.rem(me + step, seq), me).wait_send()
            route(lax.rem(me + step, seq), me).wait_send()
            source = lax.rem(me + seq - step, seq)
            route(source, source).wait_recv()

        def small_end(step, carry):
            small(lax.rem(rank + step, devices), rank).wait_send()
            source = lax.rem(rank + devices - step, devices)
            small(source, source).wait_recv()
            return carry

        lax.fori_loop(1, devices, small_end, 0)
        own_x.wait()

    dma = pltpu.SemaphoreType.DMA
    hbm, vmem = pl.BlockSpec(memory_space=pl.ANY), pl.BlockSpec(memory_space=pltpu.VMEM)
    return pl.pallas_call(
        kernel,
        out_shape=[
            jax.ShapeDtypeStruct((seq, rows, width), BF),
            jax.ShapeDtypeStruct((ndp,) + qkv_rows.shape, BF),
            jax.ShapeDtypeStruct((ndp,) + proj_rows.shape, BF),
            jax.ShapeDtypeStruct((devices,) + packed.shape, BF),
            jax.ShapeDtypeStruct((seq,) + routes.shape, jnp.int32),
        ],
        in_specs=[hbm, hbm, hbm, vmem, vmem],
        out_specs=[hbm, hbm, hbm, vmem, vmem],
        scratch_shapes=[
            dma((2,)),
            dma((seq,)),
            dma((seq,)),
            dma,
            dma((ndp, seq, 4)),
            dma((ndp, seq)),
            dma,
            dma((ndp,)),
            dma((ndp, 4)),
            dma((devices,)),
            dma((devices,)),
            dma((seq,)),
            dma((seq,)),
        ]
        + gather_sems(seq, rows),
        compiler_params=pltpu.CompilerParams(collective_id=collective_id, has_side_effects=True),
        name="first_transfers",
        cost_estimate=cost_of(120),
    )(tokens, qkv_rows, proj_rows, packed, routes)


def small_exchange(arrays, axes, collective_id):
    sizes = [lax.axis_size(axis) for axis in axes]
    peers = math.prod(sizes)
    seq = lax.axis_size("seq")
    count = len(arrays)

    def kernel(*refs):
        ins, outs, (send_sem, recv_sem) = refs[:count], refs[count : 2 * count], refs[2 * count :]
        dp, sq = lax.axis_index("dp"), lax.axis_index("seq")
        me = sq if len(axes) == 1 else dp * seq + sq

        def device(peer):
            return (dp, peer) if len(axes) == 1 else (lax.div(peer, seq), lax.rem(peer, seq))

        barrier = pltpu.get_barrier_semaphore()
        for step in range(1, peers):
            pl.semaphore_signal(
                barrier, 1, device_id=device(lax.rem(me + step, peers)), device_id_type=MESH
            )
        pl.semaphore_wait(barrier, peers - 1)

        def copy(i, peer, src_slot):
            src = ins[i].at[0] if arrays[i].shape[0] == 1 else ins[i].at[peer]
            return pltpu.make_async_remote_copy(
                src_ref=src,
                dst_ref=outs[i].at[src_slot],
                send_sem=send_sem.at[i, peer],
                recv_sem=recv_sem.at[i, src_slot],
                device_id=device(peer),
                device_id_type=MESH,
            )

        for step in range(1, peers):
            for i in range(count):
                copy(i, lax.rem(me + step, peers), me).start()
        for i in range(count):
            outs[i][me] = ins[i][0] if arrays[i].shape[0] == 1 else ins[i][me]
        for step in range(1, peers):
            for i in range(count):
                copy(i, lax.rem(me + step, peers), me).wait_send()
                source = lax.rem(me + peers - step, peers)
                copy(i, source, source).wait_recv()

    return pl.pallas_call(
        kernel,
        out_shape=[jax.ShapeDtypeStruct((peers,) + a.shape[1:], a.dtype) for a in arrays],
        in_specs=[pl.BlockSpec(memory_space=pltpu.VMEM)] * count,
        out_specs=[pl.BlockSpec(memory_space=pltpu.VMEM)] * count,
        scratch_shapes=[
            pltpu.SemaphoreType.DMA((count, peers)),
            pltpu.SemaphoreType.DMA((count, peers)),
        ],
        compiler_params=pltpu.CompilerParams(collective_id=collective_id, has_side_effects=True),
        name="small_exchange",
        cost_estimate=cost_of(8),
    )(*arrays)


def last_transfers(terms, qkv_terms, proj_terms, packed, collective_id):
    seq, ndp = lax.axis_size("seq"), lax.axis_size("dp")
    devices = seq * ndp
    _, rows, width = terms.shape
    part_rows, cols = qkv_terms.shape[1] // seq, qkv_terms.shape[2]
    proj_rows = proj_terms.shape[1]
    n_scratch = len(reduce_scratch(seq, rows, width))
    n_reduce = 5

    def kernel(p_ref, qkv_ref, proj_ref, packed_ref, o_ref, qkv_out, proj_out, sum_out, acc, *scratch):
        seq_scratch, rest = scratch[: n_scratch - 1], scratch[n_scratch - 1 :]
        qkv_acc, qkv_sum, proj_acc, proj_sum, got = rest[:5]
        qkv_scratch, proj_scratch = rest[5 : 5 + n_reduce], rest[5 + n_reduce : 5 + 2 * n_reduce]
        (part_send, part_recv, move_send, move_recv, small_send, small_recv, own_sem) = rest[5 + 2 * n_reduce :]
        _, _, me, _ = seq_lines()
        x_line, core_line, dp, dp_flat = dp_lines()
        rank = dp * seq + me
        barrier = pltpu.get_barrier_semaphore()

        def device(peer):
            return (lax.div(peer, seq), lax.rem(peer, seq))

        def meet(step, carry):
            pl.semaphore_signal(
                barrier, 1, device_id=device(lax.rem(rank + step, devices)), device_id_type=MESH
            )
            return carry

        lax.fori_loop(1, devices, meet, 0)
        pl.semaphore_wait(barrier, devices - 1)

        programs = seq_reduces(p_ref, acc, o_ref, seq_scratch)

        def over_dp(refs, total, out, buffers):
            return Reduce(
                core_line,
                x_line,
                dp,
                lambda core, x: dp_flat(x, core),
                [(0, refs.shape[1])],
                refs,
                total,
                out,
                *buffers[0:2],
                buffers[2:5],
            )

        owners = [
            over_dp(qkv_ref, qkv_acc, qkv_sum, qkv_scratch),
            over_dp(proj_ref, proj_acc, proj_sum, proj_scratch),
        ]
        for owner in owners:
            for step in owner.outward():
                step()
        for step in woven(*[p.outward() for p in programs]):
            step()

        def small(peer, origin):
            return send_to(
                packed_ref.at[peer], got.at[origin], small_send.at[peer], small_recv.at[origin], device(peer)
            )

        def small_start(step, carry):
            small(lax.rem(rank + step, devices), rank).start()
            return carry

        lax.fori_loop(1, devices, small_start, 0)
        inner = [list(owner.inward()) for owner in owners]
        for steps in inner:
            for step in steps[:-1]:
                step()

        def part(peer, origin):
            return send_to(
                qkv_sum.at[pl.ds(pl.multiple_of(peer * part_rows, 16), part_rows)],
                qkv_out.at[origin],
                part_send.at[peer],
                part_recv.at[origin],
                (dp, peer),
            )

        own_part = pltpu.make_async_copy(
            qkv_sum.at[pl.ds(pl.multiple_of(me * part_rows, 16), part_rows)], qkv_out.at[me], own_sem.at[0]
        )
        goal = me * ndp + dp
        stays = goal == rank
        own_move = pltpu.make_async_copy(proj_sum, proj_out, own_sem.at[1])

        def move():
            return send_to(proj_sum, proj_out, move_send, move_recv, device(goal))

        steps = woven(*[p.inward() for p in programs])
        half = len(steps) // 2
        for step in steps[:half]:
            step()
        for owner_steps in inner:
            owner_steps[-1]()
        own_part.start()
        for step in range(1, seq):
            part(lax.rem(me + step, seq), me).start()
        pl.when(stays)(own_move.start)
        pl.when(jnp.logical_not(stays))(lambda: move().start())
        for step in steps[half:]:
            step()

        got[rank] = packed_ref[rank]

        def small_end(step, carry):
            small(lax.rem(rank + step, devices), rank).wait_send()
            source = lax.rem(rank + devices - step, devices)
            small(source, source).wait_recv()
            return carry

        lax.fori_loop(1, devices, small_end, 0)
        sum_out[...] = jnp.sum(got[...], axis=0)
        for program in (*programs, *owners):
            program.finish()
        for step in range(1, seq):
            part(lax.rem(me + step, seq), me).wait_send()
            source = lax.rem(me + seq - step, seq)
            part(source, source).wait_recv()
        own_part.wait()

        @pl.when(stays)
        def _():
            own_move.wait()

        @pl.when(jnp.logical_not(stays))
        def _():
            move().wait_send()
            move().wait_recv()

    dma = pltpu.SemaphoreType.DMA
    vmem = pl.BlockSpec(memory_space=pltpu.VMEM)

    def over_dp_scratch(array):
        return Reduce.scratch([(0, array.shape[1])], 2, ndp // 2, array.shape[2])

    return pl.pallas_call(
        kernel,
        out_shape=[
            jax.ShapeDtypeStruct((rows, width), F32),
            jax.ShapeDtypeStruct((seq, part_rows, cols), BF),
            jax.ShapeDtypeStruct((proj_rows, width), BF),
            jax.ShapeDtypeStruct(packed.shape[1:], F32),
        ],
        in_specs=[vmem] * 4,
        out_specs=[vmem] * 4,
        scratch_shapes=reduce_scratch(seq, rows, width)
        + [
            pltpu.VMEM(qkv_terms.shape, BF),
            pltpu.VMEM(qkv_terms.shape[1:], BF),
            pltpu.VMEM(proj_terms.shape, BF),
            pltpu.VMEM(proj_terms.shape[1:], BF),
            pltpu.VMEM(packed.shape, F32),
        ]
        + over_dp_scratch(qkv_terms)
        + over_dp_scratch(proj_terms)
        + [dma((seq,)), dma((seq,)), dma, dma, dma((devices,)), dma((devices,)), dma((2,))],
        compiler_params=pltpu.CompilerParams(
            collective_id=collective_id, has_side_effects=True, vmem_limit_bytes=VMEM_MOST
        ),
        name="last_transfers",
        cost_estimate=cost_of(100),
    )(terms, qkv_terms, proj_terms, packed)


def packed_rows(parts, sublanes):
    flat = jnp.concatenate(parts, axis=1)
    fill = -flat.shape[1] % (sublanes * 128)
    return jnp.pad(flat, ((0, 0), (0, fill))).reshape(flat.shape[0], -1, 128)


def rms_factor(values):
    return lax.rsqrt(jnp.mean(values * values, axis=-1, keepdims=True) + NORM_EPS)


def norm_back(values, factor, gain_row, incoming):
    scaled = incoming * gain_row
    gain_part = jnp.sum(incoming * values * factor, axis=0)
    inner = jnp.mean(scaled * values, axis=-1, keepdims=True)
    return (factor * (scaled - values * factor * factor * inner), gain_part)


def rotary(positions):
    half_dim = HEAD_DIM // 2
    freqs = jnp.exp(
        -math.log(ROPE_BASE) * (2.0 * jnp.arange(half_dim, dtype=F32) / HEAD_DIM)
    )
    angles = positions.astype(F32)[:, None] * freqs[None, :]
    return (jnp.cos(angles)[:, None, :], jnp.sin(angles)[:, None, :])


def rotate(values, cosine, sine):
    half_dim = values.shape[-1] // 2
    first = values[..., :half_dim]
    second = values[..., half_dim:]
    return jnp.concatenate(
        [first * cosine - second * sine, second * cosine + first * sine], axis=-1
    )


def attend_forward(pieces):
    queries, key_rows, value_rows, seg_ids = pieces
    score_scale = HEAD_DIM ** (-0.5)
    scores = jnp.einsum("qhd,khd->hqk", queries, key_rows, preferred_element_type=F32) * score_scale
    allowed = seg_ids[None, :] <= seg_ids[:, None]
    scores = jnp.where(allowed[None], scores, MASKED_SCORE)
    row_max = jnp.max(scores, axis=-1, keepdims=True)
    exp_scores = jnp.exp(scores - row_max)
    row_sum = jnp.sum(exp_scores, axis=-1, keepdims=True)
    attn_probs = exp_scores / row_sum
    attended = jnp.einsum(
        "hqk,khd->qhd", attn_probs.astype(BF), value_rows, preferred_element_type=F32
    )
    return (attended.astype(BF), (row_max + jnp.log(row_sum))[..., 0])


def attend_backward(pieces):
    queries, key_rows, value_rows, grad_out, log_norm, seg_ids = pieces
    score_scale = HEAD_DIM ** (-0.5)
    scores = jnp.einsum("qhd,khd->hqk", queries, key_rows, preferred_element_type=F32) * score_scale
    allowed = seg_ids[None, :] <= seg_ids[:, None]
    attn_probs = jnp.where(allowed[None], jnp.exp(scores - log_norm[..., None]), 0.0)
    grad_probs = jnp.einsum("qhd,khd->hqk", grad_out, value_rows, preferred_element_type=F32)
    inner = jnp.sum(attn_probs * grad_probs, axis=-1, keepdims=True)
    grad_scores = (attn_probs * (grad_probs - inner)).astype(BF)
    grad_query = (
        jnp.einsum("hqk,khd->qhd", grad_scores, key_rows, preferred_element_type=F32) * score_scale
    )
    grad_key = (
        jnp.einsum("hqk,qhd->khd", grad_scores, queries, preferred_element_type=F32) * score_scale
    )
    grad_value = jnp.einsum(
        "hqk,qhd->khd", attn_probs.astype(BF), grad_out, preferred_element_type=F32
    )
    return (grad_query.astype(BF), grad_key.astype(BF), grad_value.astype(BF))


def swiglu(gate_vals, up_vals):
    return jax.nn.silu(gate_vals) * up_vals


def local(
    tokens,
    segments,
    routes,
    cotangent,
    attn_weight,
    router_weight,
    norm_gains,
    expert_in,
    expert_out,
):
    num_seqs, local_len, width = tokens.shape
    seq_length = segments.shape[1]
    seq, ndp = lax.axis_size("seq"), lax.axis_size("dp")
    me = lax.axis_index("seq")
    devices = seq * ndp
    heads_here = HEADS // seq
    cols = heads_here * HEAD_DIM
    tok = num_seqs * local_len
    group = tok * seq
    own_rows = attn_weight.shape[0]
    experts_all = router_weight.shape[1]
    experts = experts_all // seq
    top = routes.shape[-1]
    capacity = (9 * tok * top + 8 * experts_all - 1) // (8 * experts_all)

    n_router, n_gain = own_rows * experts_all, 4 * own_rows
    token_rows = tokens.reshape(tok, width)
    x_all, qkv_got, proj_got, small_all, routes_all = first_transfers(
        token_rows,
        attn_weight[:, :3].reshape(own_rows, 3, seq, cols).transpose(2, 1, 0, 3),
        attn_weight[:, 3],
        packed_rows([router_weight.reshape(1, -1), norm_gains.reshape(1, -1)], 16)[0],
        routes.reshape(-1, 128),
        1,
    )
    expert_in, expert_out, small_all = lax.optimization_barrier((expert_in, expert_out, small_all))
    in_full = lax.all_gather(expert_in, "dp", axis=1, tiled=True)
    out_full = lax.all_gather(expert_out, "dp", axis=2, tiled=True)
    small_all = small_all.reshape(devices, -1)
    router_full = small_all[:, :n_router].reshape(width, experts_all)
    gain_rows = (
        small_all[:, n_router : n_router + n_gain]
        .reshape(devices, 4, own_rows)
        .transpose(1, 0, 2)
        .reshape(4, width)
        .astype(F32)
    )
    routes_all = routes_all.reshape(seq, tok, top)
    qkv_weight = qkv_got.transpose(2, 0, 1, 3, 4).reshape(3, width, cols)
    proj_weight = proj_got.reshape(cols, width)

    resid_in = token_rows.astype(F32)
    factor_attn = rms_factor(resid_in)
    group_in = x_all.reshape(group, width).astype(F32)
    normed_all = (group_in * rms_factor(group_in) * gain_rows[0]).astype(BF)
    raw = jnp.einsum("td,jde->jte", normed_all, qkv_weight, preferred_element_type=F32)
    squares = jnp.sum(raw[:2] * raw[:2], axis=-1).reshape(1, -1, 128)
    (sums,) = small_exchange([squares], ("seq",), 4)
    factors = lax.rsqrt(jnp.sum(sums, axis=0).reshape(2, group, 1) / width + NORM_EPS)
    head_gains = lax.dynamic_slice_in_dim(gain_rows, me * cols, cols, axis=1)

    position = (
        jnp.arange(seq, dtype=jnp.int32)[:, None, None] * local_len
        + jnp.zeros((1, num_seqs, 1), jnp.int32)
        + jnp.arange(local_len, dtype=jnp.int32)[None, None, :]
    ).reshape(group)
    cosine, sine = rotary(position)

    def to_heads(values):
        return values.reshape(group, heads_here, HEAD_DIM)

    def by_sequence(values):
        return (
            values.reshape(seq, num_seqs, local_len, heads_here, HEAD_DIM)
            .transpose(1, 0, 2, 3, 4)
            .reshape(num_seqs, seq_length, heads_here, HEAD_DIM)
        )

    def by_source(values):
        return (
            values.reshape(num_seqs, seq, local_len, cols).transpose(1, 0, 2, 3).reshape(group, cols)
        )

    qn = raw[0] * factors[0] * head_gains[1]
    kn = raw[1] * factors[1] * head_gains[2]
    query_head = by_sequence(rotate(to_heads(qn), cosine, sine).astype(BF))
    key_head = by_sequence(rotate(to_heads(kn), cosine, sine).astype(BF))
    value_head = by_sequence(raw[2].astype(BF))
    attended, log_norm = lax.map(attend_forward, (query_head, key_head, value_head, segments))
    o_head = by_source(attended.reshape(num_seqs, seq_length, cols))
    z_terms = jnp.dot(o_head, proj_weight, preferred_element_type=F32).astype(BF)
    z = seq_reduce(z_terms.reshape(seq, tok, width), 5)

    middle = resid_in + z
    factor_ffn = rms_factor(middle)
    ffn_low = (middle * factor_ffn * gain_rows[3]).astype(BF)
    ffn_all = seq_gather(ffn_low, 6)
    cot_low = cotangent.reshape(tok, width)
    cot_all = seq_gather(cot_low, 7)

    logits_all = jnp.einsum("std,de->ste", ffn_all, router_full, preferred_element_type=F32)
    probs_all = jax.nn.softmax(logits_all, axis=-1)
    here = me * experts + jnp.arange(experts, dtype=jnp.int32)
    hits = jnp.any(routes_all[:, :, :, None] == here, axis=2)
    token_ids = jnp.arange(tok, dtype=jnp.int32)
    earlier = (token_ids[:, None] > token_ids[None, :]).astype(BF)
    slot = jnp.einsum("tu,sue->ste", earlier, hits.astype(BF), preferred_element_type=F32)
    slot = jnp.where(hits, slot, float(tok + 1)).astype(jnp.int32)
    place = slot.transpose(2, 0, 1)[:, :, None, :] == jnp.arange(capacity, dtype=jnp.int32)[
        None, None, :, None
    ]
    place_low = place.astype(BF)
    probs_here = lax.dynamic_slice_in_dim(probs_all, me * experts, experts, axis=2).transpose(2, 0, 1)
    place_gate = jnp.where(place, probs_here[:, :, None, :], 0.0)
    slot_gate = jnp.sum(place_gate, axis=-1)
    slots = seq * capacity
    rows = (
        jnp.einsum("esjt,std->esjd", place_low, ffn_all, preferred_element_type=F32)
        .astype(BF)
        .reshape(experts, slots, width)
    )
    cot_rows = jnp.einsum("esjt,std->esjd", place_low, cot_all, preferred_element_type=F32).reshape(
        experts, slots, width
    )

    gate_up = jnp.einsum("erd,edjf->erjf", rows, in_full, preferred_element_type=F32)
    hidden_f, swiglu_pull = jax.vjp(swiglu, gate_up[:, :, 0], gate_up[:, :, 1])
    hidden = hidden_f.astype(BF)
    expert_res = jnp.einsum("erf,efd->erd", hidden, out_full, preferred_element_type=F32).astype(BF)
    mixed_terms = jnp.einsum(
        "esjt,esjd->std",
        place_gate.astype(BF),
        expert_res.reshape(experts, seq, capacity, width),
        preferred_element_type=F32,
    ).astype(BF)
    mixed = seq_reduce(mixed_terms, 8)
    block_out = (middle + mixed).astype(BF).reshape(num_seqs, local_len, width)

    slot_dgate = jnp.sum(cot_rows * expert_res.astype(F32), axis=-1).reshape(experts, seq, capacity)
    grad_prob_here = jnp.sum(jnp.where(place, slot_dgate[..., None], 0.0), axis=2)
    grad_res = (cot_rows * slot_gate.reshape(experts, slots, 1)).astype(BF)
    grad_hidden = jnp.einsum("erd,efd->erf", grad_res, out_full, preferred_element_type=F32)
    grad_gatev, grad_upv = swiglu_pull(grad_hidden)
    grad_gu = jnp.stack([grad_gatev, grad_upv], axis=2).astype(BF)
    grad_rows = jnp.einsum("erjf,edjf->erd", grad_gu, in_full, preferred_element_type=F32).astype(BF)
    out_term = jnp.einsum("erf,erd->efd", hidden, grad_res, preferred_element_type=F32).astype(BF)
    in_term = jnp.einsum("erd,erjf->edjf", rows, grad_gu, preferred_element_type=F32).astype(BF)
    out_term, in_term, grad_rows = lax.optimization_barrier((out_term, in_term, grad_rows))
    expert_out_grad = lax.psum_scatter(out_term, "dp", scatter_dimension=2, tiled=True).astype(F32)
    expert_in_grad = lax.psum_scatter(in_term, "dp", scatter_dimension=1, tiled=True).astype(F32)
    dffn_terms = jnp.einsum(
        "esjt,esjd->std",
        place_low,
        grad_rows.reshape(experts, seq, capacity, width),
        preferred_element_type=F32,
    ).astype(BF)
    grad_ffn = seq_reduce(dffn_terms, 9)
    (grad_prob,) = small_exchange(
        [grad_prob_here.transpose(1, 0, 2).reshape(seq, -1, 128)], ("seq",), 10
    )
    grad_prob = grad_prob.reshape(experts_all, tok).T

    route_probs = jax.nn.softmax(
        jnp.dot(ffn_low, router_full, preferred_element_type=F32), axis=-1
    )
    grad_logits = (
        route_probs * (grad_prob - jnp.sum(route_probs * grad_prob, axis=-1, keepdims=True))
    ).astype(BF)
    router_term = jnp.einsum("td,te->de", ffn_low, grad_logits, preferred_element_type=F32)
    grad_ffn = grad_ffn + jnp.einsum(
        "te,de->td", grad_logits, router_full, preferred_element_type=F32
    )
    grad_middle, gain_ffn = norm_back(middle, factor_ffn, gain_rows[3], grad_ffn)
    grad_middle = grad_middle + cot_low.astype(F32)

    dz_all = seq_gather(grad_middle.astype(BF), 11).reshape(group, width)
    grad_o = jnp.einsum("te,de->td", dz_all, proj_weight, preferred_element_type=F32).astype(BF)
    proj_term = jnp.einsum("td,te->de", o_head, dz_all, preferred_element_type=F32).astype(BF)
    grad_q, grad_k, grad_v = lax.map(
        attend_backward,
        (query_head, key_head, value_head, by_sequence(grad_o), log_norm, segments),
    )
    flat = (num_seqs, seq_length, cols)
    grad_qn = rotate(to_heads(by_source(grad_q.reshape(flat)).astype(F32)), cosine, -sine).reshape(
        group, cols
    )
    grad_kn = rotate(to_heads(by_source(grad_k.reshape(flat)).astype(F32)), cosine, -sine).reshape(
        group, cols
    )
    grad_n = jnp.stack([grad_qn, grad_kn])
    scaled = grad_n * head_gains[1:3, None, :]
    inner = jnp.sum(scaled * raw[:2], axis=-1).reshape(1, -1, 128)
    (inners,) = small_exchange([inner], ("seq",), 12)
    inner = jnp.sum(inners, axis=0).reshape(2, group, 1) / width
    gain_heads = jnp.sum(grad_n * raw[:2] * factors, axis=1)
    grad_raw = factors * (scaled - raw[:2] * factors * factors * inner)
    grad_stack = jnp.concatenate(
        [grad_raw.astype(BF), by_source(grad_v.reshape(flat))[None]], axis=0
    )
    dn_terms = jnp.einsum("jte,jde->td", grad_stack, qkv_weight, preferred_element_type=F32).astype(BF)
    qkv_term = jnp.einsum("td,jte->jde", normed_all, grad_stack, preferred_element_type=F32)
    gain_attn = jnp.sum(qkv_term * qkv_weight.astype(F32), axis=(0, 2)) / gain_rows[0]

    gain_heads = lax.dynamic_update_slice_in_dim(jnp.zeros((2, width), F32), gain_heads, me * cols, axis=1)
    gain_term = jnp.concatenate([gain_attn[None], gain_heads, gain_ffn[None]], axis=0)
    gain_send = gain_term.reshape(4, devices, own_rows).transpose(1, 0, 2)
    grad_normed, qkv_out, proj_grad, total = last_transfers(
        dn_terms.reshape(seq, tok, width),
        qkv_term.astype(BF)
        .reshape(3, ndp, seq, own_rows, cols)
        .transpose(1, 2, 0, 3, 4)
        .reshape(ndp, seq * 3 * own_rows, cols),
        proj_term.reshape(ndp, own_rows, width),
        packed_rows([router_term.reshape(devices, -1), gain_send.reshape(devices, -1)], 8),
        14,
    )
    grad_resid, _ = norm_back(resid_in, factor_attn, gain_rows[0], grad_normed)
    input_grad = (grad_resid + grad_middle).reshape(num_seqs, local_len, width)
    qkv_grad = qkv_out.reshape(seq, 3, own_rows, cols).transpose(2, 1, 0, 3).reshape(own_rows, 3, width)
    attn_grad = jnp.concatenate([qkv_grad, proj_grad[:, None, :]], axis=1).astype(F32)
    total = total.reshape(-1)
    router_grad = total[:n_router].reshape(own_rows, experts_all)
    gain_grad = total[n_router : n_router + n_gain].reshape(4, own_rows)
    return (
        block_out,
        input_grad,
        attn_grad,
        router_grad,
        gain_grad,
        expert_in_grad,
        expert_out_grad,
    )


def solution(mesh):
    in_specs = (
        P("dp", "seq", None),
        P("dp", None),
        P("dp", "seq", None),
        P("dp", "seq", None),
        P(("dp", "seq"), None, None),
        P(("dp", "seq"), None),
        P(None, ("dp", "seq")),
        P("seq", "dp", None, None),
        P("seq", None, "dp"),
    )
    out_specs = (
        P("dp", "seq", None),
        P("dp", "seq", None),
        P(("dp", "seq"), None, None),
        P(("dp", "seq"), None),
        P(None, ("dp", "seq")),
        P("seq", "dp", None, None),
        P("seq", None, "dp"),
    )
    return jax.shard_map(local, mesh=mesh, in_specs=in_specs, out_specs=out_specs, check_vma=False)
```

```python
import math

import jax
import jax.numpy as jnp
from jax import lax
from jax.experimental import pallas as pl
from jax.experimental.pallas import tpu as pltpu
from jax.sharding import PartitionSpec as P

HEADS = 16
HEAD_DIM = 128
NORM_EPS = 1e-05
ROPE_BASE = 10000.0
MASKED_SCORE = -1e30
BF = jnp.bfloat16
F32 = jnp.float32
MESH = pl.DeviceIdType.MESH
VMEM_MOST = 60 << 20


class Line:
    def __init__(self, size, place, device):
        self.size, self.place, self.device = size, place, device

    def has(self, turn):
        return self.place < self.size - 1 if turn > 0 else self.place > 0

    def inside(self, place):
        return (place >= 0) & (place < self.size)


def grid_of(seq_size):
    lines = 4 if seq_size % 4 == 0 else 1
    return lines, seq_size // lines


def seq_lines():
    dp, me = lax.axis_index("dp"), lax.axis_index("seq")
    nz, ny = grid_of(lax.axis_size("seq"))
    along = Line(nz, lax.div(me, ny), lambda turn: (dp, me + turn * ny))
    across = Line(ny, lax.rem(me, ny), lambda turn: (dp, me + turn))
    return along, across, me, lambda z, y: z * ny + y


def dp_lines():
    dp, me = lax.axis_index("dp"), lax.axis_index("seq")
    along = Line(lax.axis_size("dp") // 2, lax.div(dp, 2), lambda turn: (dp + 2 * turn, me))
    across = Line(2, lax.rem(dp, 2), lambda turn: (dp + turn, me))
    return along, across, dp, lambda x, core: 2 * x + core


def cost_of(microseconds):
    return pl.CostEstimate(flops=0, bytes_accessed=microseconds * 3_600_000, transcendentals=0)


def send_to(src, dst, send_sem, recv_sem, device):
    return pltpu.make_async_remote_copy(
        src_ref=src,
        dst_ref=dst,
        send_sem=send_sem,
        recv_sem=recv_sem,
        device_id=device,
        device_id_type=MESH,
    )


def greet(targets):
    barrier = pltpu.get_barrier_semaphore()
    count = 0
    for cond, device in targets:

        @pl.when(cond)
        def _(device=device):
            pl.semaphore_signal(barrier, 1, device_id=device, device_id_type=MESH)

        count = count + cond.astype(jnp.int32)
    pl.semaphore_wait(barrier, count)


def greet_lines(*lines):
    greet([(line.has(turn), line.device(turn)) for line in lines for turn in (1, -1)])


def cuts_of(rows, ny):
    unit = rows // 16
    late = max(1, unit * 3 // 16) if ny == 2 else unit // 2
    early = unit - late
    half = (early + 1) // 2
    firsts = [(0, half * 16)] + ([(half * 16, (early - half) * 16)] if early > half else [])
    return firsts, [(early * 16, late * 16)]


class Gather:
    def __init__(self, first, second, me, flat, pieces, own, slot, send_sem, recv_sem, ready=None):
        self.first, self.second, self.me, self.flat = first, second, me, flat
        self.pieces, self.own, self.slot = pieces, own, slot
        self.send_sem, self.recv_sem, self.ready = send_sem, recv_sem, ready
        self.sent = []

    def _copy(self, src, origin, h, line, turn):
        way = (0 if line is self.first else 2) + (turn > 0)
        return send_to(
            src,
            self.slot(origin, h),
            self.send_sem.at[origin, h, way],
            self.recv_sem.at[origin, h],
            line.device(turn),
        )

    def _send(self, src, origin, h, line, turn, cond):
        ok = cond & line.has(turn)
        pl.when(ok)(lambda: self._copy(src, origin, h, line, turn).start())
        self.sent.append((ok, src, origin, h, line, turn))

    def start(self):
        for h in range(self.pieces):
            if self.ready is not None:
                self.ready(h)
            for line in (self.first, self.second):
                for turn in (1, -1):
                    self._send(self.own(h), self.me, h, line, turn, self.me >= 0)

    def _arrive(self, place, side, h, sends):
        first, second = self.first, self.second
        cond = first.inside(place) & second.inside(side)
        origin = lax.select(cond, self.flat(place, side), self.me)

        @pl.when(cond)
        def _():
            self._copy(self.slot(origin, h), origin, h, first, 1).wait_recv()

        for line, turn in sends:
            self._send(self.slot(origin, h), origin, h, line, turn, cond)

    def steps(self):
        first, second = self.first, self.second
        listed = []
        for far in range(1, first.size):
            for h in range(self.pieces):
                for sign in (1, -1):
                    listed.append(
                        (
                            far,
                            lambda far=far, h=h, sign=sign: self._arrive(
                                first.place - sign * far,
                                second.place,
                                h,
                                [(first, sign), (second, 1), (second, -1)],
                            ),
                        )
                    )
        for step in range(1, second.size):
            for far in range(first.size):
                for h in range(self.pieces):
                    for sign in (1, -1) if far else (1,):
                        for turn in (1, -1):
                            listed.append(
                                (
                                    far + step + 0.5,
                                    lambda far=far, step=step, h=h, sign=sign, turn=turn: self._arrive(
                                        first.place - sign * far,
                                        second.place - turn * step,
                                        h,
                                        [(second, turn)] if step < second.size - 1 else [],
                                    ),
                                )
                            )
        return listed

    def finish(self):
        for ok, src, origin, h, line, turn in self.sent:
            pl.when(ok)(lambda: self._copy(src, origin, h, line, turn).wait_send())


def run_steps(*programs):
    for _, step in sorted((s for p in programs for s in p.steps()), key=lambda s: s[0]):
        step()


def seq_gathers(block_ref, out_ref, sems):
    along, across, me, flat = seq_lines()
    early, late = cuts_of(block_ref.shape[0], across.size)
    made = []
    for cuts, first, second, index, (send_sem, recv_sem) in (
        (early, along, across, flat, sems[0:2]),
        (late, across, along, lambda y, z: flat(z, y), sems[2:4]),
    ):
        made.append(
            Gather(
                first,
                second,
                me,
                index,
                len(cuts),
                lambda h, cuts=cuts: block_ref.at[pl.ds(*cuts[h])],
                lambda origin, h, cuts=cuts: out_ref.at[origin, pl.ds(*cuts[h])],
                send_sem,
                recv_sem,
            )
        )
    return made


def gather_sems(seq, rows):
    early, late = cuts_of(rows, grid_of(seq)[1])
    return [
        pltpu.SemaphoreType.DMA((seq, len(early), 4)),
        pltpu.SemaphoreType.DMA((seq, len(early))),
        pltpu.SemaphoreType.DMA((seq, len(late), 4)),
        pltpu.SemaphoreType.DMA((seq, len(late))),
    ]


def seq_gather(block, collective_id):
    rows, width = block.shape
    seq = lax.axis_size("seq")

    def kernel(x_ref, o_ref, local_sem, *sems):
        along, across, me, _ = seq_lines()
        greet_lines(along, across)
        own = pltpu.make_async_copy(x_ref, o_ref.at[me], local_sem)
        own.start()
        programs = seq_gathers(x_ref, o_ref, sems)
        for program in programs:
            program.start()
        run_steps(*programs)
        for program in programs:
            program.finish()
        own.wait()

    return pl.pallas_call(
        kernel,
        out_shape=jax.ShapeDtypeStruct((seq, rows, width), block.dtype),
        in_specs=[pl.BlockSpec(memory_space=pl.ANY)],
        out_specs=pl.BlockSpec(memory_space=pl.ANY),
        scratch_shapes=[pltpu.SemaphoreType.DMA] + gather_sems(seq, rows),
        compiler_params=pltpu.CompilerParams(collective_id=collective_id, has_side_effects=True),
        name="seq_gather",
        cost_estimate=cost_of(80),
    )(block)


class Reduce:
    def __init__(self, first, second, me, flat, cuts, terms, acc, out, from_first, from_second, sems):
        self.first, self.second, self.me, self.flat, self.cuts = first, second, me, flat, cuts
        self.terms, self.acc, self.out = terms, acc, out
        self.from_first, self.from_second = from_first, from_second
        self.send_sem, self.first_sem, self.second_sem = sems
        self.base = cuts[0][0]
        self.sent = []

    @staticmethod
    def scratch(rows_of, first_size, second_size, width):
        seq, rows, pieces = first_size * second_size, sum(r for _, r in rows_of), len(rows_of)
        lanes = 1 if first_size == 2 else 2
        return [
            pltpu.VMEM((lanes, seq, rows, width), BF),
            pltpu.VMEM((2, second_size, rows, width), BF),
            pltpu.SemaphoreType.DMA((seq, pieces)),
            pltpu.SemaphoreType.DMA((lanes, seq, pieces)),
            pltpu.SemaphoreType.DMA((2, second_size, pieces)),
        ]

    def _lane(self, turn):
        return 0 if self.first.size == 2 or turn > 0 else 1

    def _cut(self, h):
        return pl.ds(*self.cuts[h])

    def _inner(self, h):
        return pl.ds(self.cuts[h][0] - self.base, self.cuts[h][1])

    def _copy(self, src, dest, spot, h, line, turn):
        if line is self.first:
            lane = self._lane(turn)
            dst, sem = self.from_first.at[lane, dest, self._inner(h)], self.first_sem.at[lane, dest, h]
        else:
            side = 0 if turn > 0 else 1
            dst, sem = self.from_second.at[side, spot, self._inner(h)], self.second_sem.at[side, spot, h]
        return send_to(src, dst, self.send_sem.at[dest, h], sem, line.device(turn))

    def _send(self, src, dest, spot, h, line, turn, ok):
        pl.when(ok)(lambda: self._copy(src, dest, spot, h, line, turn).start())
        self.sent.append((ok, src, dest, spot, h, line, turn))

    def _add(self, cond, whole, parts, out, h):
        first, count = self.cuts[h]

        @pl.when(cond)
        def _():
            def body(i, carry):
                at = pl.ds(pl.multiple_of(first + i * 16, 16), 16)
                inner = pl.ds(pl.multiple_of(first - self.base + i * 16, 16), 16)
                total = None
                for ref in whole:
                    total = ref[at, :].astype(F32) if total is None else total + ref[at, :].astype(F32)
                for ref in parts:
                    total = total + ref[inner, :].astype(F32)
                out[at, :] = total.astype(out.dtype)
                return carry

            lax.fori_loop(0, count // 16, body, 0)

    def _spread(self):
        for far in range(self.second.size - 1, -1, -1):
            for sign in (1, -1) if far else (1,):
                spot = self.second.place + sign * far
                yield far, sign, spot, self.second.inside(spot)

    def outward(self):
        first = self.first
        for step in range(first.size - 1, 0, -1):
            for far, sign, spot, ok in self._spread():
                for h in range(len(self.cuts)):
                    for turn in (1, -1):
                        yield lambda a=(step, spot, ok, h, turn): self._pass_on(*a)

    def _pass_on(self, step, spot, ok, h, turn):
        first = self.first
        goal = first.place + turn * step
        go = ok & first.inside(goal)
        dest = lax.select(go, self.flat(goal, spot), self.me)
        if first.size == 2:
            self._send(self.terms.at[dest, self._cut(h)], dest, spot, h, first, turn, go)
            return
        behind = first.has(-turn)
        self._await(go & behind, dest, spot, h, first, turn)
        self._add(go & behind, [self.terms.at[dest]], [self.from_first.at[self._lane(turn), dest]], self.acc.at[dest], h)
        self._add(go & jnp.logical_not(behind), [self.terms.at[dest]], [], self.acc.at[dest], h)
        self._send(self.acc.at[dest, self._cut(h)], dest, spot, h, first, turn, go)

    def _await(self, cond, dest, spot, h, line, turn):
        @pl.when(cond)
        def _():
            self._copy(self.acc.at[dest, self._cut(h)], dest, spot, h, line, turn).wait_recv()

    def inward(self):
        for far, sign, spot, ok in self._spread():
            for h in range(len(self.cuts)):
                yield lambda a=(far, sign, spot, ok, h): self._collect(*a)

    def _collect(self, far, sign, spot, ok, h):
        first, second, acc = self.first, self.second, self.acc
        dest = lax.select(ok, self.flat(first.place, spot), self.me)
        for turn in (1, -1):
            self._await(ok & first.has(-turn), dest, spot, h, first, turn)
        if first.size == 2:
            self._add(ok, [self.terms.at[dest]], [self.from_first.at[0, dest]], acc.at[dest], h)
        else:
            low, high = first.has(-1), first.has(1)
            lows, highs = self.from_first.at[self._lane(1), dest], self.from_first.at[self._lane(-1), dest]
            self._add(ok & low & high, [self.terms.at[dest]], [lows, highs], acc.at[dest], h)
            self._add(ok & low & jnp.logical_not(high), [self.terms.at[dest]], [lows], acc.at[dest], h)
            self._add(ok & high & jnp.logical_not(low), [self.terms.at[dest]], [highs], acc.at[dest], h)
        if far:
            behind = second.has(-sign)
            side = 0 if sign > 0 else 1
            self._await(ok & behind, dest, spot, h, second, sign)
            self._add(ok & behind, [acc.at[dest]], [self.from_second.at[side, spot]], acc.at[dest], h)
            self._send(acc.at[dest, self._cut(h)], dest, spot, h, second, sign, ok)
            return
        low, high = second.has(-1), second.has(1)
        self._await(low, dest, spot, h, second, 1)
        self._await(high, dest, spot, h, second, -1)
        lows, highs = self.from_second.at[0, spot], self.from_second.at[1, spot]
        self._add(low & high, [acc.at[dest]], [lows, highs], self.out, h)
        self._add(low & jnp.logical_not(high), [acc.at[dest]], [lows], self.out, h)
        self._add(high & jnp.logical_not(low), [acc.at[dest]], [highs], self.out, h)

    def finish(self):
        for ok, src, dest, spot, h, line, turn in self.sent:
            pl.when(ok)(lambda: self._copy(src, dest, spot, h, line, turn).wait_send())


def woven(*lists):
    keyed = [((i + 1) / len(entries), n, entry) for n, entries in enumerate(map(list, lists)) for i, entry in enumerate(entries)]
    return [entry for _, _, entry in sorted(keyed, key=lambda k: k[:2])]


def seq_reduces(terms, acc, out, scratch):
    along, across, me, flat = seq_lines()
    early, late = cuts_of(terms.shape[1], across.size)
    return [
        Reduce(across, along, me, lambda y, z: flat(z, y), early, terms, acc, out, *scratch[0:2], scratch[2:5]),
        Reduce(along, across, me, flat, late, terms, acc, out, *scratch[5:7], scratch[7:10]),
    ]


def reduce_scratch(seq, rows, width):
    nz, ny = grid_of(seq)
    early, late = cuts_of(rows, ny)
    return (
        [pltpu.VMEM((seq, rows, width), BF)]
        + Reduce.scratch(early, ny, nz, width)
        + Reduce.scratch(late, nz, ny, width)
    )


def seq_reduce(terms, collective_id):
    seq, rows, width = terms.shape

    def kernel(p_ref, o_ref, acc, *scratch):
        along, across, _, _ = seq_lines()
        greet_lines(along, across)
        programs = seq_reduces(p_ref, acc, o_ref, scratch)
        for step in woven(*[p.outward() for p in programs]):
            step()
        for step in woven(*[p.inward() for p in programs]):
            step()
        for program in programs:
            program.finish()

    return pl.pallas_call(
        kernel,
        out_shape=jax.ShapeDtypeStruct((rows, width), F32),
        in_specs=[pl.BlockSpec(memory_space=pltpu.VMEM)],
        out_specs=pl.BlockSpec(memory_space=pltpu.VMEM),
        scratch_shapes=reduce_scratch(seq, rows, width),
        compiler_params=pltpu.CompilerParams(
            collective_id=collective_id, has_side_effects=True, vmem_limit_bytes=VMEM_MOST
        ),
        name="seq_reduce",
        cost_estimate=cost_of(80),
    )(terms)


def rotary_tables(length):
    half_dim = HEAD_DIM // 2
    freqs = jnp.exp(-math.log(ROPE_BASE) * (2.0 * jnp.arange(half_dim, dtype=F32) / HEAD_DIM))
    angles = jnp.arange(length, dtype=jnp.int32).astype(F32)[:, None] * freqs[None, :]
    cosine, sine = jnp.cos(angles), jnp.sin(angles)
    return jnp.concatenate([cosine, cosine], axis=1), jnp.concatenate([-sine, sine], axis=1)


def turn_heads(values, cosine, sine):
    return values * cosine + pltpu.roll(values, HEAD_DIM // 2, 1) * sine


def as_columns(row):
    return jnp.broadcast_to(row, (128, row.shape[1])).T


def as_row(column):
    return jnp.broadcast_to(column, (column.shape[0], 128)).T[0:1]


def dot_rows(a, b):
    return lax.dot_general(a, b, (((1,), (1,)), ((), ())), preferred_element_type=F32)


def attend_first(tokens, cotangent, qkv_rows, proj_rows, packed, routes, tables, segments, n_router, collective_id):
    seq, ndp = lax.axis_size("seq"), lax.axis_size("dp")
    devices = seq * ndp
    rows, width = tokens.shape
    _, _, own_rows, cols = qkv_rows.shape
    num_seqs, length = segments.shape
    local_len = length // seq
    heads_here = cols // HEAD_DIM
    tile = 256
    per_block = 128 // own_rows

    def kernel(*refs):
        (x_ref, c_ref, qkv_ref, proj_ref, packed_ref, routes_ref, cos_ref, sin_ref, col_ref, row_ref) = refs[:10]
        (normed_out, c_out, w_v, proj_out, packed_out, routes_out) = refs[10:16]
        (raw_out, q_out, k_out, v_out, o_out, total_out) = refs[16:22]
        (x_v, normed_v, gains_v, sums_v, sums_got, local_sem, normed_sem) = refs[22:29]
        (part_send, part_recv, own_sem, qkv_send, qkv_recv, proj_send, proj_recv, proj_fwd) = refs[29:37]
        (small_send, small_recv, routes_send, routes_recv, sums_send, sums_recv) = refs[37:43]
        x_sems, c_sems = refs[43:47], refs[47:51]
        along, across, me, _ = seq_lines()
        x_line, core_line, dp, dp_flat = dp_lines()
        rank = dp * seq + me
        barrier = pltpu.get_barrier_semaphore()

        def device(peer):
            return (lax.div(peer, seq), lax.rem(peer, seq))

        def meet(step, carry):
            pl.semaphore_signal(
                barrier, 1, device_id=device(lax.rem(rank + step, devices)), device_id_type=MESH
            )
            return carry

        lax.fori_loop(1, devices, meet, 0)
        pl.semaphore_wait(barrier, devices - 1)

        def weight_rows(origin, h):
            return w_v.at[:, pl.ds(pl.multiple_of((origin * seq + h) * own_rows, own_rows), own_rows), :]

        own_x = pltpu.make_async_copy(x_ref, x_v.at[me], local_sem.at[0])
        own_c = pltpu.make_async_copy(c_ref, c_out.at[me], local_sem.at[2])
        own_qkv = pltpu.make_async_copy(qkv_ref.at[me], weight_rows(dp, me), own_sem)
        own_x.start()
        own_qkv.start()

        def part(peer, origin):
            return send_to(
                qkv_ref.at[peer], weight_rows(dp, origin), part_send.at[peer], part_recv.at[origin], (dp, peer)
            )

        for step in range(1, seq):
            part(lax.rem(me + step, seq), me).start()

        def small(peer, origin):
            return send_to(
                packed_ref, packed_out.at[origin], small_send.at[peer], small_recv.at[origin], device(peer)
            )

        def small_start(step, carry):
            small(lax.rem(rank + step, devices), rank).start()
            return carry

        lax.fori_loop(1, devices, small_start, 0)

        goal = lax.div(rank, ndp)
        place = lax.rem(rank, ndp)

        def proj_first(slot):
            return send_to(proj_ref, proj_out.at[slot], proj_send, proj_recv.at[slot], (dp, goal))

        stays = goal == me
        own_proj = pltpu.make_async_copy(proj_ref, proj_out.at[place], local_sem.at[1])
        pl.when(stays)(own_proj.start)
        pl.when(jnp.logical_not(stays))(lambda: proj_first(place).start())

        def route(peer, origin):
            return send_to(
                routes_ref, routes_out.at[origin], routes_send.at[peer], routes_recv.at[origin], (dp, peer)
            )

        for step in range(1, seq):
            route(lax.rem(me + step, seq), me).start()
        packed_out[rank] = packed_ref[...]
        routes_out[me] = routes_ref[...]

        gathers = seq_gathers(x_ref, x_v, x_sems)
        for program in gathers:
            program.start()

        def ready(h):
            @pl.when(h == me)
            def _():
                own_qkv.wait()

            @pl.when(h != me)
            def _():
                part(h, h).wait_recv()

        spread = Gather(
            x_line,
            core_line,
            dp,
            dp_flat,
            seq,
            lambda h: weight_rows(dp, h),
            weight_rows,
            qkv_send,
            qkv_recv,
            ready,
        )
        x_steps = sorted((s for p in gathers for s in p.steps()), key=lambda s: s[0])
        for hops, step in x_steps:
            if hops <= 1:
                step()
        spread.start()
        root = lax.div(me * ndp, seq)
        root_x, root_core = lax.div(root, 2), lax.rem(root, 2)
        on_line = core_line.place == root_core
        ways = [
            (on_line & (x_line.place >= root_x) & x_line.has(1), x_line.device(1), 0),
            (on_line & (x_line.place <= root_x) & x_line.has(-1), x_line.device(-1), 1),
            (on_line & core_line.has(1), core_line.device(1), 2),
            (on_line & core_line.has(-1), core_line.device(-1), 3),
        ]

        def onward(slot, way, target):
            return send_to(
                proj_out.at[slot], proj_out.at[slot], proj_fwd.at[slot, way], proj_recv.at[slot], target
            )

        rest = sorted(
            [s for s in x_steps if s[0] > 1] + [(hops + 0.75, step) for hops, step in spread.steps()],
            key=lambda s: s[0],
        )
        for _, step in rest:
            step()

        c_gathers = seq_gathers(c_ref, c_out, c_sems)
        own_c.start()
        for program in c_gathers:
            program.start()
        c_steps = sorted((s for p in c_gathers for s in p.steps()), key=lambda s: s[0])

        def move_cotangent(hops):
            while c_steps and c_steps[0][0] <= hops:
                c_steps.pop(0)[1]()

        for slot in range(ndp):
            held = (dp == root) & (lax.rem(me * ndp + slot, seq) == me)

            @pl.when(held)
            def _():
                own_proj.wait()

            @pl.when(jnp.logical_not(held))
            def _():
                onward(slot, 0, x_line.device(1)).wait_recv()

            for cond, target, way in ways:
                pl.when(cond)(lambda: onward(slot, way, target).start())

        def small_end(step, carry):
            source = lax.rem(rank + devices - step, devices)
            small(source, source).wait_recv()
            return carry

        lax.fori_loop(1, devices, small_end, 0)
        for block in range(width // 128):
            total = packed_out[block * per_block, n_router : n_router + 16, :].astype(F32)
            for i in range(1, per_block):
                total = total + packed_out[block * per_block + i, n_router : n_router + 16, :].astype(F32)
            gains_v[:, block * 128 : (block + 1) * 128] = total[0:8]
        own_x.wait()

        def normed_copy(src):
            return pltpu.make_async_copy(normed_v.at[src], normed_out.at[src], normed_sem.at[src])

        def project(src, carry):
            def strip(i, inner):
                at = pl.ds(pl.multiple_of(i * 16, 16), 16)
                values = x_v[src, at, :].astype(F32)
                factor = lax.rsqrt(jnp.mean(values * values, axis=-1, keepdims=True) + NORM_EPS)
                normed_v[src, at, :] = (values * factor * gains_v[0:1, :]).astype(BF)
                return inner

            lax.fori_loop(0, rows // 16, strip, 0)
            normed_copy(src).start()
            at = pl.ds(pl.multiple_of(src * rows, rows), rows)
            for j in range(2):
                raw = jnp.dot(normed_v[src], w_v[j], preferred_element_type=F32)
                raw_out[j, at, :] = raw
                sums_v[pl.ds(j * seq + src, 1), :] = as_row(jnp.sum(raw * raw, axis=1, keepdims=True))
            values = jnp.dot(normed_v[src], w_v[2], preferred_element_type=F32).astype(BF)
            for n in range(num_seqs):
                v_out[n, pl.ds(pl.multiple_of(src * local_len, local_len), local_len), :] = values[
                    n * local_len : (n + 1) * local_len
                ]
            return carry

        lax.fori_loop(0, seq // 2, project, 0)
        move_cotangent(1)
        lax.fori_loop(seq // 2, seq, project, 0)

        def square_sums(peer, origin):
            return send_to(sums_v, sums_got.at[origin], sums_send.at[peer], sums_recv.at[origin], (dp, peer))

        for step in range(1, seq):
            square_sums(lax.rem(me + step, seq), me).start()
        move_cotangent(2)
        total = sums_v[...]
        for step in range(1, seq):
            source = lax.rem(me + seq - step, seq)
            square_sums(source, source).wait_recv()
        sums_got[me] = sums_v[...]
        total = jnp.sum(sums_got[...], axis=0)
        for step in range(1, seq):
            square_sums(lax.rem(me + step, seq), me).wait_send()
        total_out[...] = total
        sums_v[...] = lax.rsqrt(total / width + NORM_EPS)

        def turn(src, carry):
            spots = pl.ds(pl.multiple_of(src * local_len, local_len), local_len)
            cosine, sine = cos_ref[spots, :], sin_ref[spots, :]
            for j, out in ((0, q_out), (1, k_out)):
                factor = as_columns(sums_v[pl.ds(j * seq + src, 1), :])
                for h in range(heads_here):
                    at = slice(h * HEAD_DIM, (h + 1) * HEAD_DIM)
                    gain = gains_v[
                        1 + j : 2 + j, pl.ds(pl.multiple_of(me * cols + h * HEAD_DIM, HEAD_DIM), HEAD_DIM)
                    ]
                    for n in range(num_seqs):
                        low, high = n * local_len, (n + 1) * local_len
                        values = raw_out[
                            j, pl.ds(pl.multiple_of(src * rows + low, local_len), local_len), at
                        ]
                        values = values * factor[low:high] * gain
                        out[n, spots, at] = turn_heads(values, cosine, sine).astype(BF)
            return carry

        lax.fori_loop(0, seq, turn, 0)
        move_cotangent(2.5)

        def attend(index, carry):
            n = lax.div(index, heads_here)
            head = pl.ds(pl.multiple_of(lax.rem(index, heads_here) * HEAD_DIM, HEAD_DIM), HEAD_DIM)
            for block in range(length // tile):
                low = block * tile
                limit = min(length, low + 2 * tile)
                scores = dot_rows(q_out[n, low : low + tile, head], k_out[n, 0:limit, head]) * HEAD_DIM**-0.5
                allowed = row_ref[n, 0:1, 0:limit] <= col_ref[n, low : low + tile, :]
                scores = jnp.where(allowed, scores, MASKED_SCORE)
                exps = jnp.exp(scores - jnp.max(scores, axis=-1, keepdims=True))
                probs = (exps / jnp.sum(exps, axis=-1, keepdims=True)).astype(BF)
                result = jnp.dot(probs, v_out[n, 0:limit, head], preferred_element_type=F32).astype(BF)
                for i in range(tile // local_len):
                    src = low // local_len + i
                    o_out[src, pl.ds(pl.multiple_of(n * local_len, local_len), local_len), head] = result[
                        i * local_len : (i + 1) * local_len
                    ]
            return carry

        lax.fori_loop(0, heads_here, attend, 0)
        move_cotangent(3)
        lax.fori_loop(heads_here, num_seqs * heads_here, attend, 0)
        move_cotangent(1000)

        for program in (*gathers, spread, *c_gathers):
            program.finish()
        for slot in range(ndp):
            for cond, target, way in ways:
                pl.when(cond)(lambda: onward(slot, way, target).wait_send())
        pl.when(jnp.logical_not(stays))(lambda: proj_first(place).wait_send())
        for step in range(1, seq):
            part(lax.rem(me + step, seq), me).wait_send()
            route(lax.rem(me + step, seq), me).wait_send()
            source = lax.rem(me + seq - step, seq)
            route(source, source).wait_recv()

        def small_sent(step, carry):
            small(lax.rem(rank + step, devices), rank).wait_send()
            return carry

        lax.fori_loop(1, devices, small_sent, 0)
        for src in range(seq):
            normed_copy(src).wait()
        own_c.wait()

    dma = pltpu.SemaphoreType.DMA
    hbm, vmem = pl.BlockSpec(memory_space=pl.ANY), pl.BlockSpec(memory_space=pltpu.VMEM)
    shaped = jax.ShapeDtypeStruct
    outs = [
        (shaped((seq, rows, width), BF), hbm),
        (shaped((seq, rows, width), BF), hbm),
        (shaped((3, width, cols), BF), vmem),
        (shaped((ndp,) + proj_rows.shape, BF), hbm),
        (shaped((devices,) + packed.shape, BF), vmem),
        (shaped((seq,) + routes.shape, jnp.int32), vmem),
        (shaped((2, seq * rows, cols), F32), vmem),
        (shaped((num_seqs, length, cols), BF), vmem),
        (shaped((num_seqs, length, cols), BF), vmem),
        (shaped((num_seqs, length, cols), BF), vmem),
        (shaped((seq, rows, cols), BF), vmem),
        (shaped((2 * seq, rows), F32), vmem),
    ]
    return pl.pallas_call(
        kernel,
        out_shape=[shape for shape, _ in outs],
        in_specs=[hbm] * 4 + [vmem] * 6,
        out_specs=[spec for _, spec in outs],
        scratch_shapes=[
            pltpu.VMEM((seq, rows, width), BF),
            pltpu.VMEM((seq, rows, width), BF),
            pltpu.VMEM((8, width), F32),
            pltpu.VMEM((2 * seq, rows), F32),
            pltpu.VMEM((seq, 2 * seq, rows), F32),
            dma((3,)),
            dma((seq,)),
            dma((seq,)),
            dma((seq,)),
            dma,
            dma((ndp, seq, 4)),
            dma((ndp, seq)),
            dma,
            dma((ndp,)),
            dma((ndp, 4)),
            dma((devices,)),
            dma((devices,)),
            dma((seq,)),
            dma((seq,)),
            dma((seq,)),
            dma((seq,)),
        ]
        + gather_sems(seq, rows)
        + gather_sems(seq, rows),
        compiler_params=pltpu.CompilerParams(
            collective_id=collective_id, has_side_effects=True, vmem_limit_bytes=VMEM_MOST
        ),
        name="attend_first",
        cost_estimate=cost_of(210),
    )(
        tokens,
        cotangent,
        qkv_rows,
        proj_rows,
        packed,
        routes,
        *tables,
        segments[:, :, None],
        segments[:, None, :],
    )


def small_exchange(arrays, axes, collective_id):
    sizes = [lax.axis_size(axis) for axis in axes]
    peers = math.prod(sizes)
    seq = lax.axis_size("seq")
    count = len(arrays)

    def kernel(*refs):
        ins, outs, (send_sem, recv_sem) = refs[:count], refs[count : 2 * count], refs[2 * count :]
        dp, sq = lax.axis_index("dp"), lax.axis_index("seq")
        me = sq if len(axes) == 1 else dp * seq + sq

        def device(peer):
            return (dp, peer) if len(axes) == 1 else (lax.div(peer, seq), lax.rem(peer, seq))

        barrier = pltpu.get_barrier_semaphore()
        for step in range(1, peers):
            pl.semaphore_signal(
                barrier, 1, device_id=device(lax.rem(me + step, peers)), device_id_type=MESH
            )
        pl.semaphore_wait(barrier, peers - 1)

        def copy(i, peer, src_slot):
            src = ins[i].at[0] if arrays[i].shape[0] == 1 else ins[i].at[peer]
            return pltpu.make_async_remote_copy(
                src_ref=src,
                dst_ref=outs[i].at[src_slot],
                send_sem=send_sem.at[i, peer],
                recv_sem=recv_sem.at[i, src_slot],
                device_id=device(peer),
                device_id_type=MESH,
            )

        for step in range(1, peers):
            for i in range(count):
                copy(i, lax.rem(me + step, peers), me).start()
        for i in range(count):
            outs[i][me] = ins[i][0] if arrays[i].shape[0] == 1 else ins[i][me]
        for step in range(1, peers):
            for i in range(count):
                copy(i, lax.rem(me + step, peers), me).wait_send()
                source = lax.rem(me + peers - step, peers)
                copy(i, source, source).wait_recv()

    return pl.pallas_call(
        kernel,
        out_shape=[jax.ShapeDtypeStruct((peers,) + a.shape[1:], a.dtype) for a in arrays],
        in_specs=[pl.BlockSpec(memory_space=pltpu.VMEM)] * count,
        out_specs=[pl.BlockSpec(memory_space=pltpu.VMEM)] * count,
        scratch_shapes=[
            pltpu.SemaphoreType.DMA((count, peers)),
            pltpu.SemaphoreType.DMA((count, peers)),
        ],
        compiler_params=pltpu.CompilerParams(collective_id=collective_id, has_side_effects=True),
        name="small_exchange",
        cost_estimate=cost_of(8),
    )(*arrays)


def attend_back(dz, proj_weight, o_head, query, key, value, raw, squares, gains, tables, segments, collective_id):
    seq = lax.axis_size("seq")
    rows, width = dz.shape
    num_seqs, length, cols = query.shape
    local_len = length // seq
    heads_here = cols // HEAD_DIM
    tile = 256
    scale = HEAD_DIM**-0.5

    def kernel(*refs):
        (dz_ref, w_ref, o_ref, q_ref, k_ref, v_ref, raw_ref, squares_ref, gains_ref) = refs[:9]
        (cos_ref, sin_ref, col_ref, row_ref) = refs[9:13]
        d_out, proj_out, gain_out = refs[13:16]
        (dz_v, do_v, turned, dk_acc, dv_acc, proj_acc, factor_v, inner_v, inner_got) = refs[16:25]
        own_sem, inner_send, inner_recv = refs[25:28]
        sems = refs[28:]
        dp = lax.axis_index("dp")
        along, across, me, _ = seq_lines()
        barrier = pltpu.get_barrier_semaphore()
        for step in range(1, seq):
            pl.semaphore_signal(
                barrier, 1, device_id=(dp, lax.rem(me + step, seq)), device_id_type=MESH
            )
        pl.semaphore_wait(barrier, seq - 1)
        own = pltpu.make_async_copy(dz_ref, dz_v.at[me], own_sem)
        own.start()
        programs = seq_gathers(dz_ref, dz_v, sems)
        for program in programs:
            program.start()
        factor_v[...] = lax.rsqrt(squares_ref[...] / width + NORM_EPS)
        proj_acc[...] = jnp.zeros_like(proj_acc)
        own.wait()
        run_steps(*programs)

        def project(src, carry):
            back = dot_rows(dz_v[src], w_ref[...]).astype(BF)
            for n in range(num_seqs):
                do_v[n, pl.ds(pl.multiple_of(src * local_len, local_len), local_len), :] = back[
                    n * local_len : (n + 1) * local_len
                ]
            proj_acc[...] += lax.dot_general(
                o_ref[src], dz_v[src], (((0,), (0,)), ((), ())), preferred_element_type=F32
            )
            return carry

        lax.fori_loop(0, seq, project, 0)
        proj_out[...] = proj_acc[...].astype(BF)

        def unturn(values, at):
            return values * cos_ref[at, :] - pltpu.roll(values, HEAD_DIM // 2, 1) * sin_ref[at, :]

        def attend(index, carry):
            n = lax.div(index, heads_here)
            head = pl.ds(pl.multiple_of(lax.rem(index, heads_here) * HEAD_DIM, HEAD_DIM), HEAD_DIM)
            dk_acc[...] = jnp.zeros_like(dk_acc)
            dv_acc[...] = jnp.zeros_like(dv_acc)
            for block in range(length // tile):
                low = block * tile
                limit = min(length, low + 2 * tile)
                spots = slice(low, low + tile)
                queries, keys, grads = q_ref[n, spots, head], k_ref[n, 0:limit, head], do_v[n, spots, head]
                scores = dot_rows(queries, keys) * scale
                allowed = row_ref[n, 0:1, 0:limit] <= col_ref[n, spots, :]
                scores = jnp.where(allowed, scores, MASKED_SCORE)
                exps = jnp.exp(scores - jnp.max(scores, axis=-1, keepdims=True))
                probs = exps / jnp.sum(exps, axis=-1, keepdims=True)
                grad_probs = dot_rows(grads, v_ref[n, 0:limit, head])
                inner = jnp.sum(probs * grad_probs, axis=-1, keepdims=True)
                grad_scores = (probs * (grad_probs - inner)).astype(BF)
                dq = jnp.dot(grad_scores, keys, preferred_element_type=F32) * scale
                turned[0, n, spots, head] = unturn(dq, spots)
                dk_acc[0:limit, :] += lax.dot_general(
                    grad_scores, queries, (((0,), (0,)), ((), ())), preferred_element_type=F32
                )
                dv_acc[0:limit, :] += lax.dot_general(
                    probs.astype(BF), grads, (((0,), (0,)), ((), ())), preferred_element_type=F32
                )
            for block in range(length // tile):
                spots = slice(block * tile, (block + 1) * tile)
                turned[1, n, spots, head] = unturn(dk_acc[spots, :] * scale, spots)
            for src in range(seq):
                d_out[2, src, pl.ds(pl.multiple_of(n * local_len, local_len), local_len), head] = dv_acc[
                    src * local_len : (src + 1) * local_len, :
                ].astype(BF)
            return carry

        lax.fori_loop(0, num_seqs * heads_here, attend, 0)

        def pieces(j, src):
            spots = pl.ds(pl.multiple_of(src * local_len, local_len), local_len)
            grads = jnp.concatenate([turned[j, n, spots, :] for n in range(num_seqs)], axis=0)
            return grads, raw_ref[j, pl.ds(pl.multiple_of(src * rows, rows), rows), :]

        def wide(row):
            return jnp.concatenate([as_columns(row)] * heads_here, axis=1)

        def measure(src, carry):
            sums = []
            for j in range(2):
                grads, values = pieces(j, src)
                scaled = grads * gains_ref[j : j + 1, :]
                inner_v[pl.ds(j * seq + src, 1), :] = as_row(
                    jnp.sum(scaled * values, axis=1, keepdims=True)
                )
                factor = wide(factor_v[pl.ds(j * seq + src, 1), :])
                sums.append(carry[j] + jnp.sum(grads * values * factor, axis=0, keepdims=True))
            return tuple(sums)

        zero = jnp.zeros((1, cols), F32)
        gain_q, gain_k = lax.fori_loop(0, seq, measure, (zero, zero))
        gain_out[0:1, :] = gain_q
        gain_out[1:2, :] = gain_k
        gain_out[2:8, :] = jnp.zeros((6, cols), F32)

        def inner_copy(peer, origin):
            return send_to(
                inner_v, inner_got.at[origin], inner_send.at[peer], inner_recv.at[origin], (dp, peer)
            )

        for step in range(1, seq):
            inner_copy(lax.rem(me + step, seq), me).start()
        inner_got[me] = inner_v[...]
        for program in programs:
            program.finish()
        for step in range(1, seq):
            source = lax.rem(me + seq - step, seq)
            inner_copy(source, source).wait_recv()
            inner_copy(lax.rem(me + step, seq), me).wait_send()
        inner_v[...] = jnp.sum(inner_got[...], axis=0) / width

        def normalize(src, carry):
            for j in range(2):
                grads, values = pieces(j, src)
                factor = wide(factor_v[pl.ds(j * seq + src, 1), :])
                inner = wide(inner_v[pl.ds(j * seq + src, 1), :])
                scaled = grads * gains_ref[j : j + 1, :]
                d_out[j, src] = (factor * (scaled - values * factor * factor * inner)).astype(BF)
            return carry

        lax.fori_loop(0, seq, normalize, 0)

    dma = pltpu.SemaphoreType.DMA
    hbm, vmem = pl.BlockSpec(memory_space=pl.ANY), pl.BlockSpec(memory_space=pltpu.VMEM)
    return pl.pallas_call(
        kernel,
        out_shape=[
            jax.ShapeDtypeStruct((3, seq, rows, cols), BF),
            jax.ShapeDtypeStruct((cols, width), BF),
            jax.ShapeDtypeStruct((8, cols), F32),
        ],
        in_specs=[hbm] + [vmem] * 12,
        out_specs=[vmem] * 3,
        scratch_shapes=[
            pltpu.VMEM((seq, rows, width), BF),
            pltpu.VMEM((num_seqs, length, cols), BF),
            pltpu.VMEM((2, num_seqs, length, cols), F32),
            pltpu.VMEM((length, HEAD_DIM), F32),
            pltpu.VMEM((length, HEAD_DIM), F32),
            pltpu.VMEM((cols, width), F32),
            pltpu.VMEM((2 * seq, rows), F32),
            pltpu.VMEM((2 * seq, rows), F32),
            pltpu.VMEM((seq, 2 * seq, rows), F32),
            dma,
            dma((seq,)),
            dma((seq,)),
        ]
        + gather_sems(seq, rows),
        compiler_params=pltpu.CompilerParams(
            collective_id=collective_id, has_side_effects=True, vmem_limit_bytes=VMEM_MOST
        ),
        name="attend_back",
        cost_estimate=cost_of(130),
    )(
        dz,
        proj_weight,
        o_head,
        query,
        key,
        value,
        raw,
        squares,
        gains,
        *tables,
        segments[:, :, None],
        segments[:, None, :],
    )


def last_transfers(terms, qkv_terms, proj_terms, packed, collective_id):
    seq, ndp = lax.axis_size("seq"), lax.axis_size("dp")
    devices = seq * ndp
    _, rows, width = terms.shape
    part_rows, cols = qkv_terms.shape[1] // seq, qkv_terms.shape[2]
    proj_rows = proj_terms.shape[1]
    n_scratch = len(reduce_scratch(seq, rows, width))
    n_reduce = 5

    def kernel(p_ref, qkv_ref, proj_ref, packed_ref, o_ref, qkv_out, proj_out, sum_out, acc, *scratch):
        seq_scratch, rest = scratch[: n_scratch - 1], scratch[n_scratch - 1 :]
        qkv_acc, qkv_sum, proj_acc, proj_sum, got = rest[:5]
        qkv_scratch, proj_scratch = rest[5 : 5 + n_reduce], rest[5 + n_reduce : 5 + 2 * n_reduce]
        (part_send, part_recv, move_send, move_recv, small_send, small_recv, own_sem) = rest[5 + 2 * n_reduce :]
        _, _, me, _ = seq_lines()
        x_line, core_line, dp, dp_flat = dp_lines()
        rank = dp * seq + me
        barrier = pltpu.get_barrier_semaphore()

        def device(peer):
            return (lax.div(peer, seq), lax.rem(peer, seq))

        def meet(step, carry):
            pl.semaphore_signal(
                barrier, 1, device_id=device(lax.rem(rank + step, devices)), device_id_type=MESH
            )
            return carry

        lax.fori_loop(1, devices, meet, 0)
        pl.semaphore_wait(barrier, devices - 1)

        programs = seq_reduces(p_ref, acc, o_ref, seq_scratch)

        def over_dp(refs, total, out, buffers):
            return Reduce(
                core_line,
                x_line,
                dp,
                lambda core, x: dp_flat(x, core),
                [(0, refs.shape[1])],
                refs,
                total,
                out,
                *buffers[0:2],
                buffers[2:5],
            )

        owners = [
            over_dp(qkv_ref, qkv_acc, qkv_sum, qkv_scratch),
            over_dp(proj_ref, proj_acc, proj_sum, proj_scratch),
        ]
        for owner in owners:
            for step in owner.outward():
                step()
        for step in woven(*[p.outward() for p in programs]):
            step()

        def small(peer, origin):
            return send_to(
                packed_ref.at[peer], got.at[origin], small_send.at[peer], small_recv.at[origin], device(peer)
            )

        def small_start(step, carry):
            small(lax.rem(rank + step, devices), rank).start()
            return carry

        lax.fori_loop(1, devices, small_start, 0)
        inner = [list(owner.inward()) for owner in owners]
        for steps in inner:
            for step in steps[:-1]:
                step()

        def part(peer, origin):
            return send_to(
                qkv_sum.at[pl.ds(pl.multiple_of(peer * part_rows, 16), part_rows)],
                qkv_out.at[origin],
                part_send.at[peer],
                part_recv.at[origin],
                (dp, peer),
            )

        own_part = pltpu.make_async_copy(
            qkv_sum.at[pl.ds(pl.multiple_of(me * part_rows, 16), part_rows)], qkv_out.at[me], own_sem.at[0]
        )
        goal = me * ndp + dp
        stays = goal == rank
        own_move = pltpu.make_async_copy(proj_sum, proj_out, own_sem.at[1])

        def move():
            return send_to(proj_sum, proj_out, move_send, move_recv, device(goal))

        steps = woven(*[p.inward() for p in programs])
        half = len(steps) // 2
        for step in steps[:half]:
            step()
        for owner_steps in inner:
            owner_steps[-1]()
        own_part.start()
        for step in range(1, seq):
            part(lax.rem(me + step, seq), me).start()
        pl.when(stays)(own_move.start)
        pl.when(jnp.logical_not(stays))(lambda: move().start())
        for step in steps[half:]:
            step()

        got[rank] = packed_ref[rank]

        def small_end(step, carry):
            small(lax.rem(rank + step, devices), rank).wait_send()
            source = lax.rem(rank + devices - step, devices)
            small(source, source).wait_recv()
            return carry

        lax.fori_loop(1, devices, small_end, 0)
        sum_out[...] = jnp.sum(got[...], axis=0)
        for program in (*programs, *owners):
            program.finish()
        for step in range(1, seq):
            part(lax.rem(me + step, seq), me).wait_send()
            source = lax.rem(me + seq - step, seq)
            part(source, source).wait_recv()
        own_part.wait()

        @pl.when(stays)
        def _():
            own_move.wait()

        @pl.when(jnp.logical_not(stays))
        def _():
            move().wait_send()
            move().wait_recv()

    dma = pltpu.SemaphoreType.DMA
    vmem = pl.BlockSpec(memory_space=pltpu.VMEM)

    def over_dp_scratch(array):
        return Reduce.scratch([(0, array.shape[1])], 2, ndp // 2, array.shape[2])

    return pl.pallas_call(
        kernel,
        out_shape=[
            jax.ShapeDtypeStruct((rows, width), F32),
            jax.ShapeDtypeStruct((seq, part_rows, cols), BF),
            jax.ShapeDtypeStruct((proj_rows, width), BF),
            jax.ShapeDtypeStruct(packed.shape[1:], F32),
        ],
        in_specs=[vmem] * 4,
        out_specs=[vmem] * 4,
        scratch_shapes=reduce_scratch(seq, rows, width)
        + [
            pltpu.VMEM(qkv_terms.shape, BF),
            pltpu.VMEM(qkv_terms.shape[1:], BF),
            pltpu.VMEM(proj_terms.shape, BF),
            pltpu.VMEM(proj_terms.shape[1:], BF),
            pltpu.VMEM(packed.shape, F32),
        ]
        + over_dp_scratch(qkv_terms)
        + over_dp_scratch(proj_terms)
        + [dma((seq,)), dma((seq,)), dma, dma, dma((devices,)), dma((devices,)), dma((2,))],
        compiler_params=pltpu.CompilerParams(
            collective_id=collective_id, has_side_effects=True, vmem_limit_bytes=VMEM_MOST
        ),
        name="last_transfers",
        cost_estimate=cost_of(100),
    )(terms, qkv_terms, proj_terms, packed)


def packed_rows(parts, sublanes):
    flat = jnp.concatenate(parts, axis=1)
    fill = -flat.shape[1] % (sublanes * 128)
    return jnp.pad(flat, ((0, 0), (0, fill))).reshape(flat.shape[0], -1, 128)


def rms_factor(values):
    return lax.rsqrt(jnp.mean(values * values, axis=-1, keepdims=True) + NORM_EPS)


def norm_back(values, factor, gain_row, incoming):
    scaled = incoming * gain_row
    gain_part = jnp.sum(incoming * values * factor, axis=0)
    inner = jnp.mean(scaled * values, axis=-1, keepdims=True)
    return (factor * (scaled - values * factor * factor * inner), gain_part)


def swiglu(gate_vals, up_vals):
    return jax.nn.silu(gate_vals) * up_vals


def local(
    tokens,
    segments,
    routes,
    cotangent,
    attn_weight,
    router_weight,
    norm_gains,
    expert_in,
    expert_out,
):
    num_seqs, local_len, width = tokens.shape
    seq_length = segments.shape[1]
    seq, ndp = lax.axis_size("seq"), lax.axis_size("dp")
    me = lax.axis_index("seq")
    devices = seq * ndp
    cols = HEADS // seq * HEAD_DIM
    tok = num_seqs * local_len
    group = tok * seq
    own_rows = attn_weight.shape[0]
    experts_all = router_weight.shape[1]
    experts = experts_all // seq
    top = routes.shape[-1]
    capacity = (9 * tok * top + 8 * experts_all - 1) // (8 * experts_all)

    n_router, n_gain = own_rows * experts_all, 4 * own_rows
    token_rows, cot_low = tokens.reshape(tok, width), cotangent.reshape(tok, width)
    (router_rows,) = (packed_rows([router_weight.reshape(1, -1)], 16)[0],)
    rank = lax.axis_index("dp") * seq + me
    gain_rows_own = lax.dynamic_update_slice(
        jnp.zeros((16, 128), BF), norm_gains, (0, lax.rem(rank, 128 // own_rows) * own_rows)
    )
    tables = rotary_tables(seq_length)
    normed_all, cot_all, qkv_weight, proj_got, small_all, routes_all, raw, query_head, key_head, value_head, o_head, sums = (
        attend_first(
            token_rows,
            cot_low,
            attn_weight[:, :3].reshape(own_rows, 3, seq, cols).transpose(2, 1, 0, 3),
            attn_weight[:, 3],
            jnp.concatenate([router_rows, gain_rows_own], axis=0),
            routes.reshape(-1, 128),
            tables,
            segments,
            router_rows.shape[0],
            1,
        )
    )
    in_full = lax.all_gather(expert_in, "dp", axis=1, tiled=True)
    out_full = lax.all_gather(expert_out, "dp", axis=2, tiled=True)
    router_full = (
        small_all[:, : router_rows.shape[0]].reshape(devices, -1)[:, :n_router].reshape(width, experts_all)
    )
    gain_rows = (
        jnp.sum(
            small_all[:, router_rows.shape[0] : router_rows.shape[0] + 4]
            .reshape(width // 128, 128 // own_rows, 4, 128)
            .astype(F32),
            axis=1,
        )
        .transpose(1, 0, 2)
        .reshape(4, width)
    )
    routes_all = routes_all.reshape(seq, tok, top)
    normed_all = normed_all.reshape(group, width)
    proj_weight = proj_got.reshape(cols, width)
    resid_in = token_rows.astype(F32)
    factor_attn = rms_factor(resid_in)
    z_terms = jnp.dot(o_head.reshape(group, cols), proj_weight, preferred_element_type=F32).astype(BF)
    z = seq_reduce(z_terms.reshape(seq, tok, width), 5)

    middle = resid_in + z
    factor_ffn = rms_factor(middle)
    ffn_low = (middle * factor_ffn * gain_rows[3]).astype(BF)
    ffn_all = seq_gather(ffn_low, 6)

    logits_all = jnp.einsum("std,de->ste", ffn_all, router_full, preferred_element_type=F32)
    probs_all = jax.nn.softmax(logits_all, axis=-1)
    here = me * experts + jnp.arange(experts, dtype=jnp.int32)
    hits = jnp.any(routes_all[:, :, :, None] == here, axis=2)
    token_ids = jnp.arange(tok, dtype=jnp.int32)
    earlier = (token_ids[:, None] > token_ids[None, :]).astype(BF)
    slot = jnp.einsum("tu,sue->ste", earlier, hits.astype(BF), preferred_element_type=F32)
    slot = jnp.where(hits, slot, float(tok + 1)).astype(jnp.int32)
    place = slot.transpose(2, 0, 1)[:, :, None, :] == jnp.arange(capacity, dtype=jnp.int32)[
        None, None, :, None
    ]
    place_low = place.astype(BF)
    probs_here = lax.dynamic_slice_in_dim(probs_all, me * experts, experts, axis=2).transpose(2, 0, 1)
    place_gate = jnp.where(place, probs_here[:, :, None, :], 0.0)
    slot_gate = jnp.sum(place_gate, axis=-1)
    slots = seq * capacity
    rows = (
        jnp.einsum("esjt,std->esjd", place_low, ffn_all, preferred_element_type=F32)
        .astype(BF)
        .reshape(experts, slots, width)
    )
    cot_rows = jnp.einsum("esjt,std->esjd", place_low, cot_all, preferred_element_type=F32).reshape(
        experts, slots, width
    )

    gate_up = jnp.einsum("erd,edjf->erjf", rows, in_full, preferred_element_type=F32)
    hidden_f, swiglu_pull = jax.vjp(swiglu, gate_up[:, :, 0], gate_up[:, :, 1])
    hidden = hidden_f.astype(BF)
    expert_res = jnp.einsum("erf,efd->erd", hidden, out_full, preferred_element_type=F32).astype(BF)
    mixed_terms = jnp.einsum(
        "esjt,esjd->std",
        place_gate.astype(BF),
        expert_res.reshape(experts, seq, capacity, width),
        preferred_element_type=F32,
    ).astype(BF)
    mixed = lax.psum_scatter(mixed_terms, "seq", scatter_dimension=0, tiled=False).astype(F32)
    block_out = (middle + mixed).astype(BF).reshape(num_seqs, local_len, width)

    slot_dgate = jnp.sum(cot_rows * expert_res.astype(F32), axis=-1).reshape(experts, seq, capacity)
    grad_prob_here = jnp.sum(jnp.where(place, slot_dgate[..., None], 0.0), axis=2)
    grad_res = (cot_rows * slot_gate.reshape(experts, slots, 1)).astype(BF)
    grad_hidden = jnp.einsum("erd,efd->erf", grad_res, out_full, preferred_element_type=F32)
    grad_gatev, grad_upv = swiglu_pull(grad_hidden)
    grad_gu = jnp.stack([grad_gatev, grad_upv], axis=2).astype(BF)
    grad_rows = jnp.einsum("erjf,edjf->erd", grad_gu, in_full, preferred_element_type=F32).astype(BF)
    out_term = jnp.einsum("erf,erd->efd", hidden, grad_res, preferred_element_type=F32).astype(BF)
    in_term = jnp.einsum("erd,erjf->edjf", rows, grad_gu, preferred_element_type=F32).astype(BF)
    out_term, in_term, grad_rows = lax.optimization_barrier((out_term, in_term, grad_rows))
    expert_out_grad = lax.psum_scatter(out_term, "dp", scatter_dimension=2, tiled=True).astype(F32)
    expert_in_grad = lax.psum_scatter(in_term, "dp", scatter_dimension=1, tiled=True).astype(F32)
    dffn_terms = jnp.einsum(
        "esjt,esjd->std",
        place_low,
        grad_rows.reshape(experts, seq, capacity, width),
        preferred_element_type=F32,
    ).astype(BF)
    grad_ffn = seq_reduce(dffn_terms, 9)
    (grad_prob,) = small_exchange(
        [grad_prob_here.transpose(1, 0, 2).reshape(seq, -1, 128)], ("seq",), 10
    )
    grad_prob = grad_prob.reshape(experts_all, tok).T

    route_probs = jax.nn.softmax(
        jnp.dot(ffn_low, router_full, preferred_element_type=F32), axis=-1
    )
    grad_logits = (
        route_probs * (grad_prob - jnp.sum(route_probs * grad_prob, axis=-1, keepdims=True))
    ).astype(BF)
    router_term = jnp.einsum("td,te->de", ffn_low, grad_logits, preferred_element_type=F32)
    grad_ffn = grad_ffn + jnp.einsum(
        "te,de->td", grad_logits, router_full, preferred_element_type=F32
    )
    grad_middle, gain_ffn = norm_back(middle, factor_ffn, gain_rows[3], grad_ffn)
    grad_middle = grad_middle + cot_low.astype(F32)

    head_gains = jnp.pad(lax.dynamic_slice(gain_rows, (1, me * cols), (2, cols)), ((0, 6), (0, 0)))
    grad_stack, proj_term, gain_heads = attend_back(
        grad_middle.astype(BF),
        proj_weight,
        o_head,
        query_head,
        key_head,
        value_head,
        raw,
        sums,
        head_gains,
        tables,
        segments,
        11,
    )
    grad_stack = grad_stack.reshape(3, group, cols)
    dn_terms = jnp.einsum("jte,jde->td", grad_stack, qkv_weight, preferred_element_type=F32).astype(BF)
    qkv_term = jnp.einsum("td,jte->jde", normed_all, grad_stack, preferred_element_type=F32)
    gain_attn = jnp.sum(qkv_term * qkv_weight.astype(F32), axis=(0, 2)) / gain_rows[0]

    gain_heads = lax.dynamic_update_slice_in_dim(jnp.zeros((2, width), F32), gain_heads[:2], me * cols, axis=1)
    gain_term = jnp.concatenate([gain_attn[None], gain_heads, gain_ffn[None]], axis=0)
    gain_send = gain_term.reshape(4, devices, own_rows).transpose(1, 0, 2)
    grad_normed, qkv_out, proj_grad, total = last_transfers(
        dn_terms.reshape(seq, tok, width),
        qkv_term.astype(BF)
        .reshape(3, ndp, seq, own_rows, cols)
        .transpose(1, 2, 0, 3, 4)
        .reshape(ndp, seq * 3 * own_rows, cols),
        proj_term.reshape(ndp, own_rows, width),
        packed_rows([router_term.reshape(devices, -1), gain_send.reshape(devices, -1)], 8),
        14,
    )
    grad_resid, _ = norm_back(resid_in, factor_attn, gain_rows[0], grad_normed)
    input_grad = (grad_resid + grad_middle).reshape(num_seqs, local_len, width)
    qkv_grad = qkv_out.reshape(seq, 3, own_rows, cols).transpose(2, 1, 0, 3).reshape(own_rows, 3, width)
    attn_grad = jnp.concatenate([qkv_grad, proj_grad[:, None, :]], axis=1).astype(F32)
    total = total.reshape(-1)
    router_grad = total[:n_router].reshape(own_rows, experts_all)
    gain_grad = total[n_router : n_router + n_gain].reshape(4, own_rows)
    return (
        block_out,
        input_grad,
        attn_grad,
        router_grad,
        gain_grad,
        expert_in_grad,
        expert_out_grad,
    )


def solution(mesh):
    in_specs = (
        P("dp", "seq", None),
        P("dp", None),
        P("dp", "seq", None),
        P("dp", "seq", None),
        P(("dp", "seq"), None, None),
        P(("dp", "seq"), None),
        P(None, ("dp", "seq")),
        P("seq", "dp", None, None),
        P("seq", None, "dp"),
    )
    out_specs = (
        P("dp", "seq", None),
        P("dp", "seq", None),
        P(("dp", "seq"), None, None),
        P(("dp", "seq"), None),
        P(None, ("dp", "seq")),
        P("seq", "dp", None, None),
        P("seq", None, "dp"),
    )
    return jax.shard_map(local, mesh=mesh, in_specs=in_specs, out_specs=out_specs, check_vma=False)
```

```python
import math

import jax
import jax.numpy as jnp
from jax import lax
from jax.experimental import pallas as pl
from jax.experimental.pallas import tpu as pltpu
from jax.sharding import PartitionSpec as P

HEADS = 16
HEAD_DIM = 128
NORM_EPS = 1e-05
ROPE_BASE = 10000.0
MASKED_SCORE = -1e30
BF = jnp.bfloat16
F32 = jnp.float32
MESH = pl.DeviceIdType.MESH
VMEM_MOST = 60 << 20


class Line:
    def __init__(self, size, place, device):
        self.size, self.place, self.device = size, place, device

    def has(self, turn):
        return self.place < self.size - 1 if turn > 0 else self.place > 0

    def inside(self, place):
        return (place >= 0) & (place < self.size)


def grid_of(seq_size):
    lines = 4 if seq_size % 4 == 0 else 1
    return lines, seq_size // lines


def seq_lines():
    dp, me = lax.axis_index("dp"), lax.axis_index("seq")
    nz, ny = grid_of(lax.axis_size("seq"))
    along = Line(nz, lax.div(me, ny), lambda turn: (dp, me + turn * ny))
    across = Line(ny, lax.rem(me, ny), lambda turn: (dp, me + turn))
    return along, across, me, lambda z, y: z * ny + y


def dp_lines():
    dp, me = lax.axis_index("dp"), lax.axis_index("seq")
    along = Line(lax.axis_size("dp") // 2, lax.div(dp, 2), lambda turn: (dp + 2 * turn, me))
    across = Line(2, lax.rem(dp, 2), lambda turn: (dp + turn, me))
    return along, across, dp, lambda x, core: 2 * x + core


def cost_of(microseconds):
    return pl.CostEstimate(flops=0, bytes_accessed=microseconds * 3_600_000, transcendentals=0)


def send_to(src, dst, send_sem, recv_sem, device):
    return pltpu.make_async_remote_copy(
        src_ref=src,
        dst_ref=dst,
        send_sem=send_sem,
        recv_sem=recv_sem,
        device_id=device,
        device_id_type=MESH,
    )


def greet(targets):
    barrier = pltpu.get_barrier_semaphore()
    count = 0
    for cond, device in targets:

        @pl.when(cond)
        def _(device=device):
            pl.semaphore_signal(barrier, 1, device_id=device, device_id_type=MESH)

        count = count + cond.astype(jnp.int32)
    pl.semaphore_wait(barrier, count)


def greet_lines(*lines):
    greet([(line.has(turn), line.device(turn)) for line in lines for turn in (1, -1)])


def cuts_of(rows, ny):
    unit = rows // 16
    late = max(1, unit * 3 // 16) if ny == 2 else unit // 2
    early = unit - late
    half = (early + 1) // 2
    firsts = [(0, half * 16)] + ([(half * 16, (early - half) * 16)] if early > half else [])
    return firsts, [(early * 16, late * 16)]


class Gather:
    def __init__(self, first, second, me, flat, pieces, own, slot, send_sem, recv_sem, ready=None):
        self.first, self.second, self.me, self.flat = first, second, me, flat
        self.pieces, self.own, self.slot = pieces, own, slot
        self.send_sem, self.recv_sem, self.ready = send_sem, recv_sem, ready
        self.sent = []

    def _copy(self, src, origin, h, line, turn):
        way = (0 if line is self.first else 2) + (turn > 0)
        return send_to(
            src,
            self.slot(origin, h),
            self.send_sem.at[origin, h, way],
            self.recv_sem.at[origin, h],
            line.device(turn),
        )

    def _send(self, src, origin, h, line, turn, cond):
        ok = cond & line.has(turn)
        pl.when(ok)(lambda: self._copy(src, origin, h, line, turn).start())
        self.sent.append((ok, src, origin, h, line, turn))

    def start(self):
        for h in range(self.pieces):
            if self.ready is not None:
                self.ready(h)
            for line in (self.first, self.second):
                for turn in (1, -1):
                    self._send(self.own(h), self.me, h, line, turn, self.me >= 0)

    def _arrive(self, place, side, h, sends):
        first, second = self.first, self.second
        cond = first.inside(place) & second.inside(side)
        origin = lax.select(cond, self.flat(place, side), self.me)

        @pl.when(cond)
        def _():
            self._copy(self.slot(origin, h), origin, h, first, 1).wait_recv()

        for line, turn in sends:
            self._send(self.slot(origin, h), origin, h, line, turn, cond)

    def steps(self):
        first, second = self.first, self.second
        listed = []
        for far in range(1, first.size):
            for h in range(self.pieces):
                for sign in (1, -1):
                    listed.append(
                        (
                            far,
                            lambda far=far, h=h, sign=sign: self._arrive(
                                first.place - sign * far,
                                second.place,
                                h,
                                [(first, sign), (second, 1), (second, -1)],
                            ),
                        )
                    )
        for step in range(1, second.size):
            for far in range(first.size):
                for h in range(self.pieces):
                    for sign in (1, -1) if far else (1,):
                        for turn in (1, -1):
                            listed.append(
                                (
                                    far + step + 0.5,
                                    lambda far=far, step=step, h=h, sign=sign, turn=turn: self._arrive(
                                        first.place - sign * far,
                                        second.place - turn * step,
                                        h,
                                        [(second, turn)] if step < second.size - 1 else [],
                                    ),
                                )
                            )
        return listed

    def finish(self):
        for ok, src, origin, h, line, turn in self.sent:
            pl.when(ok)(lambda: self._copy(src, origin, h, line, turn).wait_send())


def run_steps(*programs):
    for _, step in sorted((s for p in programs for s in p.steps()), key=lambda s: s[0]):
        step()


def seq_gathers(block_ref, out_ref, sems):
    along, across, me, flat = seq_lines()
    early, late = cuts_of(block_ref.shape[0], across.size)
    made = []
    for cuts, first, second, index, (send_sem, recv_sem) in (
        (early, along, across, flat, sems[0:2]),
        (late, across, along, lambda y, z: flat(z, y), sems[2:4]),
    ):
        made.append(
            Gather(
                first,
                second,
                me,
                index,
                len(cuts),
                lambda h, cuts=cuts: block_ref.at[pl.ds(*cuts[h])],
                lambda origin, h, cuts=cuts: out_ref.at[origin, pl.ds(*cuts[h])],
                send_sem,
                recv_sem,
            )
        )
    return made


def gather_sems(seq, rows):
    early, late = cuts_of(rows, grid_of(seq)[1])
    return [
        pltpu.SemaphoreType.DMA((seq, len(early), 4)),
        pltpu.SemaphoreType.DMA((seq, len(early))),
        pltpu.SemaphoreType.DMA((seq, len(late), 4)),
        pltpu.SemaphoreType.DMA((seq, len(late))),
    ]


def seq_gather(block, collective_id):
    rows, width = block.shape
    seq = lax.axis_size("seq")

    def kernel(x_ref, o_ref, local_sem, *sems):
        along, across, me, _ = seq_lines()
        greet_lines(along, across)
        own = pltpu.make_async_copy(x_ref, o_ref.at[me], local_sem)
        own.start()
        programs = seq_gathers(x_ref, o_ref, sems)
        for program in programs:
            program.start()
        run_steps(*programs)
        for program in programs:
            program.finish()
        own.wait()

    return pl.pallas_call(
        kernel,
        out_shape=jax.ShapeDtypeStruct((seq, rows, width), block.dtype),
        in_specs=[pl.BlockSpec(memory_space=pl.ANY)],
        out_specs=pl.BlockSpec(memory_space=pl.ANY),
        scratch_shapes=[pltpu.SemaphoreType.DMA] + gather_sems(seq, rows),
        compiler_params=pltpu.CompilerParams(collective_id=collective_id, has_side_effects=True),
        name="seq_gather",
        cost_estimate=cost_of(80),
    )(block)


class Reduce:
    def __init__(self, first, second, me, flat, cuts, terms, out, from_first, from_second, sems):
        self.first, self.second, self.me, self.flat, self.cuts = first, second, me, flat, cuts
        self.terms, self.out = terms, out
        self.from_first, self.from_second = from_first, from_second
        self.send_sem, self.first_sem, self.second_sem = sems
        self.base = cuts[0][0]
        self.sent = []

    @staticmethod
    def scratch(rows_of, first_size, second_size, width):
        seq, rows, pieces = first_size * second_size, sum(r for _, r in rows_of), len(rows_of)
        lanes = 1 if first_size == 2 else 2
        return [
            pltpu.VMEM((lanes, second_size if first_size == 2 else seq, rows, width), BF),
            pltpu.VMEM((2, second_size, rows, width), BF),
            pltpu.SemaphoreType.DMA((seq, pieces)),
            pltpu.SemaphoreType.DMA((lanes, seq, pieces)),
            pltpu.SemaphoreType.DMA((2, second_size, pieces)),
        ]

    def _lane(self, turn):
        return 0 if self.first.size == 2 or turn > 0 else 1

    def _held(self, dest, spot):
        return spot if self.first.size == 2 else dest

    def _cut(self, h):
        return pl.ds(*self.cuts[h])

    def _inner(self, h):
        return pl.ds(self.cuts[h][0] - self.base, self.cuts[h][1])

    def _copy(self, src, dest, spot, h, line, turn):
        if line is self.first:
            lane = self._lane(turn)
            held = self._held(dest, spot)
            dst, sem = self.from_first.at[lane, held, self._inner(h)], self.first_sem.at[lane, dest, h]
        else:
            side = 0 if turn > 0 else 1
            dst, sem = self.from_second.at[side, spot, self._inner(h)], self.second_sem.at[side, spot, h]
        return send_to(src, dst, self.send_sem.at[dest, h], sem, line.device(turn))

    def _send(self, src, dest, spot, h, line, turn, ok):
        pl.when(ok)(lambda: self._copy(src, dest, spot, h, line, turn).start())
        self.sent.append((ok, src, dest, spot, h, line, turn))

    def _add(self, cond, whole, parts, out, h):
        first, count = self.cuts[h]

        @pl.when(cond)
        def _():
            def body(i, carry):
                at = pl.ds(pl.multiple_of(first + i * 16, 16), 16)
                inner = pl.ds(pl.multiple_of(first - self.base + i * 16, 16), 16)
                total = None
                for ref in whole:
                    total = ref[at, :].astype(F32) if total is None else total + ref[at, :].astype(F32)
                for ref in parts:
                    total = total + ref[inner, :].astype(F32)
                out[at, :] = total.astype(out.dtype)
                return carry

            lax.fori_loop(0, count // 16, body, 0)

    def _spread(self):
        for far in range(self.second.size - 1, -1, -1):
            for sign in (1, -1) if far else (1,):
                spot = self.second.place + sign * far
                yield far, sign, spot, self.second.inside(spot)

    def outward(self):
        first = self.first
        for step in range(first.size - 1, 0, -1):
            for far, sign, spot, ok in self._spread():
                for h in range(len(self.cuts)):
                    for turn in (1, -1):
                        yield lambda a=(step, spot, ok, h, turn): self._pass_on(*a)

    def _pass_on(self, step, spot, ok, h, turn):
        first = self.first
        goal = first.place + turn * step
        go = ok & first.inside(goal)
        dest = lax.select(go, self.flat(goal, spot), self.me)
        if first.size == 2:
            self._send(self.terms.at[dest, self._cut(h)], dest, spot, h, first, turn, go)
            return
        behind = first.has(-turn)
        self._await(go & behind, dest, spot, h, first, turn)
        self._add(go & behind, [self.terms.at[dest]], [self.from_first.at[self._lane(turn), dest]], self.terms.at[dest], h)
        self._send(self.terms.at[dest, self._cut(h)], dest, spot, h, first, turn, go)

    def _await(self, cond, dest, spot, h, line, turn):
        @pl.when(cond)
        def _():
            self._copy(self.terms.at[dest, self._cut(h)], dest, spot, h, line, turn).wait_recv()

    def inward(self):
        for far, sign, spot, ok in self._spread():
            for h in range(len(self.cuts)):
                yield lambda a=(far, sign, spot, ok, h): self._collect(*a)

    def _collect(self, far, sign, spot, ok, h):
        first, second, acc = self.first, self.second, self.terms
        dest = lax.select(ok, self.flat(first.place, spot), self.me)
        for turn in (1, -1):
            self._await(ok & first.has(-turn), dest, spot, h, first, turn)
        if first.size == 2:
            self._add(ok, [self.terms.at[dest]], [self.from_first.at[0, spot]], acc.at[dest], h)
        else:
            low, high = first.has(-1), first.has(1)
            lows, highs = self.from_first.at[self._lane(1), dest], self.from_first.at[self._lane(-1), dest]
            self._add(ok & low & high, [self.terms.at[dest]], [lows, highs], acc.at[dest], h)
            self._add(ok & low & jnp.logical_not(high), [self.terms.at[dest]], [lows], acc.at[dest], h)
            self._add(ok & high & jnp.logical_not(low), [self.terms.at[dest]], [highs], acc.at[dest], h)
        if far:
            behind = second.has(-sign)
            side = 0 if sign > 0 else 1
            self._await(ok & behind, dest, spot, h, second, sign)
            self._add(ok & behind, [acc.at[dest]], [self.from_second.at[side, spot]], acc.at[dest], h)
            self._send(acc.at[dest, self._cut(h)], dest, spot, h, second, sign, ok)
            return
        low, high = second.has(-1), second.has(1)
        self._await(low, dest, spot, h, second, 1)
        self._await(high, dest, spot, h, second, -1)
        lows, highs = self.from_second.at[0, spot], self.from_second.at[1, spot]
        self._add(low & high, [acc.at[dest]], [lows, highs], self.out, h)
        self._add(low & jnp.logical_not(high), [acc.at[dest]], [lows], self.out, h)
        self._add(high & jnp.logical_not(low), [acc.at[dest]], [highs], self.out, h)

    def finish(self):
        for ok, src, dest, spot, h, line, turn in self.sent:
            pl.when(ok)(lambda: self._copy(src, dest, spot, h, line, turn).wait_send())


def woven(*lists):
    keyed = [((i + 1) / len(entries), n, entry) for n, entries in enumerate(map(list, lists)) for i, entry in enumerate(entries)]
    return [entry for _, _, entry in sorted(keyed, key=lambda k: k[:2])]


def seq_reduces(terms, out, scratch):
    along, across, me, flat = seq_lines()
    early, late = cuts_of(terms.shape[1], across.size)
    return [
        Reduce(across, along, me, lambda y, z: flat(z, y), early, terms, out, *scratch[0:2], scratch[2:5]),
        Reduce(along, across, me, flat, late, terms, out, *scratch[5:7], scratch[7:10]),
    ]


def reduce_scratch(seq, rows, width):
    nz, ny = grid_of(seq)
    early, late = cuts_of(rows, ny)
    return Reduce.scratch(early, ny, nz, width) + Reduce.scratch(late, nz, ny, width)


def seq_reduce(terms, collective_id):
    seq, rows, width = terms.shape

    def kernel(p_ref, o_ref, sums, load_sem, *scratch):
        load = pltpu.make_async_copy(p_ref, sums, load_sem)
        load.start()
        along, across, _, _ = seq_lines()
        greet_lines(along, across)
        programs = seq_reduces(sums, o_ref, scratch)
        load.wait()
        for step in woven(*[p.outward() for p in programs]):
            step()
        for step in woven(*[p.inward() for p in programs]):
            step()
        for program in programs:
            program.finish()

    return pl.pallas_call(
        kernel,
        out_shape=jax.ShapeDtypeStruct((rows, width), F32),
        in_specs=[pl.BlockSpec(memory_space=pl.ANY)],
        out_specs=pl.BlockSpec(memory_space=pltpu.VMEM),
        scratch_shapes=[pltpu.VMEM((seq, rows, width), BF), pltpu.SemaphoreType.DMA] + reduce_scratch(seq, rows, width),
        compiler_params=pltpu.CompilerParams(
            collective_id=collective_id, has_side_effects=True, vmem_limit_bytes=VMEM_MOST
        ),
        name="seq_reduce",
        cost_estimate=cost_of(80),
    )(terms)


def rotary_tables(length):
    half_dim = HEAD_DIM // 2
    freqs = jnp.exp(-math.log(ROPE_BASE) * (2.0 * jnp.arange(half_dim, dtype=F32) / HEAD_DIM))
    angles = jnp.arange(length, dtype=jnp.int32).astype(F32)[:, None] * freqs[None, :]
    cosine, sine = jnp.cos(angles), jnp.sin(angles)
    return jnp.concatenate([cosine, cosine], axis=1), jnp.concatenate([-sine, sine], axis=1)


def turn_heads(values, cosine, sine):
    return values * cosine + pltpu.roll(values, HEAD_DIM // 2, 1) * sine


def as_columns(row):
    return jnp.broadcast_to(row, (128, row.shape[1])).T


def as_row(column):
    return jnp.broadcast_to(column, (column.shape[0], 128)).T[0:1]


def dot_rows(a, b):
    return lax.dot_general(a, b, (((1,), (1,)), ((), ())), preferred_element_type=F32)


def attend_first(tokens, cotangent, qkv_rows, proj_rows, packed, routes, tables, segments, n_router, collective_id):
    seq, ndp = lax.axis_size("seq"), lax.axis_size("dp")
    devices = seq * ndp
    rows, width = tokens.shape
    _, _, own_rows, cols = qkv_rows.shape
    num_seqs, length = segments.shape
    local_len = length // seq
    heads_here = cols // HEAD_DIM
    tile = 256
    per_block = 128 // own_rows

    def kernel(*refs):
        (x_ref, c_ref, qkv_ref, proj_ref, packed_ref, routes_ref, cos_ref, sin_ref, col_ref, row_ref) = refs[:10]
        (normed_out, c_out, w_v, proj_out, packed_out, routes_out) = refs[10:16]
        (raw_out, q_out, k_out, v_out, o_out, total_out) = refs[16:22]
        (x_v, normed_v, gains_v, sums_v, sums_got, local_sem, normed_sem) = refs[22:29]
        (part_send, part_recv, own_sem, qkv_send, qkv_recv, proj_send, proj_recv, proj_fwd) = refs[29:37]
        (small_send, small_recv, routes_send, routes_recv, sums_send, sums_recv) = refs[37:43]
        x_sems, c_sems = refs[43:47], refs[47:51]
        along, across, me, _ = seq_lines()
        x_line, core_line, dp, dp_flat = dp_lines()
        rank = dp * seq + me
        barrier = pltpu.get_barrier_semaphore()

        def device(peer):
            return (lax.div(peer, seq), lax.rem(peer, seq))

        def meet(step, carry):
            pl.semaphore_signal(
                barrier, 1, device_id=device(lax.rem(rank + step, devices)), device_id_type=MESH
            )
            return carry

        lax.fori_loop(1, devices, meet, 0)
        pl.semaphore_wait(barrier, devices - 1)

        def weight_rows(origin, h):
            return w_v.at[:, pl.ds(pl.multiple_of((origin * seq + h) * own_rows, own_rows), own_rows), :]

        own_x = pltpu.make_async_copy(x_ref, x_v.at[me], local_sem.at[0])
        own_c = pltpu.make_async_copy(c_ref, c_out.at[me], local_sem.at[2])
        own_qkv = pltpu.make_async_copy(qkv_ref.at[me], weight_rows(dp, me), own_sem)
        own_x.start()
        own_qkv.start()

        def part(peer, origin):
            return send_to(
                qkv_ref.at[peer], weight_rows(dp, origin), part_send.at[peer], part_recv.at[origin], (dp, peer)
            )

        for step in range(1, seq):
            part(lax.rem(me + step, seq), me).start()

        def small(peer, origin):
            return send_to(
                packed_ref, packed_out.at[origin], small_send.at[peer], small_recv.at[origin], device(peer)
            )

        def small_start(step, carry):
            small(lax.rem(rank + step, devices), rank).start()
            return carry

        lax.fori_loop(1, devices, small_start, 0)

        goal = lax.div(rank, ndp)
        place = lax.rem(rank, ndp)

        def proj_first(slot):
            return send_to(proj_ref, proj_out.at[slot], proj_send, proj_recv.at[slot], (dp, goal))

        stays = goal == me
        own_proj = pltpu.make_async_copy(proj_ref, proj_out.at[place], local_sem.at[1])
        pl.when(stays)(own_proj.start)
        pl.when(jnp.logical_not(stays))(lambda: proj_first(place).start())

        def route(peer, origin):
            return send_to(
                routes_ref, routes_out.at[origin], routes_send.at[peer], routes_recv.at[origin], (dp, peer)
            )

        for step in range(1, seq):
            route(lax.rem(me + step, seq), me).start()
        packed_out[rank] = packed_ref[...]
        routes_out[me] = routes_ref[...]

        gathers = seq_gathers(x_ref, x_v, x_sems)
        for program in gathers:
            program.start()

        def ready(h):
            @pl.when(h == me)
            def _():
                own_qkv.wait()

            @pl.when(h != me)
            def _():
                part(h, h).wait_recv()

        spread = Gather(
            x_line,
            core_line,
            dp,
            dp_flat,
            seq,
            lambda h: weight_rows(dp, h),
            weight_rows,
            qkv_send,
            qkv_recv,
            ready,
        )
        x_steps = sorted((s for p in gathers for s in p.steps()), key=lambda s: s[0])
        for hops, step in x_steps:
            if hops <= 1:
                step()
        spread.start()
        root = lax.div(me * ndp, seq)
        root_x, root_core = lax.div(root, 2), lax.rem(root, 2)
        on_line = core_line.place == root_core
        ways = [
            (on_line & (x_line.place >= root_x) & x_line.has(1), x_line.device(1), 0),
            (on_line & (x_line.place <= root_x) & x_line.has(-1), x_line.device(-1), 1),
            (on_line & core_line.has(1), core_line.device(1), 2),
            (on_line & core_line.has(-1), core_line.device(-1), 3),
        ]

        def onward(slot, way, target):
            return send_to(
                proj_out.at[slot], proj_out.at[slot], proj_fwd.at[slot, way], proj_recv.at[slot], target
            )

        rest = sorted(
            [s for s in x_steps if s[0] > 1] + [(hops + 0.75, step) for hops, step in spread.steps()],
            key=lambda s: s[0],
        )
        for _, step in rest:
            step()

        c_gathers = seq_gathers(c_ref, c_out, c_sems)
        own_c.start()
        for program in c_gathers:
            program.start()
        c_steps = sorted((s for p in c_gathers for s in p.steps()), key=lambda s: s[0])

        def move_cotangent(hops):
            while c_steps and c_steps[0][0] <= hops:
                c_steps.pop(0)[1]()

        for slot in range(ndp):
            held = (dp == root) & (lax.rem(me * ndp + slot, seq) == me)

            @pl.when(held)
            def _():
                own_proj.wait()

            @pl.when(jnp.logical_not(held))
            def _():
                onward(slot, 0, x_line.device(1)).wait_recv()

            for cond, target, way in ways:
                pl.when(cond)(lambda: onward(slot, way, target).start())

        def small_end(step, carry):
            source = lax.rem(rank + devices - step, devices)
            small(source, source).wait_recv()
            return carry

        lax.fori_loop(1, devices, small_end, 0)
        for block in range(width // 128):
            total = packed_out[block * per_block, n_router : n_router + 16, :].astype(F32)
            for i in range(1, per_block):
                total = total + packed_out[block * per_block + i, n_router : n_router + 16, :].astype(F32)
            gains_v[:, block * 128 : (block + 1) * 128] = total[0:8]
        own_x.wait()

        def normed_copy(src):
            return pltpu.make_async_copy(normed_v.at[src], normed_out.at[src], normed_sem.at[src])

        def project(src, carry):
            def strip(i, inner):
                at = pl.ds(pl.multiple_of(i * 16, 16), 16)
                values = x_v[src, at, :].astype(F32)
                factor = lax.rsqrt(jnp.mean(values * values, axis=-1, keepdims=True) + NORM_EPS)
                normed_v[src, at, :] = (values * factor * gains_v[0:1, :]).astype(BF)
                return inner

            lax.fori_loop(0, rows // 16, strip, 0)
            normed_copy(src).start()
            at = pl.ds(pl.multiple_of(src * rows, rows), rows)
            for j in range(2):
                raw = jnp.dot(normed_v[src], w_v[j], preferred_element_type=F32)
                raw_out[j, at, :] = raw
                sums_v[pl.ds(j * seq + src, 1), :] = as_row(jnp.sum(raw * raw, axis=1, keepdims=True))
            values = jnp.dot(normed_v[src], w_v[2], preferred_element_type=F32).astype(BF)
            for n in range(num_seqs):
                v_out[n, pl.ds(pl.multiple_of(src * local_len, local_len), local_len), :] = values[
                    n * local_len : (n + 1) * local_len
                ]
            return carry

        lax.fori_loop(0, seq // 2, project, 0)
        move_cotangent(1)
        lax.fori_loop(seq // 2, seq, project, 0)

        def square_sums(peer, origin):
            return send_to(sums_v, sums_got.at[origin], sums_send.at[peer], sums_recv.at[origin], (dp, peer))

        for step in range(1, seq):
            square_sums(lax.rem(me + step, seq), me).start()
        move_cotangent(2)
        total = sums_v[...]
        for step in range(1, seq):
            source = lax.rem(me + seq - step, seq)
            square_sums(source, source).wait_recv()
        sums_got[me] = sums_v[...]
        total = jnp.sum(sums_got[...], axis=0)
        for step in range(1, seq):
            square_sums(lax.rem(me + step, seq), me).wait_send()
        total_out[...] = total
        sums_v[...] = lax.rsqrt(total / width + NORM_EPS)

        def turn(src, carry):
            spots = pl.ds(pl.multiple_of(src * local_len, local_len), local_len)
            cosine, sine = cos_ref[spots, :], sin_ref[spots, :]
            for j, out in ((0, q_out), (1, k_out)):
                factor = as_columns(sums_v[pl.ds(j * seq + src, 1), :])
                for h in range(heads_here):
                    at = slice(h * HEAD_DIM, (h + 1) * HEAD_DIM)
                    gain = gains_v[
                        1 + j : 2 + j, pl.ds(pl.multiple_of(me * cols + h * HEAD_DIM, HEAD_DIM), HEAD_DIM)
                    ]
                    for n in range(num_seqs):
                        low, high = n * local_len, (n + 1) * local_len
                        values = raw_out[
                            j, pl.ds(pl.multiple_of(src * rows + low, local_len), local_len), at
                        ]
                        values = values * factor[low:high] * gain
                        out[n, spots, at] = turn_heads(values, cosine, sine).astype(BF)
            return carry

        lax.fori_loop(0, seq, turn, 0)
        move_cotangent(2.5)

        def attend(index, carry):
            n = lax.div(index, heads_here)
            head = pl.ds(pl.multiple_of(lax.rem(index, heads_here) * HEAD_DIM, HEAD_DIM), HEAD_DIM)
            for block in range(length // tile):
                low = block * tile
                limit = min(length, low + 2 * tile)
                scores = dot_rows(q_out[n, low : low + tile, head], k_out[n, 0:limit, head]) * HEAD_DIM**-0.5
                allowed = row_ref[n, 0:1, 0:limit] <= col_ref[n, low : low + tile, :]
                scores = jnp.where(allowed, scores, MASKED_SCORE)
                exps = jnp.exp(scores - jnp.max(scores, axis=-1, keepdims=True))
                probs = (exps / jnp.sum(exps, axis=-1, keepdims=True)).astype(BF)
                result = jnp.dot(probs, v_out[n, 0:limit, head], preferred_element_type=F32).astype(BF)
                for i in range(tile // local_len):
                    src = low // local_len + i
                    o_out[src, pl.ds(pl.multiple_of(n * local_len, local_len), local_len), head] = result[
                        i * local_len : (i + 1) * local_len
                    ]
            return carry

        lax.fori_loop(0, heads_here, attend, 0)
        move_cotangent(3)
        lax.fori_loop(heads_here, num_seqs * heads_here, attend, 0)
        move_cotangent(1000)

        for program in (*gathers, spread, *c_gathers):
            program.finish()
        for slot in range(ndp):
            for cond, target, way in ways:
                pl.when(cond)(lambda: onward(slot, way, target).wait_send())
        pl.when(jnp.logical_not(stays))(lambda: proj_first(place).wait_send())
        for step in range(1, seq):
            part(lax.rem(me + step, seq), me).wait_send()
            route(lax.rem(me + step, seq), me).wait_send()
            source = lax.rem(me + seq - step, seq)
            route(source, source).wait_recv()

        def small_sent(step, carry):
            small(lax.rem(rank + step, devices), rank).wait_send()
            return carry

        lax.fori_loop(1, devices, small_sent, 0)
        for src in range(seq):
            normed_copy(src).wait()
        own_c.wait()

    dma = pltpu.SemaphoreType.DMA
    hbm, vmem = pl.BlockSpec(memory_space=pl.ANY), pl.BlockSpec(memory_space=pltpu.VMEM)
    shaped = jax.ShapeDtypeStruct
    outs = [
        (shaped((seq, rows, width), BF), hbm),
        (shaped((seq, rows, width), BF), hbm),
        (shaped((3, width, cols), BF), vmem),
        (shaped((ndp,) + proj_rows.shape, BF), hbm),
        (shaped((devices,) + packed.shape, BF), vmem),
        (shaped((seq,) + routes.shape, jnp.int32), vmem),
        (shaped((2, seq * rows, cols), F32), vmem),
        (shaped((num_seqs, length, cols), BF), vmem),
        (shaped((num_seqs, length, cols), BF), vmem),
        (shaped((num_seqs, length, cols), BF), vmem),
        (shaped((seq, rows, cols), BF), vmem),
        (shaped((2 * seq, rows), F32), vmem),
    ]
    return pl.pallas_call(
        kernel,
        out_shape=[shape for shape, _ in outs],
        in_specs=[hbm] * 4 + [vmem] * 6,
        out_specs=[spec for _, spec in outs],
        scratch_shapes=[
            pltpu.VMEM((seq, rows, width), BF),
            pltpu.VMEM((seq, rows, width), BF),
            pltpu.VMEM((8, width), F32),
            pltpu.VMEM((2 * seq, rows), F32),
            pltpu.VMEM((seq, 2 * seq, rows), F32),
            dma((3,)),
            dma((seq,)),
            dma((seq,)),
            dma((seq,)),
            dma,
            dma((ndp, seq, 4)),
            dma((ndp, seq)),
            dma,
            dma((ndp,)),
            dma((ndp, 4)),
            dma((devices,)),
            dma((devices,)),
            dma((seq,)),
            dma((seq,)),
            dma((seq,)),
            dma((seq,)),
        ]
        + gather_sems(seq, rows)
        + gather_sems(seq, rows),
        compiler_params=pltpu.CompilerParams(
            collective_id=collective_id, has_side_effects=True, vmem_limit_bytes=VMEM_MOST
        ),
        name="attend_first",
        cost_estimate=cost_of(210),
    )(
        tokens,
        cotangent,
        qkv_rows,
        proj_rows,
        packed,
        routes,
        *tables,
        segments[:, :, None],
        segments[:, None, :],
    )


def small_exchange(arrays, axes, collective_id):
    sizes = [lax.axis_size(axis) for axis in axes]
    peers = math.prod(sizes)
    seq = lax.axis_size("seq")
    count = len(arrays)

    def kernel(*refs):
        ins, outs, (send_sem, recv_sem) = refs[:count], refs[count : 2 * count], refs[2 * count :]
        dp, sq = lax.axis_index("dp"), lax.axis_index("seq")
        me = sq if len(axes) == 1 else dp * seq + sq

        def device(peer):
            return (dp, peer) if len(axes) == 1 else (lax.div(peer, seq), lax.rem(peer, seq))

        barrier = pltpu.get_barrier_semaphore()
        for step in range(1, peers):
            pl.semaphore_signal(
                barrier, 1, device_id=device(lax.rem(me + step, peers)), device_id_type=MESH
            )
        pl.semaphore_wait(barrier, peers - 1)

        def copy(i, peer, src_slot):
            src = ins[i].at[0] if arrays[i].shape[0] == 1 else ins[i].at[peer]
            return pltpu.make_async_remote_copy(
                src_ref=src,
                dst_ref=outs[i].at[src_slot],
                send_sem=send_sem.at[i, peer],
                recv_sem=recv_sem.at[i, src_slot],
                device_id=device(peer),
                device_id_type=MESH,
            )

        for step in range(1, peers):
            for i in range(count):
                copy(i, lax.rem(me + step, peers), me).start()
        for i in range(count):
            outs[i][me] = ins[i][0] if arrays[i].shape[0] == 1 else ins[i][me]
        for step in range(1, peers):
            for i in range(count):
                copy(i, lax.rem(me + step, peers), me).wait_send()
                source = lax.rem(me + peers - step, peers)
                copy(i, source, source).wait_recv()

    return pl.pallas_call(
        kernel,
        out_shape=[jax.ShapeDtypeStruct((peers,) + a.shape[1:], a.dtype) for a in arrays],
        in_specs=[pl.BlockSpec(memory_space=pltpu.VMEM)] * count,
        out_specs=[pl.BlockSpec(memory_space=pltpu.VMEM)] * count,
        scratch_shapes=[
            pltpu.SemaphoreType.DMA((count, peers)),
            pltpu.SemaphoreType.DMA((count, peers)),
        ],
        compiler_params=pltpu.CompilerParams(collective_id=collective_id, has_side_effects=True),
        name="small_exchange",
        cost_estimate=cost_of(8),
    )(*arrays)


def middle_rows(o_head, proj_weight, tokens, gain, collective_id):
    seq, rows, cols = o_head.shape
    width = tokens.shape[1]
    nz, ny = grid_of(seq)
    n_seq = 10

    def kernel(*refs):
        o_ref, w_ref, x_ref, gain_ref, middle_out, ffn_out, all_out, terms_v, own_sem = refs[:9]
        scratch, sems = refs[9 : 9 + n_seq], refs[9 + n_seq :]
        along, across, me, _ = seq_lines()
        barrier = pltpu.get_barrier_semaphore()
        count = 0
        for line in (along, across):
            for turn in (1, -1):
                pl.when(line.has(turn))(
                    lambda: pl.semaphore_signal(
                        barrier, 1, device_id=line.device(turn), device_id_type=MESH
                    )
                )
                count = count + line.has(turn).astype(jnp.int32)

        def term(i, carry):
            dest = lax.rem(i, nz) * ny + lax.rem(across.place + 1 + lax.div(i, nz), ny)
            terms_v[dest] = jnp.dot(o_ref[dest], w_ref[...], preferred_element_type=F32).astype(BF)
            return carry

        lax.fori_loop(0, seq, term, 0)
        pl.semaphore_wait(barrier, count)
        reduces = seq_reduces(terms_v, middle_out, scratch)
        for step in woven(*[p.outward() for p in reduces]):
            step()
        for step in woven(*[p.inward() for p in reduces]):
            step()

        def strip(i, carry):
            at = pl.ds(pl.multiple_of(i * 16, 16), 16)
            values = middle_out[at, :] + x_ref[at, :].astype(F32)
            middle_out[at, :] = values
            factor = lax.rsqrt(jnp.mean(values * values, axis=-1, keepdims=True) + NORM_EPS)
            ffn_out[at, :] = (values * factor * gain_ref[...]).astype(BF)
            return carry

        lax.fori_loop(0, rows // 16, strip, 0)
        own = pltpu.make_async_copy(ffn_out, all_out.at[me], own_sem)
        own.start()
        gathers = seq_gathers(ffn_out, all_out, sems)
        for program in gathers:
            program.start()
        for program in reduces:
            program.finish()
        run_steps(*gathers)
        for program in gathers:
            program.finish()
        own.wait()

    vmem = pl.BlockSpec(memory_space=pltpu.VMEM)
    return pl.pallas_call(
        kernel,
        out_shape=[
            jax.ShapeDtypeStruct((rows, width), F32),
            jax.ShapeDtypeStruct((rows, width), BF),
            jax.ShapeDtypeStruct((seq, rows, width), BF),
        ],
        in_specs=[vmem] * 4,
        out_specs=[vmem, vmem, pl.BlockSpec(memory_space=pl.ANY)],
        scratch_shapes=[pltpu.VMEM((seq, rows, width), BF), pltpu.SemaphoreType.DMA]
        + reduce_scratch(seq, rows, width)
        + gather_sems(seq, rows),
        compiler_params=pltpu.CompilerParams(
            collective_id=collective_id, has_side_effects=True, vmem_limit_bytes=VMEM_MOST
        ),
        name="middle_rows",
        cost_estimate=cost_of(175),
    )(o_head, proj_weight, tokens, gain)


def attend_back(dz, mixed_terms, proj_weight, o_head, query, key, value, raw, squares, gains, tables, segments, collective_id):
    seq = lax.axis_size("seq")
    rows, width = dz.shape
    num_seqs, length, cols = query.shape
    local_len = length // seq
    heads_here = cols // HEAD_DIM
    tile = 256
    scale = HEAD_DIM**-0.5

    def kernel(*refs):
        (dz_ref, mixed_ref, w_ref, o_ref, q_ref, k_ref, v_ref, raw_ref, squares_ref, gains_ref) = refs[:10]
        (cos_ref, sin_ref, col_ref, row_ref) = refs[10:14]
        d_out, proj_out, gain_out, mixed_out = refs[14:18]
        (dz_v, do_v, turned, dk_acc, dv_acc, proj_acc, factor_v, inner_v, inner_got, mixed_v) = refs[18:28]
        own_sem, inner_send, inner_recv, mixed_sem = refs[28:32]
        sems, mixed_scratch = refs[32:36], refs[36:]
        dp = lax.axis_index("dp")
        along, across, me, _ = seq_lines()
        barrier = pltpu.get_barrier_semaphore()
        for step in range(1, seq):
            pl.semaphore_signal(
                barrier, 1, device_id=(dp, lax.rem(me + step, seq)), device_id_type=MESH
            )
        pl.semaphore_wait(barrier, seq - 1)
        own = pltpu.make_async_copy(dz_ref, dz_v.at[me], own_sem)
        own.start()
        mixed_load = pltpu.make_async_copy(mixed_ref, mixed_v, mixed_sem)
        mixed_load.start()
        programs = seq_gathers(dz_ref, dz_v, sems)
        for program in programs:
            program.start()
        factor_v[...] = lax.rsqrt(squares_ref[...] / width + NORM_EPS)
        proj_acc[...] = jnp.zeros_like(proj_acc)
        own.wait()
        run_steps(*programs)
        mixed_load.wait()
        reduces = seq_reduces(mixed_v, mixed_out, mixed_scratch)
        for step in woven(*[p.outward() for p in reduces]):
            step()
        inward = woven(*[p.inward() for p in reduces])
        in_all = len(inward)

        def move_mixed(share):
            while inward and in_all - len(inward) < share * in_all:
                inward.pop(0)()

        def project(src, carry):
            back = dot_rows(dz_v[src], w_ref[...]).astype(BF)
            for n in range(num_seqs):
                do_v[n, pl.ds(pl.multiple_of(src * local_len, local_len), local_len), :] = back[
                    n * local_len : (n + 1) * local_len
                ]
            proj_acc[...] += lax.dot_general(
                o_ref[src], dz_v[src], (((0,), (0,)), ((), ())), preferred_element_type=F32
            )
            return carry

        lax.fori_loop(0, seq, project, 0)
        proj_out[...] = proj_acc[...].astype(BF)

        def unturn(values, at):
            return values * cos_ref[at, :] - pltpu.roll(values, HEAD_DIM // 2, 1) * sin_ref[at, :]

        def attend(index, carry):
            n = lax.div(index, heads_here)
            head = pl.ds(pl.multiple_of(lax.rem(index, heads_here) * HEAD_DIM, HEAD_DIM), HEAD_DIM)
            dk_acc[...] = jnp.zeros_like(dk_acc)
            dv_acc[...] = jnp.zeros_like(dv_acc)
            for block in range(length // tile):
                low = block * tile
                limit = min(length, low + 2 * tile)
                spots = slice(low, low + tile)
                queries, keys, grads = q_ref[n, spots, head], k_ref[n, 0:limit, head], do_v[n, spots, head]
                scores = dot_rows(queries, keys) * scale
                allowed = row_ref[n, 0:1, 0:limit] <= col_ref[n, spots, :]
                scores = jnp.where(allowed, scores, MASKED_SCORE)
                exps = jnp.exp(scores - jnp.max(scores, axis=-1, keepdims=True))
                probs = exps / jnp.sum(exps, axis=-1, keepdims=True)
                grad_probs = dot_rows(grads, v_ref[n, 0:limit, head])
                inner = jnp.sum(probs * grad_probs, axis=-1, keepdims=True)
                grad_scores = (probs * (grad_probs - inner)).astype(BF)
                dq = jnp.dot(grad_scores, keys, preferred_element_type=F32) * scale
                turned[0, n, spots, head] = unturn(dq, spots)
                dk_acc[0:limit, :] += lax.dot_general(
                    grad_scores, queries, (((0,), (0,)), ((), ())), preferred_element_type=F32
                )
                dv_acc[0:limit, :] += lax.dot_general(
                    probs.astype(BF), grads, (((0,), (0,)), ((), ())), preferred_element_type=F32
                )
            for block in range(length // tile):
                spots = slice(block * tile, (block + 1) * tile)
                turned[1, n, spots, head] = unturn(dk_acc[spots, :] * scale, spots)
            for src in range(seq):
                d_out[2, src, pl.ds(pl.multiple_of(n * local_len, local_len), local_len), head] = dv_acc[
                    src * local_len : (src + 1) * local_len, :
                ].astype(BF)
            return carry

        lax.fori_loop(0, heads_here, attend, 0)
        move_mixed(0.3)
        lax.fori_loop(heads_here, num_seqs * heads_here, attend, 0)
        move_mixed(0.5)

        def pieces(j, src):
            spots = pl.ds(pl.multiple_of(src * local_len, local_len), local_len)
            grads = jnp.concatenate([turned[j, n, spots, :] for n in range(num_seqs)], axis=0)
            return grads, raw_ref[j, pl.ds(pl.multiple_of(src * rows, rows), rows), :]

        def wide(row):
            return jnp.concatenate([as_columns(row)] * heads_here, axis=1)

        def measure(src, carry):
            sums = []
            for j in range(2):
                grads, values = pieces(j, src)
                scaled = grads * gains_ref[j : j + 1, :]
                inner_v[pl.ds(j * seq + src, 1), :] = as_row(
                    jnp.sum(scaled * values, axis=1, keepdims=True)
                )
                factor = wide(factor_v[pl.ds(j * seq + src, 1), :])
                sums.append(carry[j] + jnp.sum(grads * values * factor, axis=0, keepdims=True))
            return tuple(sums)

        zero = jnp.zeros((1, cols), F32)
        gain_q, gain_k = lax.fori_loop(0, seq, measure, (zero, zero))
        gain_out[0:1, :] = gain_q
        gain_out[1:2, :] = gain_k
        gain_out[2:8, :] = jnp.zeros((6, cols), F32)

        def inner_copy(peer, origin):
            return send_to(
                inner_v, inner_got.at[origin], inner_send.at[peer], inner_recv.at[origin], (dp, peer)
            )

        for step in range(1, seq):
            inner_copy(lax.rem(me + step, seq), me).start()
        inner_got[me] = inner_v[...]
        move_mixed(0.7)
        for program in programs:
            program.finish()
        for step in range(1, seq):
            source = lax.rem(me + seq - step, seq)
            inner_copy(source, source).wait_recv()
            inner_copy(lax.rem(me + step, seq), me).wait_send()
        inner_v[...] = jnp.sum(inner_got[...], axis=0) / width

        def normalize(src, carry):
            for j in range(2):
                grads, values = pieces(j, src)
                factor = wide(factor_v[pl.ds(j * seq + src, 1), :])
                inner = wide(inner_v[pl.ds(j * seq + src, 1), :])
                scaled = grads * gains_ref[j : j + 1, :]
                d_out[j, src] = (factor * (scaled - values * factor * factor * inner)).astype(BF)
            return carry

        lax.fori_loop(0, seq, normalize, 0)
        move_mixed(1.0)
        for program in reduces:
            program.finish()

    dma = pltpu.SemaphoreType.DMA
    hbm, vmem = pl.BlockSpec(memory_space=pl.ANY), pl.BlockSpec(memory_space=pltpu.VMEM)
    return pl.pallas_call(
        kernel,
        out_shape=[
            jax.ShapeDtypeStruct((3, seq, rows, cols), BF),
            jax.ShapeDtypeStruct((cols, width), BF),
            jax.ShapeDtypeStruct((8, cols), F32),
            jax.ShapeDtypeStruct((rows, width), F32),
        ],
        in_specs=[hbm] * 2 + [vmem] * 12,
        out_specs=[vmem] * 4,
        scratch_shapes=[
            pltpu.VMEM((seq, rows, width), BF),
            pltpu.VMEM((num_seqs, length, cols), BF),
            pltpu.VMEM((2, num_seqs, length, cols), F32),
            pltpu.VMEM((length, HEAD_DIM), F32),
            pltpu.VMEM((length, HEAD_DIM), F32),
            pltpu.VMEM((cols, width), F32),
            pltpu.VMEM((2 * seq, rows), F32),
            pltpu.VMEM((2 * seq, rows), F32),
            pltpu.VMEM((seq, 2 * seq, rows), F32),
            pltpu.VMEM((seq, rows, width), BF),
            dma,
            dma((seq,)),
            dma((seq,)),
            dma,
        ]
        + gather_sems(seq, rows)
        + reduce_scratch(seq, rows, width),
        compiler_params=pltpu.CompilerParams(
            collective_id=collective_id, has_side_effects=True, vmem_limit_bytes=VMEM_MOST
        ),
        name="attend_back",
        cost_estimate=cost_of(180),
    )(
        dz,
        mixed_terms,
        proj_weight,
        o_head,
        query,
        key,
        value,
        raw,
        squares,
        gains,
        *tables,
        segments[:, :, None],
        segments[:, None, :],
    )


def last_sums(grads, normed, qkv_weight, proj_terms, router_terms, gain_heads, gain_ffn, gain_attn, collective_id):
    seq, ndp = lax.axis_size("seq"), lax.axis_size("dp")
    devices = seq * ndp
    _, _, rows, cols = grads.shape
    width = normed.shape[2]
    nz, ny = grid_of(seq)
    own_rows = proj_terms.shape[1]
    part_rows = 3 * own_rows
    n_router = router_terms.shape[1]
    per_block = 128 // own_rows
    n_seq = 10
    n_dp = 5
    block = 256

    def kernel(*refs):
        (d_ref, normed_ref, w_ref, proj_ref, router_ref, heads_ref, ffn_ref, gain_ref) = refs[:8]
        (o_ref, qkv_out, proj_out, sum_out) = refs[8:12]
        (terms_v, normed_v, qkv_v, qkv_sum, proj_v, proj_sum, packed_v, got, gains_v, normed_sem, proj_sem) = refs[12:23]
        rest = refs[23:]
        seq_scratch, rest = rest[:n_seq], rest[n_seq:]
        qkv_scratch, proj_scratch, rest = rest[:n_dp], rest[n_dp : 2 * n_dp], rest[2 * n_dp :]
        (part_send, part_recv, move_send, move_recv, small_send, small_recv, own_sem) = rest
        _, across, me, _ = seq_lines()
        x_line, core_line, dp, dp_flat = dp_lines()
        rank = dp * seq + me
        load_normed = pltpu.make_async_copy(normed_ref, normed_v, normed_sem)
        load_normed.start()
        load_proj = pltpu.make_async_copy(proj_ref, proj_v, proj_sem)
        load_proj.start()
        barrier = pltpu.get_barrier_semaphore()

        def device(peer):
            return (lax.div(peer, seq), lax.rem(peer, seq))

        def meet(step, carry):
            pl.semaphore_signal(
                barrier, 1, device_id=device(lax.rem(rank + step, devices)), device_id_type=MESH
            )
            return carry

        lax.fori_loop(1, devices, meet, 0)

        def normed_term(i, carry):
            dest = lax.rem(i, nz) * ny + lax.rem(across.place + 1 + lax.div(i, nz), ny)
            total = dot_rows(d_ref[0, dest], w_ref[0])
            for j in range(1, 3):
                total = total + dot_rows(d_ref[j, dest], w_ref[j])
            terms_v[dest] = total.astype(BF)
            return carry

        programs = seq_reduces(terms_v, o_ref, seq_scratch)
        lax.fori_loop(0, seq - nz, normed_term, 0)
        pl.semaphore_wait(barrier, devices - 1)
        for step in programs[0].outward():
            step()
        lax.fori_loop(seq - nz, seq, normed_term, 0)
        for step in programs[1].outward():
            step()
        inward = woven(*[p.inward() for p in programs])
        in_all = len(inward)

        def move_sums(share):
            while inward and in_all - len(inward) < share * in_all:
                inward.pop(0)()

        load_normed.wait()
        gains_v[...] = jnp.zeros_like(gains_v)
        for j in range(2):
            gains_v[1 + j : 2 + j, pl.ds(pl.multiple_of(me * cols, 128), cols)] = heads_ref[j : j + 1, :]
        gains_v[3:4, :] = ffn_ref[...]

        def weight_term(i, carry):
            at = pl.ds(pl.multiple_of(i * block, block), block)
            turned = normed_v[:, :, at].reshape(seq * rows, block).T
            gain = jnp.zeros((block, 1), F32)
            for j in range(3):
                term = jnp.dot(turned, d_ref[j].reshape(seq * rows, cols), preferred_element_type=F32)
                gain = gain + jnp.sum(term * w_ref[j, at, :].astype(F32), axis=1, keepdims=True)
                low = term.astype(BF)
                for piece in range(block // own_rows):
                    owner = i * (block // own_rows) + piece
                    spot = pl.multiple_of(lax.rem(owner, seq) * part_rows + j * own_rows, own_rows)
                    qkv_v[lax.div(owner, seq), pl.ds(spot, own_rows), :] = low[
                        piece * own_rows : (piece + 1) * own_rows
                    ]
            gains_v[0:1, at] = as_row(gain) / gain_ref[:, at]
            return carry

        blocks = width // block
        lax.fori_loop(0, blocks // 2, weight_term, 0)
        move_sums(0.12)
        lax.fori_loop(blocks // 2, blocks, weight_term, 0)
        move_sums(0.25)
        packed_v[:, 0:n_router, :] = router_ref[...]
        for peer in range(devices):
            at = peer // per_block * 128
            packed_v[peer, n_router : n_router + 8, :] = gains_v[:, at : at + 128]

        def small(peer, origin):
            return send_to(
                packed_v.at[peer], got.at[origin], small_send.at[peer], small_recv.at[origin], device(peer)
            )

        def small_start(step, carry):
            small(lax.rem(rank + step, devices), rank).start()
            return carry

        load_proj.wait()

        def over_dp(refs, out, buffers):
            return Reduce(
                core_line,
                x_line,
                dp,
                lambda core, x: dp_flat(x, core),
                [(0, refs.shape[1])],
                refs,
                out,
                *buffers[0:2],
                buffers[2:5],
            )

        owners = [over_dp(qkv_v, qkv_sum, qkv_scratch), over_dp(proj_v, proj_sum, proj_scratch)]
        for owner in owners:
            for step in owner.outward():
                step()
        lax.fori_loop(1, devices, small_start, 0)
        inner = [list(owner.inward()) for owner in owners]
        for steps in inner:
            for step in steps[:-1]:
                step()

        def part(peer, origin):
            return send_to(
                qkv_sum.at[pl.ds(pl.multiple_of(peer * part_rows, 16), part_rows)],
                qkv_out.at[origin],
                part_send.at[peer],
                part_recv.at[origin],
                (dp, peer),
            )

        own_part = pltpu.make_async_copy(
            qkv_sum.at[pl.ds(pl.multiple_of(me * part_rows, 16), part_rows)], qkv_out.at[me], own_sem.at[0]
        )
        goal = me * ndp + dp
        stays = goal == rank
        own_move = pltpu.make_async_copy(proj_sum, proj_out, own_sem.at[1])

        def move():
            return send_to(proj_sum, proj_out, move_send, move_recv, device(goal))

        move_sums(0.6)
        for owner_steps in inner:
            owner_steps[-1]()
        own_part.start()
        for step in range(1, seq):
            part(lax.rem(me + step, seq), me).start()
        pl.when(stays)(own_move.start)
        pl.when(jnp.logical_not(stays))(lambda: move().start())
        move_sums(1.0)

        got[rank] = packed_v[rank]

        def small_end(step, carry):
            small(lax.rem(rank + step, devices), rank).wait_send()
            source = lax.rem(rank + devices - step, devices)
            small(source, source).wait_recv()
            return carry

        lax.fori_loop(1, devices, small_end, 0)
        sum_out[...] = jnp.sum(got[...], axis=0)
        for program in (*programs, *owners):
            program.finish()
        for step in range(1, seq):
            part(lax.rem(me + step, seq), me).wait_send()
            source = lax.rem(me + seq - step, seq)
            part(source, source).wait_recv()
        own_part.wait()

        @pl.when(stays)
        def _():
            own_move.wait()

        @pl.when(jnp.logical_not(stays))
        def _():
            move().wait_send()
            move().wait_recv()

    dma = pltpu.SemaphoreType.DMA
    hbm, vmem = pl.BlockSpec(memory_space=pl.ANY), pl.BlockSpec(memory_space=pltpu.VMEM)
    return pl.pallas_call(
        kernel,
        out_shape=[
            jax.ShapeDtypeStruct((rows, width), F32),
            jax.ShapeDtypeStruct((seq, part_rows, cols), BF),
            jax.ShapeDtypeStruct((own_rows, width), BF),
            jax.ShapeDtypeStruct((n_router + 8, 128), F32),
        ],
        in_specs=[vmem, hbm, vmem, hbm] + [vmem] * 4,
        out_specs=[vmem] * 4,
        scratch_shapes=[
            pltpu.VMEM((seq, rows, width), BF),
            pltpu.VMEM((seq, rows, width), BF),
            pltpu.VMEM((ndp, seq * part_rows, cols), BF),
            pltpu.VMEM((seq * part_rows, cols), BF),
            pltpu.VMEM(proj_terms.shape, BF),
            pltpu.VMEM((own_rows, width), BF),
            pltpu.VMEM((devices, n_router + 8, 128), F32),
            pltpu.VMEM((devices, n_router + 8, 128), F32),
            pltpu.VMEM((8, width), F32),
            dma,
            dma,
        ]
        + reduce_scratch(seq, rows, width)
        + Reduce.scratch([(0, seq * part_rows)], 2, ndp // 2, cols)
        + Reduce.scratch([(0, own_rows)], 2, ndp // 2, width)
        + [dma((seq,)), dma((seq,)), dma, dma, dma((devices,)), dma((devices,)), dma((2,))],
        compiler_params=pltpu.CompilerParams(
            collective_id=collective_id, has_side_effects=True, vmem_limit_bytes=VMEM_MOST
        ),
        name="last_sums",
        cost_estimate=cost_of(110),
    )(grads, normed, qkv_weight, proj_terms, router_terms, gain_heads, gain_ffn, gain_attn)


def packed_rows(parts, sublanes):
    flat = jnp.concatenate(parts, axis=1)
    fill = -flat.shape[1] % (sublanes * 128)
    return jnp.pad(flat, ((0, 0), (0, fill))).reshape(flat.shape[0], -1, 128)


def experts_dispatch(ffn_all, cot_all, routes_all, router_full, me, experts, capacity):
    seq, rows, width = ffn_all.shape
    experts_all, top = router_full.shape[1], routes_all.shape[2]

    def kernel(me_ref, ffn_ref, cot_ref, routes_ref, router_ref, rows_out, cot_out, gate_out, slot_out, col_out):
        first = me_ref[0] * experts
        logits = jnp.dot(ffn_ref[0], router_ref[...], preferred_element_type=F32)
        exps = jnp.exp(logits - jnp.max(logits, axis=-1, keepdims=True))
        probs = exps / jnp.sum(exps, axis=-1, keepdims=True)
        lane = lax.broadcasted_iota(jnp.int32, (rows, experts_all), 1)
        wide_lane = lax.broadcasted_iota(jnp.int32, (rows, 128), 1)
        hits, gates = jnp.zeros((rows, 128), F32), []
        for e in range(experts):
            hit = jnp.sum((routes_ref[0] == first + e).astype(F32), axis=1, keepdims=True)
            hits = jnp.where(wide_lane == e, hit, hits)
            gates.append(jnp.sum(jnp.where(lane == first + e, probs, 0.0), axis=1, keepdims=True))
        below = lax.broadcasted_iota(jnp.int32, (rows, rows), 0) > lax.broadcasted_iota(
            jnp.int32, (rows, rows), 1
        )
        earlier = jnp.dot(below.astype(BF), hits.astype(BF), preferred_element_type=F32)
        slots = jnp.where(hits > 0.0, earlier, float(rows + 1))
        slots_row = slots.T
        number = lax.broadcasted_iota(jnp.int32, (capacity, rows), 0).astype(F32)
        places = []
        for e in range(experts):
            place = slots_row[e : e + 1, :] == number
            gate_out[e, 0] = jnp.sum(jnp.where(place, as_row(gates[e]), 0.0), axis=1, keepdims=True)
            slot_out[0, :, e : e + 1] = slots[:, e : e + 1]
            col_out[0, :, e : e + 1] = gates[e]
            places.append(place.astype(BF))
        for e in range(experts):
            rows_out[e, 0] = jnp.dot(places[e], ffn_ref[0], preferred_element_type=F32).astype(BF)
            cot_out[e, 0] = jnp.dot(places[e], cot_ref[0], preferred_element_type=F32).astype(BF)

    def source(s, _):
        return (s, 0, 0)

    def slot(s, _):
        return (0, s, 0, 0)

    shaped = jax.ShapeDtypeStruct
    return pl.pallas_call(
        kernel,
        out_shape=[
            shaped((experts, seq, capacity, width), BF),
            shaped((experts, seq, capacity, width), BF),
            shaped((experts, seq, capacity, 1), F32),
            shaped((seq, rows, experts), F32),
            shaped((seq, rows, experts), F32),
        ],
        grid_spec=pltpu.PrefetchScalarGridSpec(
            num_scalar_prefetch=1,
            grid=(seq,),
            in_specs=[
                pl.BlockSpec((1, rows, width), source),
                pl.BlockSpec((1, rows, width), source),
                pl.BlockSpec((1, rows, top), source),
                pl.BlockSpec((width, experts_all), lambda s, _: (0, 0)),
            ],
            out_specs=[
                pl.BlockSpec((experts, 1, capacity, width), slot),
                pl.BlockSpec((experts, 1, capacity, width), slot),
                pl.BlockSpec((experts, 1, capacity, 1), slot),
                pl.BlockSpec((1, rows, experts), source),
                pl.BlockSpec((1, rows, experts), source),
            ],
        ),
        compiler_params=pltpu.CompilerParams(vmem_limit_bytes=VMEM_MOST),
        name="experts_dispatch",
        cost_estimate=cost_of(15),
    )(me.reshape(1), ffn_all, cot_all, routes_all, router_full)


def experts_run(first, count, rows, cot_rows, gates, weight_in, weight_out):
    _, slots, width = rows.shape
    hidden_width = weight_out.shape[1]
    step = 256
    steps = hidden_width // step

    def kernel(
        rows_ref, cot_ref, gate_ref, in_ref, out_ref,
        y_out, drows_out, dgate_out, in_out, outw_out,
        gate_v, up_v, hidden_v, acc, dy_v, rows_t,
    ):
        phase, f = pl.program_id(1), pl.program_id(2)

        def accumulate(value):
            @pl.when(f == 0)
            def _():
                acc[...] = value

            @pl.when(f > 0)
            def _():
                acc[...] += value

        @pl.when(phase == 0)
        def _():
            @pl.when(f == 0)
            def _():
                rows_t[...] = rows_ref[0].T

            gate = jnp.dot(rows_ref[0], in_ref[0, 0], preferred_element_type=F32)
            up = jnp.dot(rows_ref[0], in_ref[0, 1], preferred_element_type=F32)
            gate_v[f] = gate
            up_v[f] = up
            hidden = (gate / (1.0 + jnp.exp(-gate)) * up).astype(BF)
            hidden_v[f] = hidden
            accumulate(jnp.dot(hidden, out_ref[0], preferred_element_type=F32))

            @pl.when(f == steps - 1)
            def _():
                result = acc[...].astype(BF)
                y_out[0] = result
                cot = cot_ref[0].astype(F32)
                dgate_out[0] = jnp.sum(cot * result.astype(F32), axis=1, keepdims=True)
                dy_v[...] = (cot * gate_ref[0]).astype(BF)

        @pl.when(phase == 1)
        def _():
            grad = dot_rows(dy_v[...], out_ref[0])
            gate, up = gate_v[f], up_v[f]
            sig = 1.0 / (1.0 + jnp.exp(-gate))
            dgate = (grad * up * sig * (1.0 + gate * (1.0 - sig))).astype(BF)
            dup = (grad * gate * sig).astype(BF)
            outw_out[0] = lax.dot_general(
                hidden_v[f], dy_v[...], (((0,), (0,)), ((), ())), preferred_element_type=F32
            ).astype(BF)
            in_out[0, 0] = jnp.dot(rows_t[...], dgate, preferred_element_type=F32).astype(BF)
            in_out[0, 1] = jnp.dot(rows_t[...], dup, preferred_element_type=F32).astype(BF)
            accumulate(dot_rows(dgate, in_ref[0, 0]) + dot_rows(dup, in_ref[0, 1]))

            @pl.when(f == steps - 1)
            def _():
                drows_out[0] = acc[...].astype(BF)

    shaped = jax.ShapeDtypeStruct
    by_expert = pl.BlockSpec((1, slots, width), lambda e, p, f: (first + e, 0, 0))
    whole = pl.BlockSpec((1, slots, width), lambda e, p, f: (e, 0, 0))
    flops = 18 * count * slots * width * hidden_width
    return pl.pallas_call(
        kernel,
        grid=(count, 2, steps),
        out_shape=[
            shaped((count, slots, width), BF),
            shaped((count, slots, width), BF),
            shaped((count, slots, 1), F32),
            shaped((count, 2, width, hidden_width), BF),
            shaped((count, hidden_width, width), BF),
        ],
        in_specs=[
            by_expert,
            by_expert,
            pl.BlockSpec((1, slots, 1), lambda e, p, f: (first + e, 0, 0)),
            pl.BlockSpec((1, 2, width, step), lambda e, p, f: (first + e, 0, 0, f)),
            pl.BlockSpec((1, step, width), lambda e, p, f: (first + e, f, 0)),
        ],
        out_specs=[
            whole,
            whole,
            pl.BlockSpec((1, slots, 1), lambda e, p, f: (e, 0, 0)),
            pl.BlockSpec((1, 2, width, step), lambda e, p, f: (e, 0, 0, f * p)),
            pl.BlockSpec((1, step, width), lambda e, p, f: (e, f * p, 0)),
        ],
        scratch_shapes=[
            pltpu.VMEM((steps, slots, step), F32),
            pltpu.VMEM((steps, slots, step), F32),
            pltpu.VMEM((steps, slots, step), BF),
            pltpu.VMEM((slots, width), F32),
            pltpu.VMEM((slots, width), BF),
            pltpu.VMEM((width, slots), BF),
        ],
        compiler_params=pltpu.CompilerParams(vmem_limit_bytes=VMEM_MOST),
        name="experts_run",
        cost_estimate=pl.CostEstimate(
            flops=flops, bytes_accessed=50_000_000, transcendentals=2 * count * slots * hidden_width
        ),
    )(rows, cot_rows, gates, weight_in, weight_out)


def experts_combine(outputs, drows, dgates, slot_cols, gate_cols, capacity):
    seq, rows, experts = slot_cols.shape
    parts = len(outputs)
    per = experts // parts
    width = outputs[0].shape[-1]

    def kernel(*refs):
        y_refs, d_refs, g_refs = refs[:parts], refs[parts : 2 * parts], refs[2 * parts : 3 * parts]
        slot_ref, gate_ref, mixed_out, dffn_out, dprob_out, y_v, d_v = refs[3 * parts :]
        slots = slot_ref[0]
        number = lax.broadcasted_iota(jnp.int32, (rows, capacity), 1).astype(F32)
        number_rows = lax.broadcasted_iota(jnp.int32, (capacity, rows), 0).astype(F32)
        gated, plain = [], []
        for e in range(experts):
            part, at = e // per, e % per
            place = slots[:, e : e + 1] == number
            gated.append(jnp.where(place, gate_ref[0, :, e : e + 1], 0.0).astype(BF))
            plain.append(place.astype(BF))
            cut = slice(e * capacity, (e + 1) * capacity)
            y_v[cut, :] = y_refs[part][at, 0]
            d_v[cut, :] = d_refs[part][at, 0]
            across = as_row(slots[:, e : e + 1]) == number_rows
            dprob_out[0, e : e + 1, :] = jnp.sum(
                jnp.where(across, g_refs[part][at, 0], 0.0), axis=0, keepdims=True
            )
        mixed_out[0] = jnp.dot(
            jnp.concatenate(gated, axis=1), y_v[...], preferred_element_type=F32
        ).astype(BF)
        dffn_out[0] = jnp.dot(
            jnp.concatenate(plain, axis=1), d_v[...], preferred_element_type=F32
        ).astype(BF)

    def source(s):
        return (s, 0, 0)

    slot_rows = pl.BlockSpec((per, 1, capacity, width), lambda s: (0, s, 0, 0))
    slot_ones = pl.BlockSpec((per, 1, capacity, 1), lambda s: (0, s, 0, 0))

    def split(arrays):
        return [a.reshape(per, seq, capacity, a.shape[-1]) for a in arrays]

    shaped = jax.ShapeDtypeStruct
    return pl.pallas_call(
        kernel,
        grid=(seq,),
        out_shape=[
            shaped((seq, rows, width), BF),
            shaped((seq, rows, width), BF),
            shaped((seq, experts, rows), F32),
        ],
        in_specs=[slot_rows] * (2 * parts)
        + [slot_ones] * parts
        + [pl.BlockSpec((1, rows, experts), source)] * 2,
        out_specs=[
            pl.BlockSpec((1, rows, width), source),
            pl.BlockSpec((1, rows, width), source),
            pl.BlockSpec((1, experts, rows), source),
        ],
        scratch_shapes=[
            pltpu.VMEM((experts * capacity, width), BF),
            pltpu.VMEM((experts * capacity, width), BF),
        ],
        compiler_params=pltpu.CompilerParams(vmem_limit_bytes=VMEM_MOST),
        name="experts_combine",
        cost_estimate=cost_of(15),
    )(*split(outputs), *split(drows), *split(dgates), slot_cols, gate_cols)


def rms_factor(values):
    return lax.rsqrt(jnp.mean(values * values, axis=-1, keepdims=True) + NORM_EPS)


def norm_back(values, factor, gain_row, incoming):
    scaled = incoming * gain_row
    gain_part = jnp.sum(incoming * values * factor, axis=0)
    inner = jnp.mean(scaled * values, axis=-1, keepdims=True)
    return (factor * (scaled - values * factor * factor * inner), gain_part)


def local(
    tokens,
    segments,
    routes,
    cotangent,
    attn_weight,
    router_weight,
    norm_gains,
    expert_in,
    expert_out,
):
    num_seqs, local_len, width = tokens.shape
    seq_length = segments.shape[1]
    seq, ndp = lax.axis_size("seq"), lax.axis_size("dp")
    me = lax.axis_index("seq")
    devices = seq * ndp
    cols = HEADS // seq * HEAD_DIM
    tok = num_seqs * local_len
    group = tok * seq
    own_rows = attn_weight.shape[0]
    experts_all = router_weight.shape[1]
    experts = experts_all // seq
    top = routes.shape[-1]
    capacity = (9 * tok * top + 8 * experts_all - 1) // (8 * experts_all)

    n_router = own_rows * experts_all
    token_rows, cot_low = tokens.reshape(tok, width), cotangent.reshape(tok, width)
    (router_rows,) = (packed_rows([router_weight.reshape(1, -1)], 16)[0],)
    rank = lax.axis_index("dp") * seq + me
    gain_rows_own = lax.dynamic_update_slice(
        jnp.zeros((16, 128), BF), norm_gains, (0, lax.rem(rank, 128 // own_rows) * own_rows)
    )
    tables = rotary_tables(seq_length)
    normed_all, cot_all, qkv_weight, proj_got, small_all, routes_all, raw, query_head, key_head, value_head, o_head, sums = (
        attend_first(
            token_rows,
            cot_low,
            attn_weight[:, :3].reshape(own_rows, 3, seq, cols).transpose(2, 1, 0, 3),
            attn_weight[:, 3],
            jnp.concatenate([router_rows, gain_rows_own], axis=0),
            routes.reshape(-1, 128),
            tables,
            segments,
            router_rows.shape[0],
            1,
        )
    )
    in_full = lax.all_gather(expert_in, "dp", axis=1, tiled=True)
    out_full = lax.all_gather(expert_out, "dp", axis=2, tiled=True)
    router_full = (
        small_all[:, : router_rows.shape[0]].reshape(devices, -1)[:, :n_router].reshape(width, experts_all)
    )
    gain_rows = (
        jnp.sum(
            small_all[:, router_rows.shape[0] : router_rows.shape[0] + 4]
            .reshape(width // 128, 128 // own_rows, 4, 128)
            .astype(F32),
            axis=1,
        )
        .transpose(1, 0, 2)
        .reshape(4, width)
    )
    routes_all = routes_all.reshape(seq, tok, top)
    proj_weight = proj_got.reshape(cols, width)
    resid_in = token_rows.astype(F32)
    factor_attn = rms_factor(resid_in)
    middle, ffn_low, ffn_all = middle_rows(o_head, proj_weight, token_rows, gain_rows[3:4], 5)
    factor_ffn = rms_factor(middle)

    slots = seq * capacity
    rows, cot_rows, gates, slot_cols, gate_cols = experts_dispatch(
        ffn_all, cot_all, routes_all, router_full, me, experts, capacity
    )
    rows, cot_rows = rows.reshape(experts, slots, width), cot_rows.reshape(experts, slots, width)
    gates = gates.reshape(experts, slots, 1)
    halves = 1
    count = experts // halves
    runs = [
        experts_run(half * count, count, rows, cot_rows, gates, in_full.transpose(0, 2, 1, 3), out_full)
        for half in range(halves)
    ]
    in_grads = [
        lax.psum_scatter(run[3].transpose(0, 2, 1, 3), "dp", scatter_dimension=1, tiled=True) for run in runs
    ]
    out_grads = [
        lax.psum_scatter(run[4], "dp", scatter_dimension=2, tiled=True) for run in runs
    ]
    expert_in_grad = jnp.concatenate(in_grads).astype(F32)
    expert_out_grad = jnp.concatenate(out_grads).astype(F32)
    mixed_terms, dffn_terms, grad_prob_here = experts_combine(
        [run[0] for run in runs], [run[1] for run in runs], [run[2] for run in runs], slot_cols, gate_cols, capacity
    )
    grad_ffn = seq_reduce(dffn_terms, 9)
    (grad_prob,) = small_exchange(
        [grad_prob_here.reshape(seq, -1, 128)], ("seq",), 10
    )
    grad_prob = grad_prob.reshape(experts_all, tok).T

    route_probs = jax.nn.softmax(
        jnp.dot(ffn_low, router_full, preferred_element_type=F32), axis=-1
    )
    grad_logits = (
        route_probs * (grad_prob - jnp.sum(route_probs * grad_prob, axis=-1, keepdims=True))
    ).astype(BF)
    router_term = jnp.einsum("td,te->de", ffn_low, grad_logits, preferred_element_type=F32)
    grad_ffn = grad_ffn + jnp.einsum(
        "te,de->td", grad_logits, router_full, preferred_element_type=F32
    )
    grad_middle, gain_ffn = norm_back(middle, factor_ffn, gain_rows[3], grad_ffn)
    grad_middle = grad_middle + cot_low.astype(F32)

    head_gains = jnp.pad(lax.dynamic_slice(gain_rows, (1, me * cols), (2, cols)), ((0, 6), (0, 0)))
    grad_heads, proj_term, gain_heads, mixed = attend_back(
        grad_middle.astype(BF),
        mixed_terms,
        proj_weight,
        o_head,
        query_head,
        key_head,
        value_head,
        raw,
        sums,
        head_gains,
        tables,
        segments,
        11,
    )
    block_out = (middle + mixed).astype(BF).reshape(num_seqs, local_len, width)

    grad_normed, qkv_out, proj_grad, total = last_sums(
        grad_heads,
        normed_all,
        qkv_weight,
        proj_term.reshape(ndp, own_rows, width),
        packed_rows([router_term.reshape(devices, -1)], 8),
        gain_heads,
        gain_ffn[None],
        gain_rows[0:1],
        14,
    )
    grad_resid, _ = norm_back(resid_in, factor_attn, gain_rows[0], grad_normed)
    input_grad = (grad_resid + grad_middle).reshape(num_seqs, local_len, width)
    qkv_grad = qkv_out.reshape(seq, 3, own_rows, cols).transpose(2, 1, 0, 3).reshape(own_rows, 3, width)
    attn_grad = jnp.concatenate([qkv_grad, proj_grad[:, None, :]], axis=1).astype(F32)
    gain_at = total.shape[0] - 8
    router_grad = total[:gain_at].reshape(-1)[:n_router].reshape(own_rows, experts_all)
    gain_grad = lax.dynamic_slice(
        total, (gain_at, lax.rem(rank, 128 // own_rows) * own_rows), (4, own_rows)
    )
    return (
        block_out,
        input_grad,
        attn_grad,
        router_grad,
        gain_grad,
        expert_in_grad,
        expert_out_grad,
    )


def solution(mesh):
    in_specs = (
        P("dp", "seq", None),
        P("dp", None),
        P("dp", "seq", None),
        P("dp", "seq", None),
        P(("dp", "seq"), None, None),
        P(("dp", "seq"), None),
        P(None, ("dp", "seq")),
        P("seq", "dp", None, None),
        P("seq", None, "dp"),
    )
    out_specs = (
        P("dp", "seq", None),
        P("dp", "seq", None),
        P(("dp", "seq"), None, None),
        P(("dp", "seq"), None),
        P(None, ("dp", "seq")),
        P("seq", "dp", None, None),
        P("seq", None, "dp"),
    )
    return jax.shard_map(local, mesh=mesh, in_specs=in_specs, out_specs=out_specs, check_vma=False)
```

```python
import math

import jax
import jax.numpy as jnp
from jax import lax
from jax.experimental import pallas as pl
from jax.experimental.pallas import tpu as pltpu
from jax.sharding import PartitionSpec as P

HEADS = 16
HEAD_DIM = 128
NORM_EPS = 1e-05
ROPE_BASE = 10000.0
MASKED_SCORE = -1e30
BF = jnp.bfloat16
F32 = jnp.float32
MESH = pl.DeviceIdType.MESH
VMEM_MOST = 60 << 20


class Line:
    def __init__(self, size, place, device):
        self.size, self.place, self.device = size, place, device

    def has(self, turn):
        return self.place < self.size - 1 if turn > 0 else self.place > 0

    def inside(self, place):
        return (place >= 0) & (place < self.size)


def grid_of(seq_size):
    lines = 4 if seq_size % 4 == 0 else 1
    return lines, seq_size // lines


def seq_lines():
    dp, me = lax.axis_index("dp"), lax.axis_index("seq")
    nz, ny = grid_of(lax.axis_size("seq"))
    along = Line(nz, lax.div(me, ny), lambda turn: (dp, me + turn * ny))
    across = Line(ny, lax.rem(me, ny), lambda turn: (dp, me + turn))
    return along, across, me, lambda z, y: z * ny + y


def dp_lines():
    dp, me = lax.axis_index("dp"), lax.axis_index("seq")
    along = Line(lax.axis_size("dp") // 2, lax.div(dp, 2), lambda turn: (dp + 2 * turn, me))
    across = Line(2, lax.rem(dp, 2), lambda turn: (dp + turn, me))
    return along, across, dp, lambda x, core: 2 * x + core


def cost_of(microseconds):
    return pl.CostEstimate(flops=0, bytes_accessed=microseconds * 3_600_000, transcendentals=0)


def send_to(src, dst, send_sem, recv_sem, device):
    return pltpu.make_async_remote_copy(
        src_ref=src,
        dst_ref=dst,
        send_sem=send_sem,
        recv_sem=recv_sem,
        device_id=device,
        device_id_type=MESH,
    )


def greet(targets):
    barrier = pltpu.get_barrier_semaphore()
    count = 0
    for cond, device in targets:

        @pl.when(cond)
        def _(device=device):
            pl.semaphore_signal(barrier, 1, device_id=device, device_id_type=MESH)

        count = count + cond.astype(jnp.int32)
    pl.semaphore_wait(barrier, count)


def greet_lines(*lines):
    greet([(line.has(turn), line.device(turn)) for line in lines for turn in (1, -1)])


def cuts_of(rows, ny):
    unit = rows // 16
    late = max(1, unit * 3 // 16) if ny == 2 else unit // 2
    early = unit - late
    half = (early + 1) // 2
    firsts = [(0, half * 16)] + ([(half * 16, (early - half) * 16)] if early > half else [])
    return firsts, [(early * 16, late * 16)]


class Gather:
    def __init__(self, first, second, me, flat, pieces, own, slot, send_sem, recv_sem, ready=None):
        self.first, self.second, self.me, self.flat = first, second, me, flat
        self.pieces, self.own, self.slot = pieces, own, slot
        self.send_sem, self.recv_sem, self.ready = send_sem, recv_sem, ready
        self.opening = [
            (line.has(turn), h, line, turn)
            for h in range(pieces)
            for line in (first, second)
            for turn in (1, -1)
        ]
        self.sent = [(ok, me, h, line, turn) for ok, h, line, turn in self.opening]

    def _source(self, origin, h):
        return self.own(h) if origin is self.me else self.slot(origin, h)

    def _copy(self, origin, h, line, turn):
        way = (0 if line is self.first else 2) + (turn > 0)
        return send_to(
            self._source(origin, h),
            self.slot(origin, h),
            self.send_sem.at[origin, h, way],
            self.recv_sem.at[origin, h],
            line.device(turn),
        )

    def start(self):
        for h in range(self.pieces):
            if self.ready is not None:
                self.ready(h)
            for ok, piece, line, turn in self.opening:
                if piece == h:
                    pl.when(ok)(lambda: self._copy(self.me, h, line, turn).start())

    def _arrival(self, place, side, h, sends):
        first, second = self.first, self.second
        cond = first.inside(place) & second.inside(side)
        origin = lax.select(cond, self.flat(place, side), self.me)
        onward = [(cond & line.has(turn), origin, h, line, turn) for line, turn in sends]
        self.sent += onward

        def thunk():
            @pl.when(cond)
            def _():
                self._copy(origin, h, first, 1).wait_recv()

            for ok, *way in onward:
                pl.when(ok)(lambda: self._copy(*way).start())

        return thunk

    def steps(self):
        first, second = self.first, self.second
        listed = []
        for far in range(1, first.size):
            for h in range(self.pieces):
                for sign in (1, -1):
                    listed.append(
                        (
                            far,
                            self._arrival(
                                first.place - sign * far,
                                second.place,
                                h,
                                [(first, sign), (second, 1), (second, -1)],
                            ),
                        )
                    )
        for step in range(1, second.size):
            for far in range(first.size):
                for h in range(self.pieces):
                    for sign in (1, -1) if far else (1,):
                        for turn in (1, -1):
                            listed.append(
                                (
                                    far + step + 0.5,
                                    self._arrival(
                                        first.place - sign * far,
                                        second.place - turn * step,
                                        h,
                                        [(second, turn)] if step < second.size - 1 else [],
                                    ),
                                )
                            )
        return listed

    def finish(self):
        for ok, *way in self.sent:
            pl.when(ok)(lambda: self._copy(*way).wait_send())


def run_steps(*programs):
    for _, step in sorted((s for p in programs for s in p.steps()), key=lambda s: s[0]):
        step()


def seq_gathers(block_ref, out_ref, sems):
    along, across, me, flat = seq_lines()
    early, late = cuts_of(block_ref.shape[0], across.size)
    made = []
    for cuts, first, second, index, (send_sem, recv_sem) in (
        (early, along, across, flat, sems[0:2]),
        (late, across, along, lambda y, z: flat(z, y), sems[2:4]),
    ):
        made.append(
            Gather(
                first,
                second,
                me,
                index,
                len(cuts),
                lambda h, cuts=cuts: block_ref.at[pl.ds(*cuts[h])],
                lambda origin, h, cuts=cuts: out_ref.at[origin, pl.ds(*cuts[h])],
                send_sem,
                recv_sem,
            )
        )
    return made


def gather_sems(seq, rows):
    early, late = cuts_of(rows, grid_of(seq)[1])
    return [
        pltpu.SemaphoreType.DMA((seq, len(early), 4)),
        pltpu.SemaphoreType.DMA((seq, len(early))),
        pltpu.SemaphoreType.DMA((seq, len(late), 4)),
        pltpu.SemaphoreType.DMA((seq, len(late))),
    ]


def seq_gather(block, collective_id):
    rows, width = block.shape
    seq = lax.axis_size("seq")

    def kernel(x_ref, o_ref, local_sem, *sems):
        along, across, me, _ = seq_lines()
        greet_lines(along, across)
        own = pltpu.make_async_copy(x_ref, o_ref.at[me], local_sem)
        own.start()
        programs = seq_gathers(x_ref, o_ref, sems)
        for program in programs:
            program.start()
        run_steps(*programs)
        for program in programs:
            program.finish()
        own.wait()

    return pl.pallas_call(
        kernel,
        out_shape=jax.ShapeDtypeStruct((seq, rows, width), block.dtype),
        in_specs=[pl.BlockSpec(memory_space=pl.ANY)],
        out_specs=pl.BlockSpec(memory_space=pl.ANY),
        scratch_shapes=[pltpu.SemaphoreType.DMA] + gather_sems(seq, rows),
        compiler_params=pltpu.CompilerParams(collective_id=collective_id, has_side_effects=True),
        name="seq_gather",
        cost_estimate=cost_of(80),
    )(block)


class Reduce:
    def __init__(self, first, second, me, flat, cuts, terms, out, from_first, from_second, sems):
        self.first, self.second, self.me, self.flat, self.cuts = first, second, me, flat, cuts
        self.terms, self.out = terms, out
        self.from_first, self.from_second = from_first, from_second
        self.send_sem, self.first_sem, self.second_sem = sems
        self.base = cuts[0][0]
        self.sent = []

    @staticmethod
    def scratch(rows_of, first_size, second_size, width):
        seq, rows, pieces = first_size * second_size, sum(r for _, r in rows_of), len(rows_of)
        lanes = 1 if first_size == 2 else 2
        return [
            pltpu.VMEM((lanes, second_size if first_size == 2 else seq, rows, width), BF),
            pltpu.VMEM((2, max(1, second_size - 1), rows, width), BF),
            pltpu.SemaphoreType.DMA((seq, pieces)),
            pltpu.SemaphoreType.DMA((lanes, seq, pieces)),
            pltpu.SemaphoreType.DMA((2, second_size, pieces)),
        ]

    def _lane(self, turn):
        return 0 if self.first.size == 2 or turn > 0 else 1

    def _held(self, dest, spot):
        return spot if self.first.size == 2 else dest

    def _passed(self, spot, side):
        return lax.max(spot - 1, 0) if side == 0 else lax.min(spot, max(0, self.second.size - 2))

    def _cut(self, h):
        return pl.ds(*self.cuts[h])

    def _inner(self, h):
        return pl.ds(self.cuts[h][0] - self.base, self.cuts[h][1])

    def _copy(self, dest, spot, h, line, turn):
        if line is self.first:
            lane = self._lane(turn)
            held = self._held(dest, spot)
            dst, sem = self.from_first.at[lane, held, self._inner(h)], self.first_sem.at[lane, dest, h]
        else:
            side = 0 if turn > 0 else 1
            dst = self.from_second.at[side, self._passed(spot, side), self._inner(h)]
            sem = self.second_sem.at[side, spot, h]
        return send_to(
            self.terms.at[dest, self._cut(h)], dst, self.send_sem.at[dest, h], sem, line.device(turn)
        )

    def _send(self, ok, *way):
        pl.when(ok)(lambda: self._copy(*way).start())

    def _add(self, cond, whole, parts, out, h):
        first, count = self.cuts[h]

        @pl.when(cond)
        def _():
            def body(i, carry):
                at = pl.ds(pl.multiple_of(first + i * 16, 16), 16)
                inner = pl.ds(pl.multiple_of(first - self.base + i * 16, 16), 16)
                total = None
                for ref in whole:
                    total = ref[at, :].astype(F32) if total is None else total + ref[at, :].astype(F32)
                for ref in parts:
                    total = total + ref[inner, :].astype(F32)
                out[at, :] = total.astype(out.dtype)
                return carry

            lax.fori_loop(0, count // 16, body, 0)

    def _spread(self):
        for far in range(self.second.size - 1, -1, -1):
            for sign in (1, -1) if far else (1,):
                spot = self.second.place + sign * far
                yield far, sign, spot, self.second.inside(spot)

    def outward(self):
        first = self.first
        for step in range(first.size - 1, 0, -1):
            for far, sign, spot, ok in self._spread():
                for h in range(len(self.cuts)):
                    for turn in (1, -1):
                        goal = first.place + turn * step
                        go = ok & first.inside(goal)
                        dest = lax.select(go, self.flat(goal, spot), self.me)
                        way = (dest, spot, h, first, turn)
                        self.sent.append((go, *way))
                        yield lambda go=go, way=way: self._pass_on(go, *way)

    def _pass_on(self, go, dest, spot, h, first, turn):
        if first.size > 2:
            behind = go & first.has(-turn)
            self._await(behind, dest, spot, h, first, turn)
            self._add(behind, [self.terms.at[dest]], [self.from_first.at[self._lane(turn), dest]], self.terms.at[dest], h)
        self._send(go, dest, spot, h, first, turn)

    def _await(self, cond, dest, spot, h, line, turn):
        @pl.when(cond)
        def _():
            self._copy(dest, spot, h, line, turn).wait_recv()

    def inward(self):
        for far, sign, spot, ok in self._spread():
            dest = lax.select(ok, self.flat(self.first.place, spot), self.me)
            for h in range(len(self.cuts)):
                if far:
                    self.sent.append((ok, dest, spot, h, self.second, sign))
                yield lambda a=(far, sign, spot, ok, dest, h): self._collect(*a)

    def _collect(self, far, sign, spot, ok, dest, h):
        first, second, acc = self.first, self.second, self.terms
        for turn in (1, -1):
            self._await(ok & first.has(-turn), dest, spot, h, first, turn)
        if first.size == 2:
            self._add(ok, [self.terms.at[dest]], [self.from_first.at[0, spot]], acc.at[dest], h)
        else:
            low, high = first.has(-1), first.has(1)
            lows, highs = self.from_first.at[self._lane(1), dest], self.from_first.at[self._lane(-1), dest]
            self._add(ok & low & high, [self.terms.at[dest]], [lows, highs], acc.at[dest], h)
            self._add(ok & low & jnp.logical_not(high), [self.terms.at[dest]], [lows], acc.at[dest], h)
            self._add(ok & high & jnp.logical_not(low), [self.terms.at[dest]], [highs], acc.at[dest], h)
        if far:
            behind = second.has(-sign)
            side = 0 if sign > 0 else 1
            self._await(ok & behind, dest, spot, h, second, sign)
            self._add(
                ok & behind, [acc.at[dest]], [self.from_second.at[side, self._passed(spot, side)]], acc.at[dest], h
            )
            self._send(ok, dest, spot, h, second, sign)
            return
        low, high = second.has(-1), second.has(1)
        self._await(low, dest, spot, h, second, 1)
        self._await(high, dest, spot, h, second, -1)
        lows = self.from_second.at[0, self._passed(spot, 0)]
        highs = self.from_second.at[1, self._passed(spot, 1)]
        self._add(low & high, [acc.at[dest]], [lows, highs], self.out, h)
        self._add(low & jnp.logical_not(high), [acc.at[dest]], [lows], self.out, h)
        self._add(high & jnp.logical_not(low), [acc.at[dest]], [highs], self.out, h)

    def finish(self):
        for ok, *way in self.sent:
            pl.when(ok)(lambda: self._copy(*way).wait_send())


def woven(*lists):
    keyed = [((i + 1) / len(entries), n, entry) for n, entries in enumerate(map(list, lists)) for i, entry in enumerate(entries)]
    return [entry for _, _, entry in sorted(keyed, key=lambda k: k[:2])]


def seq_reduces(terms, out, scratch):
    along, across, me, flat = seq_lines()
    early, late = cuts_of(terms.shape[1], across.size)
    return [
        Reduce(across, along, me, lambda y, z: flat(z, y), early, terms, out, *scratch[0:2], scratch[2:5]),
        Reduce(along, across, me, flat, late, terms, out, *scratch[5:7], scratch[7:10]),
    ]


def reduce_scratch(seq, rows, width):
    nz, ny = grid_of(seq)
    early, late = cuts_of(rows, ny)
    return Reduce.scratch(early, ny, nz, width) + Reduce.scratch(late, nz, ny, width)


def seq_reduce(terms, collective_id):
    seq, rows, width = terms.shape

    def kernel(p_ref, o_ref, sums, load_sem, *scratch):
        load = pltpu.make_async_copy(p_ref, sums, load_sem)
        load.start()
        along, across, _, _ = seq_lines()
        greet_lines(along, across)
        programs = seq_reduces(sums, o_ref, scratch)
        load.wait()
        for step in woven(*[p.outward() for p in programs]):
            step()
        for step in woven(*[p.inward() for p in programs]):
            step()
        for program in programs:
            program.finish()

    return pl.pallas_call(
        kernel,
        out_shape=jax.ShapeDtypeStruct((rows, width), F32),
        in_specs=[pl.BlockSpec(memory_space=pl.ANY)],
        out_specs=pl.BlockSpec(memory_space=pltpu.VMEM),
        scratch_shapes=[pltpu.VMEM((seq, rows, width), BF), pltpu.SemaphoreType.DMA] + reduce_scratch(seq, rows, width),
        compiler_params=pltpu.CompilerParams(
            collective_id=collective_id, has_side_effects=True, vmem_limit_bytes=VMEM_MOST
        ),
        name="seq_reduce",
        cost_estimate=cost_of(80),
    )(terms)


def rotary_tables(length):
    half_dim = HEAD_DIM // 2
    freqs = jnp.exp(-math.log(ROPE_BASE) * (2.0 * jnp.arange(half_dim, dtype=F32) / HEAD_DIM))
    angles = jnp.arange(length, dtype=jnp.int32).astype(F32)[:, None] * freqs[None, :]
    cosine, sine = jnp.cos(angles), jnp.sin(angles)
    return jnp.concatenate([cosine, cosine], axis=1), jnp.concatenate([-sine, sine], axis=1)


def turn_heads(values, cosine, sine):
    return values * cosine + pltpu.roll(values, HEAD_DIM // 2, 1) * sine


def as_columns(row):
    return jnp.broadcast_to(row, (128, row.shape[1])).T


def as_row(column):
    return jnp.broadcast_to(column, (column.shape[0], 128)).T[0:1]


def dot_rows(a, b):
    return lax.dot_general(a, b, (((1,), (1,)), ((), ())), preferred_element_type=F32)


def attend_first(tokens, cotangent, qkv_rows, proj_rows, packed, routes, tables, segments, n_router, collective_id):
    seq, ndp = lax.axis_size("seq"), lax.axis_size("dp")
    devices = seq * ndp
    rows, width = tokens.shape
    _, _, own_rows, cols = qkv_rows.shape
    num_seqs, length = segments.shape
    local_len = length // seq
    heads_here = cols // HEAD_DIM
    tile = 256
    per_block = 128 // own_rows
    ahead = cotangent.shape[0]

    def kernel(*refs):
        (x_ref, c_ref, qkv_ref, proj_ref, packed_ref, routes_ref, cos_ref, sin_ref, col_ref, row_ref) = refs[:10]
        (normed_out, c_out, w_v, proj_out, packed_out, routes_out) = refs[10:16]
        (raw_out, q_out, k_out, v_out, o_out, total_out) = refs[16:22]
        (x_v, normed_v, gains_v, sums_v, sums_got, local_sem, normed_sem) = refs[22:29]
        (part_send, part_recv, own_sem, qkv_send, qkv_recv, proj_send, proj_recv, proj_fwd) = refs[29:37]
        (small_send, small_recv, routes_send, routes_recv, sums_send, sums_recv) = refs[37:43]
        x_sems, c_sems = refs[43:47], refs[47:51]
        along, across, me, _ = seq_lines()
        x_line, core_line, dp, dp_flat = dp_lines()
        rank = dp * seq + me
        barrier = pltpu.get_barrier_semaphore()

        def device(peer):
            return (lax.div(peer, seq), lax.rem(peer, seq))

        def meet(step, carry):
            pl.semaphore_signal(
                barrier, 1, device_id=device(lax.rem(rank + step, devices)), device_id_type=MESH
            )
            return carry

        lax.fori_loop(1, devices, meet, 0)
        pl.semaphore_wait(barrier, devices - 1)

        def weight_rows(origin, h):
            return w_v.at[:, pl.ds(pl.multiple_of((origin * seq + h) * own_rows, own_rows), own_rows), :]

        own_x = pltpu.make_async_copy(x_ref, x_v.at[me], local_sem.at[0])
        own_c = pltpu.make_async_copy(c_ref, c_out.at[me], local_sem.at[2])
        own_qkv = pltpu.make_async_copy(qkv_ref.at[me], weight_rows(dp, me), own_sem)
        own_x.start()
        own_qkv.start()

        def part(peer, origin):
            return send_to(
                qkv_ref.at[peer], weight_rows(dp, origin), part_send.at[peer], part_recv.at[origin], (dp, peer)
            )

        for step in range(1, seq):
            part(lax.rem(me + step, seq), me).start()

        def small(peer, origin):
            return send_to(
                packed_ref, packed_out.at[origin], small_send.at[peer], small_recv.at[origin], device(peer)
            )

        def small_start(step, carry):
            small(lax.rem(rank + step, devices), rank).start()
            return carry

        lax.fori_loop(1, devices, small_start, 0)

        goal = lax.div(rank, ndp)
        place = lax.rem(rank, ndp)

        def proj_first(slot):
            return send_to(proj_ref, proj_out.at[slot], proj_send, proj_recv.at[slot], (dp, goal))

        stays = goal == me
        own_proj = pltpu.make_async_copy(proj_ref, proj_out.at[place], local_sem.at[1])
        pl.when(stays)(own_proj.start)
        pl.when(jnp.logical_not(stays))(lambda: proj_first(place).start())

        def route(peer, origin):
            return send_to(
                routes_ref, routes_out.at[origin], routes_send.at[peer], routes_recv.at[origin], (dp, peer)
            )

        for step in range(1, seq):
            route(lax.rem(me + step, seq), me).start()
        packed_out[rank] = packed_ref[...]
        routes_out[me] = routes_ref[...]

        gathers = seq_gathers(x_ref, x_v, x_sems)
        for program in gathers:
            program.start()

        def ready(h):
            @pl.when(h == me)
            def _():
                own_qkv.wait()

            @pl.when(h != me)
            def _():
                part(h, h).wait_recv()

        spread = Gather(
            x_line,
            core_line,
            dp,
            dp_flat,
            seq,
            lambda h: weight_rows(dp, h),
            weight_rows,
            qkv_send,
            qkv_recv,
            ready,
        )
        x_steps = sorted((s for p in gathers for s in p.steps()), key=lambda s: s[0])
        for hops, step in x_steps:
            if hops <= 1:
                step()
        spread.start()
        root = lax.div(me * ndp, seq)
        root_x, root_core = lax.div(root, 2), lax.rem(root, 2)
        on_line = core_line.place == root_core
        ways = [
            (on_line & (x_line.place >= root_x) & x_line.has(1), x_line.device(1), 0),
            (on_line & (x_line.place <= root_x) & x_line.has(-1), x_line.device(-1), 1),
            (on_line & core_line.has(1), core_line.device(1), 2),
            (on_line & core_line.has(-1), core_line.device(-1), 3),
        ]

        def onward(slot, way, target):
            return send_to(
                proj_out.at[slot], proj_out.at[slot], proj_fwd.at[slot, way], proj_recv.at[slot], target
            )

        rest = sorted(
            [s for s in x_steps if s[0] > 1] + [(hops + 0.75, step) for hops, step in spread.steps()],
            key=lambda s: s[0],
        )
        for _, step in rest:
            step()

        c_gathers = seq_gathers(c_ref, c_out, c_sems)
        own_c.start()
        for program in c_gathers:
            program.start()
        c_steps = sorted((s for p in c_gathers for s in p.steps()), key=lambda s: s[0])

        def move_cotangent(hops):
            while c_steps and c_steps[0][0] <= hops:
                c_steps.pop(0)[1]()

        for slot in range(ndp):
            held = (dp == root) & (lax.rem(me * ndp + slot, seq) == me)

            @pl.when(held)
            def _():
                own_proj.wait()

            @pl.when(jnp.logical_not(held))
            def _():
                onward(slot, 0, x_line.device(1)).wait_recv()

            for cond, target, way in ways:
                pl.when(cond)(lambda: onward(slot, way, target).start())

        def small_end(step, carry):
            source = lax.rem(rank + devices - step, devices)
            small(source, source).wait_recv()
            return carry

        lax.fori_loop(1, devices, small_end, 0)
        for block in range(width // 128):
            total = packed_out[block * per_block, n_router : n_router + 16, :].astype(F32)
            for i in range(1, per_block):
                total = total + packed_out[block * per_block + i, n_router : n_router + 16, :].astype(F32)
            gains_v[:, block * 128 : (block + 1) * 128] = total[0:8]
        own_x.wait()

        def normed_copy(src):
            return pltpu.make_async_copy(normed_v.at[src], normed_out.at[src], normed_sem.at[src])

        def project(src, carry):
            def strip(i, inner):
                at = pl.ds(pl.multiple_of(i * 16, 16), 16)
                values = x_v[src, at, :].astype(F32)
                factor = lax.rsqrt(jnp.mean(values * values, axis=-1, keepdims=True) + NORM_EPS)
                normed_v[src, at, :] = (values * factor * gains_v[0:1, :]).astype(BF)
                return inner

            lax.fori_loop(0, rows // 16, strip, 0, unroll=4)
            normed_copy(src).start()
            at = pl.ds(pl.multiple_of(src * rows, rows), rows)
            for j in range(2):
                raw = jnp.dot(normed_v[src], w_v[j], preferred_element_type=F32)
                raw_out[j, at, :] = raw
                sums_v[pl.ds(j * seq + src, 1), :] = as_row(jnp.sum(raw * raw, axis=1, keepdims=True))
            values = jnp.dot(normed_v[src], w_v[2], preferred_element_type=F32).astype(BF)
            for n in range(num_seqs):
                v_out[n, pl.ds(pl.multiple_of(src * local_len, local_len), local_len), :] = values[
                    n * local_len : (n + 1) * local_len
                ]
            return carry

        lax.fori_loop(0, seq // 2, project, 0)
        move_cotangent(1)
        lax.fori_loop(seq // 2, seq, project, 0)

        def square_sums(peer, origin):
            return send_to(sums_v, sums_got.at[origin], sums_send.at[peer], sums_recv.at[origin], (dp, peer))

        for step in range(1, seq):
            square_sums(lax.rem(me + step, seq), me).start()
        move_cotangent(2)
        total = sums_v[...]
        for step in range(1, seq):
            source = lax.rem(me + seq - step, seq)
            square_sums(source, source).wait_recv()
        sums_got[me] = sums_v[...]
        total = jnp.sum(sums_got[...], axis=0)
        for step in range(1, seq):
            square_sums(lax.rem(me + step, seq), me).wait_send()
        total_out[...] = total
        sums_v[...] = lax.rsqrt(total / width + NORM_EPS)

        def turn(src, carry):
            spots = pl.ds(pl.multiple_of(src * local_len, local_len), local_len)
            cosine, sine = cos_ref[spots, :], sin_ref[spots, :]
            for j, out in ((0, q_out), (1, k_out)):
                factor = as_columns(sums_v[pl.ds(j * seq + src, 1), :])
                for h in range(heads_here):
                    at = slice(h * HEAD_DIM, (h + 1) * HEAD_DIM)
                    gain = gains_v[
                        1 + j : 2 + j, pl.ds(pl.multiple_of(me * cols + h * HEAD_DIM, HEAD_DIM), HEAD_DIM)
                    ]
                    for n in range(num_seqs):
                        low, high = n * local_len, (n + 1) * local_len
                        values = raw_out[
                            j, pl.ds(pl.multiple_of(src * rows + low, local_len), local_len), at
                        ]
                        values = values * factor[low:high] * gain
                        out[n, spots, at] = turn_heads(values, cosine, sine).astype(BF)
            return carry

        lax.fori_loop(0, seq, turn, 0)
        move_cotangent(2.5)

        def attend(index, carry):
            n = lax.div(index, heads_here)
            head = pl.ds(pl.multiple_of(lax.rem(index, heads_here) * HEAD_DIM, HEAD_DIM), HEAD_DIM)
            for block in range(length // tile):
                low = block * tile
                limit = min(length, low + 2 * tile)
                scores = dot_rows(q_out[n, low : low + tile, head], k_out[n, 0:limit, head]) * HEAD_DIM**-0.5
                allowed = row_ref[n, 0:1, 0:limit] <= col_ref[n, low : low + tile, :]
                scores = jnp.where(allowed, scores, MASKED_SCORE)
                exps = jnp.exp(scores - jnp.max(scores, axis=-1, keepdims=True))
                probs = (exps / jnp.sum(exps, axis=-1, keepdims=True)).astype(BF)
                result = jnp.dot(probs, v_out[n, 0:limit, head], preferred_element_type=F32).astype(BF)
                for i in range(tile // local_len):
                    src = low // local_len + i
                    o_out[src, pl.ds(pl.multiple_of(n * local_len, local_len), local_len), head] = result[
                        i * local_len : (i + 1) * local_len
                    ]
            return carry

        lax.fori_loop(0, heads_here, attend, 0)
        move_cotangent(3)
        lax.fori_loop(heads_here, num_seqs * heads_here, attend, 0)
        move_cotangent(1000)

        for program in (*gathers, spread, *c_gathers):
            program.finish()
        for slot in range(ndp):
            for cond, target, way in ways:
                pl.when(cond)(lambda: onward(slot, way, target).wait_send())
        pl.when(jnp.logical_not(stays))(lambda: proj_first(place).wait_send())
        for step in range(1, seq):
            part(lax.rem(me + step, seq), me).wait_send()
            route(lax.rem(me + step, seq), me).wait_send()
            source = lax.rem(me + seq - step, seq)
            route(source, source).wait_recv()

        def small_sent(step, carry):
            small(lax.rem(rank + step, devices), rank).wait_send()
            return carry

        lax.fori_loop(1, devices, small_sent, 0)
        for src in range(seq):
            normed_copy(src).wait()
        own_c.wait()

    dma = pltpu.SemaphoreType.DMA
    hbm, vmem = pl.BlockSpec(memory_space=pl.ANY), pl.BlockSpec(memory_space=pltpu.VMEM)
    shaped = jax.ShapeDtypeStruct
    outs = [
        (shaped((seq, rows, width), BF), hbm),
        (shaped((seq, ahead, width), BF), hbm),
        (shaped((3, width, cols), BF), vmem),
        (shaped((ndp,) + proj_rows.shape, BF), hbm),
        (shaped((devices,) + packed.shape, BF), vmem),
        (shaped((seq,) + routes.shape, jnp.int32), vmem),
        (shaped((2, seq * rows, cols), F32), vmem),
        (shaped((num_seqs, length, cols), BF), vmem),
        (shaped((num_seqs, length, cols), BF), vmem),
        (shaped((num_seqs, length, cols), BF), vmem),
        (shaped((seq, rows, cols), BF), vmem),
        (shaped((2 * seq, rows), F32), vmem),
    ]
    return pl.pallas_call(
        kernel,
        out_shape=[shape for shape, _ in outs],
        in_specs=[hbm] * 4 + [vmem] * 6,
        out_specs=[spec for _, spec in outs],
        scratch_shapes=[
            pltpu.VMEM((seq, rows, width), BF),
            pltpu.VMEM((seq, rows, width), BF),
            pltpu.VMEM((8, width), F32),
            pltpu.VMEM((2 * seq, rows), F32),
            pltpu.VMEM((seq, 2 * seq, rows), F32),
            dma((3,)),
            dma((seq,)),
            dma((seq,)),
            dma((seq,)),
            dma,
            dma((ndp, seq, 4)),
            dma((ndp, seq)),
            dma,
            dma((ndp,)),
            dma((ndp, 4)),
            dma((devices,)),
            dma((devices,)),
            dma((seq,)),
            dma((seq,)),
            dma((seq,)),
            dma((seq,)),
        ]
        + gather_sems(seq, rows)
        + gather_sems(seq, ahead),
        compiler_params=pltpu.CompilerParams(
            collective_id=collective_id, has_side_effects=True, vmem_limit_bytes=VMEM_MOST
        ),
        name="attend_first",
        cost_estimate=cost_of(210),
    )(
        tokens,
        cotangent,
        qkv_rows,
        proj_rows,
        packed,
        routes,
        *tables,
        segments[:, :, None],
        segments[:, None, :],
    )


def small_exchange(arrays, axes, collective_id):
    sizes = [lax.axis_size(axis) for axis in axes]
    peers = math.prod(sizes)
    seq = lax.axis_size("seq")
    count = len(arrays)

    def kernel(*refs):
        ins, outs, (send_sem, recv_sem) = refs[:count], refs[count : 2 * count], refs[2 * count :]
        dp, sq = lax.axis_index("dp"), lax.axis_index("seq")
        me = sq if len(axes) == 1 else dp * seq + sq

        def device(peer):
            return (dp, peer) if len(axes) == 1 else (lax.div(peer, seq), lax.rem(peer, seq))

        barrier = pltpu.get_barrier_semaphore()
        for step in range(1, peers):
            pl.semaphore_signal(
                barrier, 1, device_id=device(lax.rem(me + step, peers)), device_id_type=MESH
            )
        pl.semaphore_wait(barrier, peers - 1)

        def copy(i, peer, src_slot):
            src = ins[i].at[0] if arrays[i].shape[0] == 1 else ins[i].at[peer]
            return pltpu.make_async_remote_copy(
                src_ref=src,
                dst_ref=outs[i].at[src_slot],
                send_sem=send_sem.at[i, peer],
                recv_sem=recv_sem.at[i, src_slot],
                device_id=device(peer),
                device_id_type=MESH,
            )

        for step in range(1, peers):
            for i in range(count):
                copy(i, lax.rem(me + step, peers), me).start()
        for i in range(count):
            outs[i][me] = ins[i][0] if arrays[i].shape[0] == 1 else ins[i][me]
        for step in range(1, peers):
            for i in range(count):
                copy(i, lax.rem(me + step, peers), me).wait_send()
                source = lax.rem(me + peers - step, peers)
                copy(i, source, source).wait_recv()

    return pl.pallas_call(
        kernel,
        out_shape=[jax.ShapeDtypeStruct((peers,) + a.shape[1:], a.dtype) for a in arrays],
        in_specs=[pl.BlockSpec(memory_space=pltpu.VMEM)] * count,
        out_specs=[pl.BlockSpec(memory_space=pltpu.VMEM)] * count,
        scratch_shapes=[
            pltpu.SemaphoreType.DMA((count, peers)),
            pltpu.SemaphoreType.DMA((count, peers)),
        ],
        compiler_params=pltpu.CompilerParams(collective_id=collective_id, has_side_effects=True),
        name="small_exchange",
        cost_estimate=cost_of(8),
    )(*arrays)


def middle_rows(o_head, proj_weight, tokens, gain, collective_id):
    seq, rows, cols = o_head.shape
    width = tokens.shape[1]
    nz, ny = grid_of(seq)
    n_seq = 10

    def kernel(*refs):
        o_ref, w_ref, x_ref, gain_ref, middle_out, ffn_out, all_out, terms_v, own_sem = refs[:9]
        scratch, sems = refs[9 : 9 + n_seq], refs[9 + n_seq :]
        along, across, me, _ = seq_lines()
        barrier = pltpu.get_barrier_semaphore()
        count = 0
        for line in (along, across):
            for turn in (1, -1):
                pl.when(line.has(turn))(
                    lambda: pl.semaphore_signal(
                        barrier, 1, device_id=line.device(turn), device_id_type=MESH
                    )
                )
                count = count + line.has(turn).astype(jnp.int32)

        def term(i, carry):
            dest = lax.rem(i, nz) * ny + lax.rem(across.place + 1 + lax.div(i, nz), ny)
            terms_v[dest] = jnp.dot(o_ref[dest], w_ref[...], preferred_element_type=F32).astype(BF)
            return carry

        lax.fori_loop(0, seq, term, 0)
        pl.semaphore_wait(barrier, count)
        reduces = seq_reduces(terms_v, middle_out, scratch)
        for step in woven(*[p.outward() for p in reduces]):
            step()
        for step in woven(*[p.inward() for p in reduces]):
            step()

        def strip(i, carry):
            at = pl.ds(pl.multiple_of(i * 16, 16), 16)
            values = middle_out[at, :] + x_ref[at, :].astype(F32)
            middle_out[at, :] = values
            factor = lax.rsqrt(jnp.mean(values * values, axis=-1, keepdims=True) + NORM_EPS)
            ffn_out[at, :] = (values * factor * gain_ref[...]).astype(BF)
            return carry

        lax.fori_loop(0, rows // 16, strip, 0, unroll=4)
        own = pltpu.make_async_copy(ffn_out, all_out.at[me], own_sem)
        own.start()
        gathers = seq_gathers(ffn_out, all_out, sems)
        for program in gathers:
            program.start()
        for program in reduces:
            program.finish()
        run_steps(*gathers)
        for program in gathers:
            program.finish()
        own.wait()

    vmem = pl.BlockSpec(memory_space=pltpu.VMEM)
    return pl.pallas_call(
        kernel,
        out_shape=[
            jax.ShapeDtypeStruct((rows, width), F32),
            jax.ShapeDtypeStruct((rows, width), BF),
            jax.ShapeDtypeStruct((seq, rows, width), BF),
        ],
        in_specs=[vmem] * 4,
        out_specs=[vmem, vmem, pl.BlockSpec(memory_space=pl.ANY)],
        scratch_shapes=[pltpu.VMEM((seq, rows, width), BF), pltpu.SemaphoreType.DMA]
        + reduce_scratch(seq, rows, width)
        + gather_sems(seq, rows),
        compiler_params=pltpu.CompilerParams(
            collective_id=collective_id, has_side_effects=True, vmem_limit_bytes=VMEM_MOST
        ),
        name="middle_rows",
        cost_estimate=cost_of(175),
    )(o_head, proj_weight, tokens, gain)


def attend_back(dz, proj_weight, o_head, query, key, value, raw, squares, gains, tables, segments, collective_id):
    seq = lax.axis_size("seq")
    rows, width = dz.shape
    num_seqs, length, cols = query.shape
    local_len = length // seq
    heads_here = cols // HEAD_DIM
    tile = 256
    scale = HEAD_DIM**-0.5

    def kernel(*refs):
        (dz_ref, w_ref, o_ref, q_ref, k_ref, v_ref, raw_ref, squares_ref, gains_ref) = refs[:9]
        (cos_ref, sin_ref, col_ref, row_ref) = refs[9:13]
        d_out, proj_out, gain_out = refs[13:16]
        (dz_v, do_v, turned, dk_acc, dv_acc, proj_acc, factor_v, inner_v, inner_got) = refs[16:25]
        own_sem, inner_send, inner_recv = refs[25:28]
        sems = refs[28:]
        dp = lax.axis_index("dp")
        along, across, me, _ = seq_lines()
        barrier = pltpu.get_barrier_semaphore()
        for step in range(1, seq):
            pl.semaphore_signal(
                barrier, 1, device_id=(dp, lax.rem(me + step, seq)), device_id_type=MESH
            )
        pl.semaphore_wait(barrier, seq - 1)
        own = pltpu.make_async_copy(dz_ref, dz_v.at[me], own_sem)
        own.start()
        programs = seq_gathers(dz_ref, dz_v, sems)
        for program in programs:
            program.start()
        factor_v[...] = lax.rsqrt(squares_ref[...] / width + NORM_EPS)
        proj_acc[...] = jnp.zeros_like(proj_acc)
        own.wait()
        run_steps(*programs)

        def project(src, carry):
            back = dot_rows(dz_v[src], w_ref[...]).astype(BF)
            for n in range(num_seqs):
                do_v[n, pl.ds(pl.multiple_of(src * local_len, local_len), local_len), :] = back[
                    n * local_len : (n + 1) * local_len
                ]
            proj_acc[...] += lax.dot_general(
                o_ref[src], dz_v[src], (((0,), (0,)), ((), ())), preferred_element_type=F32
            )
            return carry

        lax.fori_loop(0, seq, project, 0)
        proj_out[...] = proj_acc[...].astype(BF)

        def unturn(values, at):
            return values * cos_ref[at, :] - pltpu.roll(values, HEAD_DIM // 2, 1) * sin_ref[at, :]

        def attend(index, carry):
            n = lax.div(index, heads_here)
            head = pl.ds(pl.multiple_of(lax.rem(index, heads_here) * HEAD_DIM, HEAD_DIM), HEAD_DIM)
            dk_acc[...] = jnp.zeros_like(dk_acc)
            dv_acc[...] = jnp.zeros_like(dv_acc)
            for block in range(length // tile):
                low = block * tile
                limit = min(length, low + 2 * tile)
                spots = slice(low, low + tile)
                queries, keys, grads = q_ref[n, spots, head], k_ref[n, 0:limit, head], do_v[n, spots, head]
                scores = dot_rows(queries, keys) * scale
                allowed = row_ref[n, 0:1, 0:limit] <= col_ref[n, spots, :]
                scores = jnp.where(allowed, scores, MASKED_SCORE)
                exps = jnp.exp(scores - jnp.max(scores, axis=-1, keepdims=True))
                probs = exps / jnp.sum(exps, axis=-1, keepdims=True)
                grad_probs = dot_rows(grads, v_ref[n, 0:limit, head])
                inner = jnp.sum(probs * grad_probs, axis=-1, keepdims=True)
                grad_scores = (probs * (grad_probs - inner)).astype(BF)
                dq = jnp.dot(grad_scores, keys, preferred_element_type=F32) * scale
                turned[0, n, spots, head] = unturn(dq, spots)
                dk_acc[0:limit, :] += lax.dot_general(
                    grad_scores, queries, (((0,), (0,)), ((), ())), preferred_element_type=F32
                )
                dv_acc[0:limit, :] += lax.dot_general(
                    probs.astype(BF), grads, (((0,), (0,)), ((), ())), preferred_element_type=F32
                )
            for block in range(length // tile):
                spots = slice(block * tile, (block + 1) * tile)
                turned[1, n, spots, head] = unturn(dk_acc[spots, :] * scale, spots)
            for src in range(seq):
                d_out[2, src, pl.ds(pl.multiple_of(n * local_len, local_len), local_len), head] = dv_acc[
                    src * local_len : (src + 1) * local_len, :
                ].astype(BF)
            return carry

        lax.fori_loop(0, num_seqs * heads_here, attend, 0)

        def pieces(j, src):
            spots = pl.ds(pl.multiple_of(src * local_len, local_len), local_len)
            grads = jnp.concatenate([turned[j, n, spots, :] for n in range(num_seqs)], axis=0)
            return grads, raw_ref[j, pl.ds(pl.multiple_of(src * rows, rows), rows), :]

        def wide(row):
            return jnp.concatenate([as_columns(row)] * heads_here, axis=1)

        def measure(src, carry):
            sums = []
            for j in range(2):
                grads, values = pieces(j, src)
                scaled = grads * gains_ref[j : j + 1, :]
                inner_v[pl.ds(j * seq + src, 1), :] = as_row(
                    jnp.sum(scaled * values, axis=1, keepdims=True)
                )
                factor = wide(factor_v[pl.ds(j * seq + src, 1), :])
                sums.append(carry[j] + jnp.sum(grads * values * factor, axis=0, keepdims=True))
            return tuple(sums)

        zero = jnp.zeros((1, cols), F32)
        gain_q, gain_k = lax.fori_loop(0, seq, measure, (zero, zero))
        gain_out[0:1, :] = gain_q
        gain_out[1:2, :] = gain_k
        gain_out[2:8, :] = jnp.zeros((6, cols), F32)

        def inner_copy(peer, origin):
            return send_to(
                inner_v, inner_got.at[origin], inner_send.at[peer], inner_recv.at[origin], (dp, peer)
            )

        for step in range(1, seq):
            inner_copy(lax.rem(me + step, seq), me).start()
        inner_got[me] = inner_v[...]
        for program in programs:
            program.finish()
        for step in range(1, seq):
            source = lax.rem(me + seq - step, seq)
            inner_copy(source, source).wait_recv()
            inner_copy(lax.rem(me + step, seq), me).wait_send()
        inner_v[...] = jnp.sum(inner_got[...], axis=0) / width

        def normalize(src, carry):
            for j in range(2):
                grads, values = pieces(j, src)
                factor = wide(factor_v[pl.ds(j * seq + src, 1), :])
                inner = wide(inner_v[pl.ds(j * seq + src, 1), :])
                scaled = grads * gains_ref[j : j + 1, :]
                d_out[j, src] = (factor * (scaled - values * factor * factor * inner)).astype(BF)
            return carry

        lax.fori_loop(0, seq, normalize, 0)

    dma = pltpu.SemaphoreType.DMA
    hbm, vmem = pl.BlockSpec(memory_space=pl.ANY), pl.BlockSpec(memory_space=pltpu.VMEM)
    return pl.pallas_call(
        kernel,
        out_shape=[
            jax.ShapeDtypeStruct((3, seq, rows, cols), BF),
            jax.ShapeDtypeStruct((cols, width), BF),
            jax.ShapeDtypeStruct((8, cols), F32),
        ],
        in_specs=[hbm] + [vmem] * 12,
        out_specs=[vmem] * 3,
        scratch_shapes=[
            pltpu.VMEM((seq, rows, width), BF),
            pltpu.VMEM((num_seqs, length, cols), BF),
            pltpu.VMEM((2, num_seqs, length, cols), F32),
            pltpu.VMEM((length, HEAD_DIM), F32),
            pltpu.VMEM((length, HEAD_DIM), F32),
            pltpu.VMEM((cols, width), F32),
            pltpu.VMEM((2 * seq, rows), F32),
            pltpu.VMEM((2 * seq, rows), F32),
            pltpu.VMEM((seq, 2 * seq, rows), F32),
            dma,
            dma((seq,)),
            dma((seq,)),
        ]
        + gather_sems(seq, rows),
        compiler_params=pltpu.CompilerParams(
            collective_id=collective_id, has_side_effects=True, vmem_limit_bytes=VMEM_MOST
        ),
        name="attend_back",
        cost_estimate=cost_of(130),
    )(
        dz,
        proj_weight,
        o_head,
        query,
        key,
        value,
        raw,
        squares,
        gains,
        *tables,
        segments[:, :, None],
        segments[:, None, :],
    )


def dp_cuts(rows):
    pieces = max(n for n in (8, 4, 2, 1) if rows % (16 * n) == 0)
    return [(i * (rows // pieces), rows // pieces) for i in range(pieces)]


def last_sums(grads, normed, qkv_weight, proj_terms, router_terms, gain_heads, gain_ffn, gain_attn, collective_id):
    seq, ndp = lax.axis_size("seq"), lax.axis_size("dp")
    devices = seq * ndp
    _, _, rows, cols = grads.shape
    width = normed.shape[2]
    nz, ny = grid_of(seq)
    own_rows = proj_terms.shape[1]
    part_rows = 3 * own_rows
    n_router = router_terms.shape[1]
    per_block = 128 // own_rows
    n_seq = 10
    n_dp = 5
    block = 256

    def kernel(*refs):
        (d_ref, normed_ref, w_ref, proj_ref, router_ref, heads_ref, ffn_ref, gain_ref) = refs[:8]
        (o_ref, qkv_out, proj_out, sum_out) = refs[8:12]
        (terms_v, normed_v, qkv_v, qkv_sum, proj_v, proj_sum, packed_v, got, gains_v, normed_sem, proj_sem) = refs[12:23]
        rest = refs[23:]
        seq_scratch, rest = rest[:n_seq], rest[n_seq:]
        qkv_scratch, proj_scratch, rest = rest[:n_dp], rest[n_dp : 2 * n_dp], rest[2 * n_dp :]
        (part_send, part_recv, move_send, move_recv, small_send, small_recv, own_sem) = rest
        _, across, me, _ = seq_lines()
        x_line, core_line, dp, dp_flat = dp_lines()
        rank = dp * seq + me
        load_normed = pltpu.make_async_copy(normed_ref, normed_v, normed_sem)
        load_normed.start()
        load_proj = pltpu.make_async_copy(proj_ref, proj_v, proj_sem)
        load_proj.start()
        barrier = pltpu.get_barrier_semaphore()

        def device(peer):
            return (lax.div(peer, seq), lax.rem(peer, seq))

        def meet(step, carry):
            pl.semaphore_signal(
                barrier, 1, device_id=device(lax.rem(rank + step, devices)), device_id_type=MESH
            )
            return carry

        lax.fori_loop(1, devices, meet, 0)

        def normed_term(i, carry):
            dest = lax.rem(i, nz) * ny + lax.rem(across.place + 1 + lax.div(i, nz), ny)
            total = dot_rows(d_ref[0, dest], w_ref[0])
            for j in range(1, 3):
                total = total + dot_rows(d_ref[j, dest], w_ref[j])
            terms_v[dest] = total.astype(BF)
            return carry

        load_normed.wait()
        gains_v[...] = jnp.zeros_like(gains_v)
        for j in range(2):
            gains_v[1 + j : 2 + j, pl.ds(pl.multiple_of(me * cols, 128), cols)] = heads_ref[j : j + 1, :]
        gains_v[3:4, :] = ffn_ref[...]

        def weight_term(i, carry):
            at = pl.ds(pl.multiple_of(i * block, block), block)
            turned = normed_v[:, :, at].reshape(seq * rows, block).T
            gain = jnp.zeros((block, 1), F32)
            for j in range(3):
                term = jnp.dot(turned, d_ref[j].reshape(seq * rows, cols), preferred_element_type=F32)
                gain = gain + jnp.sum(term * w_ref[j, at, :].astype(F32), axis=1, keepdims=True)
                low = term.astype(BF)
                for piece in range(block // own_rows):
                    owner = i * (block // own_rows) + piece
                    spot = pl.multiple_of(lax.rem(owner, seq) * part_rows + j * own_rows, own_rows)
                    qkv_v[lax.div(owner, seq), pl.ds(spot, own_rows), :] = low[
                        piece * own_rows : (piece + 1) * own_rows
                    ]
            gains_v[0:1, at] = as_row(gain) / gain_ref[:, at]
            return carry

        blocks = width // block
        near = blocks // x_line.size

        def rotated(i, carry):
            return weight_term(lax.rem((x_line.place + 1) * near + i, blocks), carry)

        load_proj.wait()

        def over_dp(refs, out, buffers):
            return Reduce(
                core_line,
                x_line,
                dp,
                lambda core, x: dp_flat(x, core),
                dp_cuts(refs.shape[1]),
                refs,
                out,
                *buffers[0:2],
                buffers[2:5],
            )

        owners = [over_dp(qkv_v, qkv_sum, qkv_scratch), over_dp(proj_v, proj_sum, proj_scratch)]
        out_lists = [(list(owner.outward()), 2 * len(owner.cuts)) for owner in owners]
        in_lists = [(list(owner.inward()), len(owner.cuts)) for owner in owners]
        programs = seq_reduces(terms_v, o_ref, seq_scratch)

        lax.fori_loop(0, seq - nz, normed_term, 0)
        pl.semaphore_wait(barrier, devices - 1)
        for step in programs[0].outward():
            step()
        lax.fori_loop(0, blocks - near, rotated, 0)
        for steps, kept in out_lists:
            for step in steps[:-kept]:
                step()
        lax.fori_loop(seq - nz, seq, normed_term, 0)
        for step in programs[1].outward():
            step()
        for steps, kept in in_lists:
            for step in steps[:-kept]:
                step()
        inward = woven(*[p.inward() for p in programs])
        in_all = len(inward)

        def move_sums(share):
            while inward and in_all - len(inward) < share * in_all:
                inward.pop(0)()

        lax.fori_loop(blocks - near, blocks, rotated, 0)
        for steps, kept in out_lists:
            for step in steps[-kept:]:
                step()
        move_sums(0.25)
        packed_v[:, 0:n_router, :] = router_ref[...]
        for peer in range(devices):
            at = peer // per_block * 128
            packed_v[peer, n_router : n_router + 8, :] = gains_v[:, at : at + 128]

        def small(peer, origin):
            return send_to(
                packed_v.at[peer], got.at[origin], small_send.at[peer], small_recv.at[origin], device(peer)
            )

        def small_start(step, carry):
            small(lax.rem(rank + step, devices), rank).start()
            return carry

        lax.fori_loop(1, devices, small_start, 0)

        def part(peer, origin):
            return send_to(
                qkv_sum.at[pl.ds(pl.multiple_of(peer * part_rows, 16), part_rows)],
                qkv_out.at[origin],
                part_send.at[peer],
                part_recv.at[origin],
                (dp, peer),
            )

        own_part = pltpu.make_async_copy(
            qkv_sum.at[pl.ds(pl.multiple_of(me * part_rows, 16), part_rows)], qkv_out.at[me], own_sem.at[0]
        )
        goal = me * ndp + dp
        stays = goal == rank
        own_move = pltpu.make_async_copy(proj_sum, proj_out, own_sem.at[1])

        def move():
            return send_to(proj_sum, proj_out, move_send, move_recv, device(goal))

        move_sums(0.8)
        for steps, kept in in_lists:
            for step in steps[-kept:]:
                step()
        own_part.start()
        for step in range(1, seq):
            part(lax.rem(me + step, seq), me).start()
        pl.when(stays)(own_move.start)
        pl.when(jnp.logical_not(stays))(lambda: move().start())
        move_sums(1.0)

        got[rank] = packed_v[rank]

        def small_end(step, carry):
            small(lax.rem(rank + step, devices), rank).wait_send()
            source = lax.rem(rank + devices - step, devices)
            small(source, source).wait_recv()
            return carry

        lax.fori_loop(1, devices, small_end, 0)
        sum_out[...] = jnp.sum(got[...], axis=0)
        for program in (*programs, *owners):
            program.finish()
        for step in range(1, seq):
            part(lax.rem(me + step, seq), me).wait_send()
            source = lax.rem(me + seq - step, seq)
            part(source, source).wait_recv()
        own_part.wait()

        @pl.when(stays)
        def _():
            own_move.wait()

        @pl.when(jnp.logical_not(stays))
        def _():
            move().wait_send()
            move().wait_recv()

    dma = pltpu.SemaphoreType.DMA
    hbm, vmem = pl.BlockSpec(memory_space=pl.ANY), pl.BlockSpec(memory_space=pltpu.VMEM)
    return pl.pallas_call(
        kernel,
        out_shape=[
            jax.ShapeDtypeStruct((rows, width), F32),
            jax.ShapeDtypeStruct((seq, part_rows, cols), BF),
            jax.ShapeDtypeStruct((own_rows, width), BF),
            jax.ShapeDtypeStruct((n_router + 8, 128), F32),
        ],
        in_specs=[vmem, hbm, vmem, hbm] + [vmem] * 4,
        out_specs=[vmem] * 4,
        scratch_shapes=[
            pltpu.VMEM((seq, rows, width), BF),
            pltpu.VMEM((seq, rows, width), BF),
            pltpu.VMEM((ndp, seq * part_rows, cols), BF),
            pltpu.VMEM((seq * part_rows, cols), BF),
            pltpu.VMEM(proj_terms.shape, BF),
            pltpu.VMEM((own_rows, width), BF),
            pltpu.VMEM((devices, n_router + 8, 128), F32),
            pltpu.VMEM((devices, n_router + 8, 128), F32),
            pltpu.VMEM((8, width), F32),
            dma,
            dma,
        ]
        + reduce_scratch(seq, rows, width)
        + Reduce.scratch(dp_cuts(seq * part_rows), 2, ndp // 2, cols)
        + Reduce.scratch(dp_cuts(own_rows), 2, ndp // 2, width)
        + [dma((seq,)), dma((seq,)), dma, dma, dma((devices,)), dma((devices,)), dma((2,))],
        compiler_params=pltpu.CompilerParams(
            collective_id=collective_id, has_side_effects=True, vmem_limit_bytes=VMEM_MOST
        ),
        name="last_sums",
        cost_estimate=cost_of(110),
    )(grads, normed, qkv_weight, proj_terms, router_terms, gain_heads, gain_ffn, gain_attn)


def packed_rows(parts, sublanes):
    flat = jnp.concatenate(parts, axis=1)
    fill = -flat.shape[1] % (sublanes * 128)
    return jnp.pad(flat, ((0, 0), (0, fill))).reshape(flat.shape[0], -1, 128)


def slot_places(slots, capacity):
    rows, experts = slots.shape
    number = lax.broadcasted_iota(jnp.int32, (capacity, rows), 0).astype(F32)
    return [as_row(slots[:, e : e + 1]) == number for e in range(experts)]


def experts_dispatch(ffn_all, routes_all, router_full, me, experts, capacity):
    seq, rows, width = ffn_all.shape
    experts_all, top = router_full.shape[1], routes_all.shape[2]

    def kernel(me_ref, ffn_ref, routes_ref, router_ref, rows_out, gate_out, slot_out, col_out):
        first = me_ref[0] * experts
        logits = jnp.dot(ffn_ref[0], router_ref[...], preferred_element_type=F32)
        exps = jnp.exp(logits - jnp.max(logits, axis=-1, keepdims=True))
        probs = exps / jnp.sum(exps, axis=-1, keepdims=True)
        lane = lax.broadcasted_iota(jnp.int32, (rows, experts_all), 1)
        wide_lane = lax.broadcasted_iota(jnp.int32, (rows, 128), 1)
        hits, gates = jnp.zeros((rows, 128), F32), []
        for e in range(experts):
            hit = jnp.sum((routes_ref[0] == first + e).astype(F32), axis=1, keepdims=True)
            hits = jnp.where(wide_lane == e, hit, hits)
            gates.append(jnp.sum(jnp.where(lane == first + e, probs, 0.0), axis=1, keepdims=True))
        below = lax.broadcasted_iota(jnp.int32, (rows, rows), 0) > lax.broadcasted_iota(
            jnp.int32, (rows, rows), 1
        )
        earlier = jnp.dot(below.astype(BF), hits.astype(BF), preferred_element_type=F32)
        slots = jnp.where(hits > 0.0, earlier, float(rows + 1))[:, 0:experts]
        places = slot_places(slots, capacity)
        slot_out[0] = slots
        for e in range(experts):
            gate_out[e, 0] = jnp.sum(jnp.where(places[e], as_row(gates[e]), 0.0), axis=1, keepdims=True)
            col_out[0, :, e : e + 1] = gates[e]
        for e in range(experts):
            rows_out[e, 0] = jnp.dot(
                places[e].astype(BF), ffn_ref[0], preferred_element_type=F32
            ).astype(BF)

    def source(s, _):
        return (s, 0, 0)

    def slot(s, _):
        return (0, s, 0, 0)

    shaped = jax.ShapeDtypeStruct
    return pl.pallas_call(
        kernel,
        out_shape=[
            shaped((experts, seq, capacity, width), BF),
            shaped((experts, seq, capacity, 1), F32),
            shaped((seq, rows, experts), F32),
            shaped((seq, rows, experts), F32),
        ],
        grid_spec=pltpu.PrefetchScalarGridSpec(
            num_scalar_prefetch=1,
            grid=(seq,),
            in_specs=[
                pl.BlockSpec((1, rows, width), source),
                pl.BlockSpec((1, rows, top), source),
                pl.BlockSpec((width, experts_all), lambda s, _: (0, 0)),
            ],
            out_specs=[
                pl.BlockSpec((experts, 1, capacity, width), slot),
                pl.BlockSpec((experts, 1, capacity, 1), slot),
                pl.BlockSpec((1, rows, experts), source),
                pl.BlockSpec((1, rows, experts), source),
            ],
        ),
        compiler_params=pltpu.CompilerParams(vmem_limit_bytes=VMEM_MOST),
        name="experts_dispatch",
        cost_estimate=cost_of(12),
    )(me.reshape(1), ffn_all, routes_all, router_full)


EXPERT_STEP = 512


def server(now, places, thunks):
    per_step, steps = places
    spots = [min(per_step * steps - 1, int(per_step * steps * share)) for share, _ in thunks]

    def serve(point):
        for mark in sorted(set(spots)):
            if mark % per_step != point:
                continue
            group = [thunk for spot, (_, thunk) in zip(spots, thunks) if spot == mark]

            @pl.when(now == mark // per_step)
            def _():
                for thunk in group:
                    thunk()

    return serve


def experts_forward(rows, weight_in, weight_out, cot_rows, collective_id):
    experts, slots, width = rows.shape
    hidden_width = weight_out.shape[1]
    step = EXPERT_STEP
    steps = hidden_width // step
    seq = lax.axis_size("seq")
    part = cot_rows.shape[0]
    last = experts * steps - 1

    def kernel(rows_ref, in_ref, out_ref, c_ref, y_out, gate_out, up_out, hidden_out, c_out, acc, own_sem, *sems):
        f = pl.program_id(1)
        now = pl.program_id(0) * steps + f
        along, across, me, _ = seq_lines()
        gathers = seq_gathers(c_ref, c_out, sems)
        moves = sorted((s for p in gathers for s in p.steps()), key=lambda s: s[0])
        most = max(hops for hops, _ in moves)
        serve = server(now, (2, last + 1), [(0.1 + 0.85 * hops / most, thunk) for hops, thunk in moves])
        own = pltpu.make_async_copy(c_ref, c_out.at[me], own_sem)

        @pl.when(now == 0)
        def _():
            greet_lines(along, across)
            own.start()
            for program in gathers:
                program.start()

        gate = jnp.dot(rows_ref[0], in_ref[0, 0], preferred_element_type=F32)
        up = jnp.dot(rows_ref[0], in_ref[0, 1], preferred_element_type=F32)
        gate_out[0] = gate.astype(BF)
        up_out[0] = up.astype(BF)
        hidden = (gate / (1.0 + jnp.exp(-gate)) * up).astype(BF)
        hidden_out[0] = hidden
        serve(0)
        value = jnp.dot(hidden, out_ref[0], preferred_element_type=F32)

        @pl.when(f == 0)
        def _():
            acc[...] = value

        @pl.when(f > 0)
        def _():
            acc[...] += value

        @pl.when(f == steps - 1)
        def _():
            y_out[0] = acc[...].astype(BF)

        serve(1)

        @pl.when(now == last)
        def _():
            for program in gathers:
                program.finish()
            own.wait()

    shaped = jax.ShapeDtypeStruct
    hbm = pl.BlockSpec(memory_space=pl.ANY)
    by_expert = pl.BlockSpec((1, slots, width), lambda e, f: (e, 0, 0))
    hidden_block = pl.BlockSpec((1, slots, step), lambda e, f: (e, 0, f))
    return pl.pallas_call(
        kernel,
        grid=(experts, steps),
        out_shape=[
            shaped((experts, slots, width), BF),
            shaped((experts, slots, hidden_width), BF),
            shaped((experts, slots, hidden_width), BF),
            shaped((experts, slots, hidden_width), BF),
            shaped((seq, part, width), BF),
        ],
        in_specs=[
            by_expert,
            pl.BlockSpec((1, 2, width, step), lambda e, f: (e, 0, 0, f)),
            pl.BlockSpec((1, step, width), lambda e, f: (e, f, 0)),
            hbm,
        ],
        out_specs=[by_expert, hidden_block, hidden_block, hidden_block, hbm],
        scratch_shapes=[pltpu.VMEM((slots, width), F32), pltpu.SemaphoreType.DMA] + gather_sems(seq, part),
        compiler_params=pltpu.CompilerParams(
            collective_id=collective_id, has_side_effects=True, vmem_limit_bytes=VMEM_MOST
        ),
        name="experts_forward",
        cost_estimate=cost_of(65),
    )(rows, weight_in, weight_out, cot_rows)


def experts_mix(outputs, cot_first, cot_rest, gates, slot_cols, gate_cols):
    experts, slots, width = outputs.shape
    seq, rows, _ = slot_cols.shape
    capacity = slots // seq
    ahead = cot_first.shape[1]

    def kernel(y_ref, a_ref, b_ref, gate_ref, slot_ref, col_ref, mixed_out, dy_out, dprob_out, y_v, c_v):
        slot_cols = slot_ref[0]
        c_v[0:ahead, :] = a_ref[0]
        c_v[ahead:rows, :] = b_ref[0]
        number = lax.broadcasted_iota(jnp.int32, (rows, capacity), 1).astype(F32)
        places = slot_places(slot_cols, capacity)
        gated = []
        for e in range(experts):
            value = y_ref[e, 0]
            y_v[e * capacity : (e + 1) * capacity, :] = value
            gated.append(
                jnp.where(slot_cols[:, e : e + 1] == number, col_ref[0, :, e : e + 1], 0.0).astype(BF)
            )
            cot = jnp.dot(places[e].astype(BF), c_v[...], preferred_element_type=F32)
            dy_out[e, 0] = (cot * gate_ref[e, 0]).astype(BF)
            dgate = jnp.sum(cot * value.astype(F32), axis=1, keepdims=True)
            dprob_out[0, e : e + 1, :] = jnp.sum(jnp.where(places[e], dgate, 0.0), axis=0, keepdims=True)
        mixed_out[0] = jnp.dot(
            jnp.concatenate(gated, axis=1), y_v[...], preferred_element_type=F32
        ).astype(BF)

    def source(s):
        return (s, 0, 0)

    def slot(s):
        return (0, s, 0, 0)

    shaped = jax.ShapeDtypeStruct
    return pl.pallas_call(
        kernel,
        grid=(seq,),
        out_shape=[
            shaped((seq, rows, width), BF),
            shaped((experts, seq, capacity, width), BF),
            shaped((seq, experts, rows), F32),
        ],
        in_specs=[
            pl.BlockSpec((experts, 1, capacity, width), slot),
            pl.BlockSpec((1, ahead, width), source),
            pl.BlockSpec((1, rows - ahead, width), source),
            pl.BlockSpec((experts, 1, capacity, 1), slot),
            pl.BlockSpec((1, rows, experts), source),
            pl.BlockSpec((1, rows, experts), source),
        ],
        out_specs=[
            pl.BlockSpec((1, rows, width), source),
            pl.BlockSpec((experts, 1, capacity, width), slot),
            pl.BlockSpec((1, experts, rows), source),
        ],
        scratch_shapes=[pltpu.VMEM((experts * capacity, width), BF), pltpu.VMEM((rows, width), BF)],
        compiler_params=pltpu.CompilerParams(vmem_limit_bytes=VMEM_MOST),
        name="experts_mix",
        cost_estimate=cost_of(15),
    )(outputs.reshape(experts, seq, capacity, width), cot_first, cot_rest, gates, slot_cols, gate_cols)


def experts_out_terms(hidden, grads):
    experts, slots, width = grads.shape
    hidden_width = hidden.shape[2]
    step = hidden_width

    def kernel(hidden_ref, dy_ref, out_ref):
        out_ref[0] = lax.dot_general(
            hidden_ref[0], dy_ref[0], (((0,), (0,)), ((), ())), preferred_element_type=F32
        ).astype(BF)

    return pl.pallas_call(
        kernel,
        grid=(experts, hidden_width // step),
        out_shape=jax.ShapeDtypeStruct((experts, hidden_width, width), BF),
        in_specs=[
            pl.BlockSpec((1, slots, step), lambda e, f: (e, 0, f)),
            pl.BlockSpec((1, slots, width), lambda e, f: (e, 0, 0)),
        ],
        out_specs=pl.BlockSpec((1, step, width), lambda e, f: (e, f, 0)),
        compiler_params=pltpu.CompilerParams(vmem_limit_bytes=VMEM_MOST),
        name="experts_out_terms",
        cost_estimate=cost_of(15),
    )(hidden, grads)


def experts_back(rows, grads, gate_in, up_in, weight_in, weight_out, mixed_terms, collective_id):
    experts, slots, width = rows.shape
    hidden_width = weight_out.shape[1]
    step = EXPERT_STEP
    steps = hidden_width // step
    seq, tok, _ = mixed_terms.shape
    last = experts * steps - 1

    def kernel(
        rows_ref, dy_ref, gate_ref, up_ref, in_ref, out_ref, mixed_ref,
        drows_out, in_out, mixed_out,
        rows_t, mixed_v, load_sem, *scratch,
    ):
        f = pl.program_id(1)
        now = pl.program_id(0) * steps + f
        along, across, _, _ = seq_lines()
        reduces = seq_reduces(mixed_v, mixed_out, scratch)
        outward, late = (list(p.outward()) for p in reduces)
        early_in, late_in = (list(p.inward()) for p in reduces)
        nz = along.size
        rank = 2 * len(reduces[0].cuts)
        thunks = [(0.06 + 0.18 * i / len(late), thunk) for i, thunk in enumerate(late)]
        thunks += [(0.07 + (i // rank + 1) / nz, thunk) for i, thunk in enumerate(early_in)]
        thunks += [((i + 1.5) / (len(late_in) + 0.5), thunk) for i, thunk in enumerate(late_in)]
        serve = server(now, (4, last + 1), sorted(thunks, key=lambda t: t[0]))
        load = pltpu.make_async_copy(mixed_ref, mixed_v, load_sem)

        @pl.when(now == 0)
        def _():
            load.start()
            greet_lines(along, across)
            load.wait()
            for thunk in outward:
                thunk()

        @pl.when(f == 0)
        def _():
            rows_t[...] = rows_ref[0].T

        grad = dot_rows(dy_ref[0], out_ref[0])
        serve(0)
        gate, up = gate_ref[0].astype(F32), up_ref[0].astype(F32)
        sig = 1.0 / (1.0 + jnp.exp(-gate))
        silu = gate * sig
        dgate = (grad * up * sig * (1.0 + gate * (1.0 - sig))).astype(BF)
        dup = (grad * silu).astype(BF)
        in_out[0, 0] = jnp.dot(rows_t[...], dgate, preferred_element_type=F32).astype(BF)
        serve(1)
        in_out[0, 1] = jnp.dot(rows_t[...], dup, preferred_element_type=F32).astype(BF)
        serve(2)
        value = dot_rows(dgate, in_ref[0, 0]) + dot_rows(dup, in_ref[0, 1])

        @pl.when(f == 0)
        def _():
            drows_out[0] = value.astype(BF)

        @pl.when(f > 0)
        def _():
            drows_out[0] = (drows_out[0].astype(F32) + value).astype(BF)

        serve(3)

        @pl.when(now == last)
        def _():
            for program in reduces:
                program.finish()

    shaped = jax.ShapeDtypeStruct
    hbm = pl.BlockSpec(memory_space=pl.ANY)
    by_expert = pl.BlockSpec((1, slots, width), lambda e, f: (e, 0, 0))
    once = pl.BlockSpec((1, slots, width), lambda e, f: (e, 0, 0), pipeline_mode=pl.Buffered(1))
    hidden_block = pl.BlockSpec((1, slots, step), lambda e, f: (e, 0, f))
    in_block = pl.BlockSpec((1, 2, width, step), lambda e, f: (e, 0, 0, f))
    out_block = pl.BlockSpec((1, step, width), lambda e, f: (e, f, 0))
    return pl.pallas_call(
        kernel,
        grid=(experts, steps),
        out_shape=[
            shaped((experts, slots, width), BF),
            shaped((experts, 2, width, hidden_width), BF),
            shaped((tok, width), F32),
        ],
        in_specs=[once, once, hidden_block, hidden_block, in_block, out_block, hbm],
        out_specs=[by_expert, in_block, pl.BlockSpec(memory_space=pltpu.VMEM)],
        scratch_shapes=[
            pltpu.VMEM((width, slots), BF),
            pltpu.VMEM((seq, tok, width), BF),
            pltpu.SemaphoreType.DMA,
        ]
        + reduce_scratch(seq, tok, width),
        compiler_params=pltpu.CompilerParams(
            collective_id=collective_id, has_side_effects=True, vmem_limit_bytes=VMEM_MOST
        ),
        name="experts_back",
        cost_estimate=cost_of(95),
    )(rows, grads, gate_in, up_in, weight_in, weight_out, mixed_terms)


def rows_back(drows, slot_cols, prob_grads, collective_id):
    seq, rows, experts = slot_cols.shape
    width = drows.shape[-1]
    capacity = drows.shape[1] // seq
    nz, ny = grid_of(seq)

    def kernel(d_ref, slot_ref, prob_ref, o_ref, prob_out, terms_v, d_v, prob_send, prob_recv, *scratch):
        dp = lax.axis_index("dp")
        _, across, me, _ = seq_lines()
        barrier = pltpu.get_barrier_semaphore()
        for step in range(1, seq):
            pl.semaphore_signal(
                barrier, 1, device_id=(dp, lax.rem(me + step, seq)), device_id_type=MESH
            )
        number = lax.broadcasted_iota(jnp.int32, (rows, capacity), 1).astype(F32)

        def term(i, carry):
            dest = lax.rem(i, nz) * ny + lax.rem(across.place + 1 + lax.div(i, nz), ny)
            places = []
            for e in range(experts):
                d_v[e * capacity : (e + 1) * capacity, :] = d_ref[e, dest]
                places.append((slot_ref[dest, :, e : e + 1] == number).astype(BF))
            terms_v[dest] = jnp.dot(
                jnp.concatenate(places, axis=1), d_v[...], preferred_element_type=F32
            ).astype(BF)
            return carry

        def prob_copy(peer, origin):
            return send_to(
                prob_ref.at[peer], prob_out.at[origin], prob_send.at[peer], prob_recv.at[origin], (dp, peer)
            )

        reduces = seq_reduces(terms_v, o_ref, scratch)
        lax.fori_loop(0, seq - nz, term, 0)
        pl.semaphore_wait(barrier, seq - 1)
        for step in range(1, seq):
            prob_copy(lax.rem(me + step, seq), me).start()
        for thunk in reduces[0].outward():
            thunk()
        lax.fori_loop(seq - nz, seq, term, 0)
        for thunk in reduces[1].outward():
            thunk()
        prob_out[me] = prob_ref[me]
        for thunk in woven(*[p.inward() for p in reduces]):
            thunk()
        for program in reduces:
            program.finish()
        for step in range(1, seq):
            prob_copy(lax.rem(me + step, seq), me).wait_send()
            source = lax.rem(me + seq - step, seq)
            prob_copy(source, source).wait_recv()

    vmem = pl.BlockSpec(memory_space=pltpu.VMEM)
    dma = pltpu.SemaphoreType.DMA
    return pl.pallas_call(
        kernel,
        out_shape=[
            jax.ShapeDtypeStruct((rows, width), F32),
            jax.ShapeDtypeStruct(prob_grads.shape, F32),
        ],
        in_specs=[vmem] * 3,
        out_specs=[vmem] * 2,
        scratch_shapes=[
            pltpu.VMEM((seq, rows, width), BF),
            pltpu.VMEM((experts * capacity, width), BF),
            dma((seq,)),
            dma((seq,)),
        ]
        + reduce_scratch(seq, rows, width),
        compiler_params=pltpu.CompilerParams(
            collective_id=collective_id, has_side_effects=True, vmem_limit_bytes=VMEM_MOST
        ),
        name="rows_back",
        cost_estimate=cost_of(90),
    )(drows.reshape(experts, seq, capacity, width), slot_cols, prob_grads)


def rms_factor(values):
    return lax.rsqrt(jnp.mean(values * values, axis=-1, keepdims=True) + NORM_EPS)


def norm_back(values, factor, gain_row, incoming):
    scaled = incoming * gain_row
    gain_part = jnp.sum(incoming * values * factor, axis=0)
    inner = jnp.mean(scaled * values, axis=-1, keepdims=True)
    return (factor * (scaled - values * factor * factor * inner), gain_part)


def local(
    tokens,
    segments,
    routes,
    cotangent,
    attn_weight,
    router_weight,
    norm_gains,
    expert_in,
    expert_out,
):
    num_seqs, local_len, width = tokens.shape
    seq_length = segments.shape[1]
    seq, ndp = lax.axis_size("seq"), lax.axis_size("dp")
    me = lax.axis_index("seq")
    devices = seq * ndp
    cols = HEADS // seq * HEAD_DIM
    tok = num_seqs * local_len
    group = tok * seq
    own_rows = attn_weight.shape[0]
    experts_all = router_weight.shape[1]
    experts = experts_all // seq
    top = routes.shape[-1]
    capacity = (9 * tok * top + 8 * experts_all - 1) // (8 * experts_all)

    n_router = own_rows * experts_all
    token_rows, cot_low = tokens.reshape(tok, width), cotangent.reshape(tok, width)
    (router_rows,) = (packed_rows([router_weight.reshape(1, -1)], 16)[0],)
    rank = lax.axis_index("dp") * seq + me
    gain_rows_own = lax.dynamic_update_slice(
        jnp.zeros((16, 128), BF), norm_gains, (0, lax.rem(rank, 128 // own_rows) * own_rows)
    )
    tables = rotary_tables(seq_length)
    ahead = tok * 10 // 256 * 16
    normed_all, cot_all, qkv_weight, proj_got, small_all, routes_all, raw, query_head, key_head, value_head, o_head, sums = (
        attend_first(
            token_rows,
            cot_low[:ahead],
            attn_weight[:, :3].reshape(own_rows, 3, seq, cols).transpose(2, 1, 0, 3),
            attn_weight[:, 3],
            jnp.concatenate([router_rows, gain_rows_own], axis=0),
            routes.reshape(-1, 128),
            tables,
            segments,
            router_rows.shape[0],
            1,
        )
    )
    in_full = lax.all_gather(expert_in, "dp", axis=1, tiled=True)
    out_full = lax.all_gather(expert_out, "dp", axis=2, tiled=True)
    router_full = (
        small_all[:, : router_rows.shape[0]].reshape(devices, -1)[:, :n_router].reshape(width, experts_all)
    )
    gain_rows = (
        jnp.sum(
            small_all[:, router_rows.shape[0] : router_rows.shape[0] + 4]
            .reshape(width // 128, 128 // own_rows, 4, 128)
            .astype(F32),
            axis=1,
        )
        .transpose(1, 0, 2)
        .reshape(4, width)
    )
    routes_all = routes_all.reshape(seq, tok, top)
    proj_weight = proj_got.reshape(cols, width)
    resid_in = token_rows.astype(F32)
    factor_attn = rms_factor(resid_in)
    middle, ffn_low, ffn_all = middle_rows(o_head, proj_weight, token_rows, gain_rows[3:4], 5)
    factor_ffn = rms_factor(middle)

    slots = seq * capacity
    in_weight = in_full.transpose(0, 2, 1, 3)
    rows, gates, slot_cols, gate_cols = experts_dispatch(
        ffn_all, routes_all, router_full, me, experts, capacity
    )
    rows = rows.reshape(experts, slots, width)
    outputs, gate_in, up_in, hidden, cot_rest = experts_forward(rows, in_weight, out_full, cot_low[ahead:], 7)
    mixed_terms, output_grads, prob_grads = experts_mix(
        outputs, cot_all, cot_rest, gates, slot_cols, gate_cols
    )
    output_grads = output_grads.reshape(experts, slots, width)
    out_term = experts_out_terms(hidden, output_grads)
    expert_out_grad = lax.psum_scatter(out_term, "dp", scatter_dimension=2, tiled=True).astype(F32)
    out_term, output_grads = lax.optimization_barrier((out_term, output_grads))
    drows, in_term, mixed = experts_back(
        rows,
        output_grads,
        gate_in,
        up_in,
        in_weight,
        out_full,
        mixed_terms,
        8,
    )
    block_out = (middle + mixed).astype(BF).reshape(num_seqs, local_len, width)
    expert_in_grad = lax.psum_scatter(
        in_term.transpose(0, 2, 1, 3), "dp", scatter_dimension=1, tiled=True
    ).astype(F32)
    grad_ffn, grad_prob = rows_back(drows, slot_cols, prob_grads, 9)
    grad_prob = grad_prob.reshape(experts_all, tok).T

    route_probs = jax.nn.softmax(
        jnp.dot(ffn_low, router_full, preferred_element_type=F32), axis=-1
    )
    grad_logits = (
        route_probs * (grad_prob - jnp.sum(route_probs * grad_prob, axis=-1, keepdims=True))
    ).astype(BF)
    router_term = jnp.einsum("td,te->de", ffn_low, grad_logits, preferred_element_type=F32)
    grad_ffn = grad_ffn + jnp.einsum(
        "te,de->td", grad_logits, router_full, preferred_element_type=F32
    )
    grad_middle, gain_ffn = norm_back(middle, factor_ffn, gain_rows[3], grad_ffn)
    grad_middle = grad_middle + cot_low.astype(F32)

    head_gains = jnp.pad(lax.dynamic_slice(gain_rows, (1, me * cols), (2, cols)), ((0, 6), (0, 0)))
    grad_heads, proj_term, gain_heads = attend_back(
        grad_middle.astype(BF),
        proj_weight,
        o_head,
        query_head,
        key_head,
        value_head,
        raw,
        sums,
        head_gains,
        tables,
        segments,
        11,
    )

    grad_normed, qkv_out, proj_grad, total = last_sums(
        grad_heads,
        normed_all,
        qkv_weight,
        proj_term.reshape(ndp, own_rows, width),
        packed_rows([router_term.reshape(devices, -1)], 8),
        gain_heads,
        gain_ffn[None],
        gain_rows[0:1],
        14,
    )
    grad_resid, _ = norm_back(resid_in, factor_attn, gain_rows[0], grad_normed)
    input_grad = (grad_resid + grad_middle).reshape(num_seqs, local_len, width)
    qkv_grad = qkv_out.reshape(seq, 3, own_rows, cols).transpose(2, 1, 0, 3).reshape(own_rows, 3, width)
    attn_grad = jnp.concatenate([qkv_grad, proj_grad[:, None, :]], axis=1).astype(F32)
    gain_at = total.shape[0] - 8
    router_grad = total[:gain_at].reshape(-1)[:n_router].reshape(own_rows, experts_all)
    gain_grad = lax.dynamic_slice(
        total, (gain_at, lax.rem(rank, 128 // own_rows) * own_rows), (4, own_rows)
    )
    return (
        block_out,
        input_grad,
        attn_grad,
        router_grad,
        gain_grad,
        expert_in_grad,
        expert_out_grad,
    )


def solution(mesh):
    in_specs = (
        P("dp", "seq", None),
        P("dp", None),
        P("dp", "seq", None),
        P("dp", "seq", None),
        P(("dp", "seq"), None, None),
        P(("dp", "seq"), None),
        P(None, ("dp", "seq")),
        P("seq", "dp", None, None),
        P("seq", None, "dp"),
    )
    out_specs = (
        P("dp", "seq", None),
        P("dp", "seq", None),
        P(("dp", "seq"), None, None),
        P(("dp", "seq"), None),
        P(None, ("dp", "seq")),
        P("seq", "dp", None, None),
        P("seq", None, "dp"),
    )
    return jax.shard_map(local, mesh=mesh, in_specs=in_specs, out_specs=out_specs, check_vma=False)
```

```python
import math

import jax
import jax.numpy as jnp
from jax import lax
from jax.experimental import pallas as pl
from jax.experimental.pallas import tpu as pltpu
from jax.sharding import PartitionSpec as P

HEADS = 16
HEAD_DIM = 128
NORM_EPS = 1e-05
ROPE_BASE = 10000.0
MASKED_SCORE = -1e30
BF = jnp.bfloat16
F32 = jnp.float32
MESH = pl.DeviceIdType.MESH
VMEM_MOST = 60 << 20


class Line:
    def __init__(self, size, place, device):
        self.size, self.place, self.device = size, place, device

    def has(self, turn):
        return self.place < self.size - 1 if turn > 0 else self.place > 0

    def inside(self, place):
        return (place >= 0) & (place < self.size)


def grid_of(seq_size):
    lines = 4 if seq_size % 4 == 0 else 1
    return lines, seq_size // lines


def seq_lines():
    dp, me = lax.axis_index("dp"), lax.axis_index("seq")
    nz, ny = grid_of(lax.axis_size("seq"))
    along = Line(nz, lax.div(me, ny), lambda turn: (dp, me + turn * ny))
    across = Line(ny, lax.rem(me, ny), lambda turn: (dp, me + turn))
    return along, across, me, lambda z, y: z * ny + y


def dp_lines():
    dp, me = lax.axis_index("dp"), lax.axis_index("seq")
    along = Line(lax.axis_size("dp") // 2, lax.div(dp, 2), lambda turn: (dp + 2 * turn, me))
    across = Line(2, lax.rem(dp, 2), lambda turn: (dp + turn, me))
    return along, across, dp, lambda x, core: 2 * x + core


def cost_of(microseconds):
    return pl.CostEstimate(flops=0, bytes_accessed=microseconds * 3_600_000, transcendentals=0)


def send_to(src, dst, send_sem, recv_sem, device):
    return pltpu.make_async_remote_copy(
        src_ref=src,
        dst_ref=dst,
        send_sem=send_sem,
        recv_sem=recv_sem,
        device_id=device,
        device_id_type=MESH,
    )


def greet(targets):
    barrier = pltpu.get_barrier_semaphore()
    count = 0
    for cond, device in targets:

        @pl.when(cond)
        def _(device=device):
            pl.semaphore_signal(barrier, 1, device_id=device, device_id_type=MESH)

        count = count + cond.astype(jnp.int32)
    pl.semaphore_wait(barrier, count)


def greet_lines(*lines):
    greet([(line.has(turn), line.device(turn)) for line in lines for turn in (1, -1)])


def cuts_of(rows, ny):
    unit = rows // 16
    late = max(1, unit * 3 // 16) if ny == 2 else unit // 2
    early = unit - late
    half = (early + 1) // 2
    firsts = [(0, half * 16)] + ([(half * 16, (early - half) * 16)] if early > half else [])
    return firsts, [(early * 16, late * 16)]


class Gather:
    def __init__(self, first, second, me, flat, pieces, own, slot, send_sem, recv_sem, ready=None):
        self.first, self.second, self.me, self.flat = first, second, me, flat
        self.pieces, self.own, self.slot = pieces, own, slot
        self.send_sem, self.recv_sem, self.ready = send_sem, recv_sem, ready
        self.opening = [
            (line.has(turn), h, line, turn)
            for h in range(pieces)
            for line in (first, second)
            for turn in (1, -1)
        ]
        self.sent = [(ok, me, h, line, turn) for ok, h, line, turn in self.opening]

    def _source(self, origin, h):
        return self.own(h) if origin is self.me else self.slot(origin, h)

    def _copy(self, origin, h, line, turn):
        way = (0 if line is self.first else 2) + (turn > 0)
        return send_to(
            self._source(origin, h),
            self.slot(origin, h),
            self.send_sem.at[origin, h, way],
            self.recv_sem.at[origin, h],
            line.device(turn),
        )

    def start(self):
        for h in range(self.pieces):
            if self.ready is not None:
                self.ready(h)
            for ok, piece, line, turn in self.opening:
                if piece == h:
                    pl.when(ok)(lambda: self._copy(self.me, h, line, turn).start())

    def _arrival(self, place, side, h, sends):
        first, second = self.first, self.second
        cond = first.inside(place) & second.inside(side)
        origin = lax.select(cond, self.flat(place, side), self.me)
        onward = [(cond & line.has(turn), origin, h, line, turn) for line, turn in sends]
        self.sent += onward

        def thunk():
            @pl.when(cond)
            def _():
                self._copy(origin, h, first, 1).wait_recv()

            for ok, *way in onward:
                pl.when(ok)(lambda: self._copy(*way).start())

        return thunk

    def steps(self):
        first, second = self.first, self.second
        listed = []
        for far in range(1, first.size):
            for h in range(self.pieces):
                for sign in (1, -1):
                    listed.append(
                        (
                            far,
                            self._arrival(
                                first.place - sign * far,
                                second.place,
                                h,
                                [(first, sign), (second, 1), (second, -1)],
                            ),
                        )
                    )
        for step in range(1, second.size):
            for far in range(first.size):
                for h in range(self.pieces):
                    for sign in (1, -1) if far else (1,):
                        for turn in (1, -1):
                            listed.append(
                                (
                                    far + step + 0.5,
                                    self._arrival(
                                        first.place - sign * far,
                                        second.place - turn * step,
                                        h,
                                        [(second, turn)] if step < second.size - 1 else [],
                                    ),
                                )
                            )
        return listed

    def finish(self):
        for ok, *way in self.sent:
            pl.when(ok)(lambda: self._copy(*way).wait_send())


def run_steps(*programs):
    for _, step in sorted((s for p in programs for s in p.steps()), key=lambda s: s[0]):
        step()


def seq_gathers(block_ref, out_ref, sems):
    along, across, me, flat = seq_lines()
    early, late = cuts_of(block_ref.shape[0], across.size)
    made = []
    for cuts, first, second, index, (send_sem, recv_sem) in (
        (early, along, across, flat, sems[0:2]),
        (late, across, along, lambda y, z: flat(z, y), sems[2:4]),
    ):
        made.append(
            Gather(
                first,
                second,
                me,
                index,
                len(cuts),
                lambda h, cuts=cuts: block_ref.at[pl.ds(*cuts[h])],
                lambda origin, h, cuts=cuts: out_ref.at[origin, pl.ds(*cuts[h])],
                send_sem,
                recv_sem,
            )
        )
    return made


def gather_sems(seq, rows):
    early, late = cuts_of(rows, grid_of(seq)[1])
    return [
        pltpu.SemaphoreType.DMA((seq, len(early), 4)),
        pltpu.SemaphoreType.DMA((seq, len(early))),
        pltpu.SemaphoreType.DMA((seq, len(late), 4)),
        pltpu.SemaphoreType.DMA((seq, len(late))),
    ]


def seq_gather(block, collective_id):
    rows, width = block.shape
    seq = lax.axis_size("seq")

    def kernel(x_ref, o_ref, local_sem, *sems):
        along, across, me, _ = seq_lines()
        greet_lines(along, across)
        own = pltpu.make_async_copy(x_ref, o_ref.at[me], local_sem)
        own.start()
        programs = seq_gathers(x_ref, o_ref, sems)
        for program in programs:
            program.start()
        run_steps(*programs)
        for program in programs:
            program.finish()
        own.wait()

    return pl.pallas_call(
        kernel,
        out_shape=jax.ShapeDtypeStruct((seq, rows, width), block.dtype),
        in_specs=[pl.BlockSpec(memory_space=pl.ANY)],
        out_specs=pl.BlockSpec(memory_space=pl.ANY),
        scratch_shapes=[pltpu.SemaphoreType.DMA] + gather_sems(seq, rows),
        compiler_params=pltpu.CompilerParams(collective_id=collective_id, has_side_effects=True),
        name="seq_gather",
        cost_estimate=cost_of(80),
    )(block)


class Reduce:
    def __init__(self, first, second, me, flat, cuts, terms, out, from_first, from_second, sems):
        self.first, self.second, self.me, self.flat, self.cuts = first, second, me, flat, cuts
        self.terms, self.out = terms, out
        self.from_first, self.from_second = from_first, from_second
        self.send_sem, self.first_sem, self.second_sem = sems
        self.base = cuts[0][0]
        self.sent = []

    @staticmethod
    def scratch(rows_of, first_size, second_size, width):
        seq, rows, pieces = first_size * second_size, sum(r for _, r in rows_of), len(rows_of)
        lanes = 1 if first_size == 2 else 2
        return [
            pltpu.VMEM((lanes, second_size if first_size == 2 else seq, rows, width), BF),
            pltpu.VMEM((2, max(1, second_size - 1), rows, width), BF),
            pltpu.SemaphoreType.DMA((seq, pieces)),
            pltpu.SemaphoreType.DMA((lanes, seq, pieces)),
            pltpu.SemaphoreType.DMA((2, second_size, pieces)),
        ]

    def _lane(self, turn):
        return 0 if self.first.size == 2 or turn > 0 else 1

    def _held(self, dest, spot):
        return spot if self.first.size == 2 else dest

    def _passed(self, spot, side):
        return lax.max(spot - 1, 0) if side == 0 else lax.min(spot, max(0, self.second.size - 2))

    def _cut(self, h):
        return pl.ds(*self.cuts[h])

    def _inner(self, h):
        return pl.ds(self.cuts[h][0] - self.base, self.cuts[h][1])

    def _copy(self, dest, spot, h, line, turn):
        if line is self.first:
            lane = self._lane(turn)
            held = self._held(dest, spot)
            dst, sem = self.from_first.at[lane, held, self._inner(h)], self.first_sem.at[lane, dest, h]
        else:
            side = 0 if turn > 0 else 1
            dst = self.from_second.at[side, self._passed(spot, side), self._inner(h)]
            sem = self.second_sem.at[side, spot, h]
        return send_to(
            self.terms.at[dest, self._cut(h)], dst, self.send_sem.at[dest, h], sem, line.device(turn)
        )

    def _send(self, ok, *way):
        pl.when(ok)(lambda: self._copy(*way).start())

    def _add(self, cond, whole, parts, out, h):
        first, count = self.cuts[h]

        @pl.when(cond)
        def _():
            def body(i, carry):
                at = pl.ds(pl.multiple_of(first + i * 16, 16), 16)
                inner = pl.ds(pl.multiple_of(first - self.base + i * 16, 16), 16)
                total = None
                for ref in whole:
                    total = ref[at, :].astype(F32) if total is None else total + ref[at, :].astype(F32)
                for ref in parts:
                    total = total + ref[inner, :].astype(F32)
                out[at, :] = total.astype(out.dtype)
                return carry

            lax.fori_loop(0, count // 16, body, 0)

    def _spread(self):
        for far in range(self.second.size - 1, -1, -1):
            for sign in (1, -1) if far else (1,):
                spot = self.second.place + sign * far
                yield far, sign, spot, self.second.inside(spot)

    def outward(self):
        first = self.first
        for step in range(first.size - 1, 0, -1):
            for far, sign, spot, ok in self._spread():
                for h in range(len(self.cuts)):
                    for turn in (1, -1):
                        goal = first.place + turn * step
                        go = ok & first.inside(goal)
                        dest = lax.select(go, self.flat(goal, spot), self.me)
                        way = (dest, spot, h, first, turn)
                        self.sent.append((go, *way))
                        yield lambda go=go, way=way: self._pass_on(go, *way)

    def _pass_on(self, go, dest, spot, h, first, turn):
        if first.size > 2:
            behind = go & first.has(-turn)
            self._await(behind, dest, spot, h, first, turn)
            self._add(behind, [self.terms.at[dest]], [self.from_first.at[self._lane(turn), dest]], self.terms.at[dest], h)
        self._send(go, dest, spot, h, first, turn)

    def _await(self, cond, dest, spot, h, line, turn):
        @pl.when(cond)
        def _():
            self._copy(dest, spot, h, line, turn).wait_recv()

    def inward(self):
        for far, sign, spot, ok in self._spread():
            dest = lax.select(ok, self.flat(self.first.place, spot), self.me)
            for h in range(len(self.cuts)):
                if far:
                    self.sent.append((ok, dest, spot, h, self.second, sign))
                yield lambda a=(far, sign, spot, ok, dest, h): self._collect(*a)

    def _collect(self, far, sign, spot, ok, dest, h):
        first, second, acc = self.first, self.second, self.terms
        for turn in (1, -1):
            self._await(ok & first.has(-turn), dest, spot, h, first, turn)
        if first.size == 2:
            self._add(ok, [self.terms.at[dest]], [self.from_first.at[0, spot]], acc.at[dest], h)
        else:
            low, high = first.has(-1), first.has(1)
            lows, highs = self.from_first.at[self._lane(1), dest], self.from_first.at[self._lane(-1), dest]
            self._add(ok & low & high, [self.terms.at[dest]], [lows, highs], acc.at[dest], h)
            self._add(ok & low & jnp.logical_not(high), [self.terms.at[dest]], [lows], acc.at[dest], h)
            self._add(ok & high & jnp.logical_not(low), [self.terms.at[dest]], [highs], acc.at[dest], h)
        if far:
            behind = second.has(-sign)
            side = 0 if sign > 0 else 1
            self._await(ok & behind, dest, spot, h, second, sign)
            self._add(
                ok & behind, [acc.at[dest]], [self.from_second.at[side, self._passed(spot, side)]], acc.at[dest], h
            )
            self._send(ok, dest, spot, h, second, sign)
            return
        low, high = second.has(-1), second.has(1)
        self._await(low, dest, spot, h, second, 1)
        self._await(high, dest, spot, h, second, -1)
        lows = self.from_second.at[0, self._passed(spot, 0)]
        highs = self.from_second.at[1, self._passed(spot, 1)]
        self._add(low & high, [acc.at[dest]], [lows, highs], self.out, h)
        self._add(low & jnp.logical_not(high), [acc.at[dest]], [lows], self.out, h)
        self._add(high & jnp.logical_not(low), [acc.at[dest]], [highs], self.out, h)

    def finish(self):
        for ok, *way in self.sent:
            pl.when(ok)(lambda: self._copy(*way).wait_send())


def woven(*lists):
    keyed = [((i + 1) / len(entries), n, entry) for n, entries in enumerate(map(list, lists)) for i, entry in enumerate(entries)]
    return [entry for _, _, entry in sorted(keyed, key=lambda k: k[:2])]


def seq_reduces(terms, out, scratch):
    along, across, me, flat = seq_lines()
    early, late = cuts_of(terms.shape[1], across.size)
    return [
        Reduce(across, along, me, lambda y, z: flat(z, y), early, terms, out, *scratch[0:2], scratch[2:5]),
        Reduce(along, across, me, flat, late, terms, out, *scratch[5:7], scratch[7:10]),
    ]


def reduce_scratch(seq, rows, width):
    nz, ny = grid_of(seq)
    early, late = cuts_of(rows, ny)
    return Reduce.scratch(early, ny, nz, width) + Reduce.scratch(late, nz, ny, width)


def seq_reduce(terms, collective_id):
    seq, rows, width = terms.shape

    def kernel(p_ref, o_ref, sums, load_sem, *scratch):
        load = pltpu.make_async_copy(p_ref, sums, load_sem)
        load.start()
        along, across, _, _ = seq_lines()
        greet_lines(along, across)
        programs = seq_reduces(sums, o_ref, scratch)
        load.wait()
        for step in woven(*[p.outward() for p in programs]):
            step()
        for step in woven(*[p.inward() for p in programs]):
            step()
        for program in programs:
            program.finish()

    return pl.pallas_call(
        kernel,
        out_shape=jax.ShapeDtypeStruct((rows, width), F32),
        in_specs=[pl.BlockSpec(memory_space=pl.ANY)],
        out_specs=pl.BlockSpec(memory_space=pltpu.VMEM),
        scratch_shapes=[pltpu.VMEM((seq, rows, width), BF), pltpu.SemaphoreType.DMA] + reduce_scratch(seq, rows, width),
        compiler_params=pltpu.CompilerParams(
            collective_id=collective_id, has_side_effects=True, vmem_limit_bytes=VMEM_MOST
        ),
        name="seq_reduce",
        cost_estimate=cost_of(80),
    )(terms)


def rotary_tables(length):
    half_dim = HEAD_DIM // 2
    freqs = jnp.exp(-math.log(ROPE_BASE) * (2.0 * jnp.arange(half_dim, dtype=F32) / HEAD_DIM))
    angles = jnp.arange(length, dtype=jnp.int32).astype(F32)[:, None] * freqs[None, :]
    cosine, sine = jnp.cos(angles), jnp.sin(angles)
    return jnp.concatenate([cosine, cosine], axis=1), jnp.concatenate([-sine, sine], axis=1)


def turn_heads(values, cosine, sine):
    return values * cosine + pltpu.roll(values, HEAD_DIM // 2, 1) * sine


def as_columns(row):
    return jnp.broadcast_to(row, (128, row.shape[1])).T


def as_row(column):
    return jnp.broadcast_to(column, (column.shape[0], 128)).T[0:1]


def dot_rows(a, b):
    return lax.dot_general(a, b, (((1,), (1,)), ((), ())), preferred_element_type=F32)


def attend_first(tokens, cotangent, qkv_rows, proj_rows, packed, routes, tables, segments, n_router, collective_id):
    seq, ndp = lax.axis_size("seq"), lax.axis_size("dp")
    devices = seq * ndp
    rows, width = tokens.shape
    _, _, own_rows, cols = qkv_rows.shape
    num_seqs, length = segments.shape
    local_len = length // seq
    heads_here = cols // HEAD_DIM
    tile = 256
    per_block = 128 // own_rows
    ahead = cotangent.shape[0]

    def kernel(*refs):
        (x_ref, c_ref, qkv_ref, proj_ref, packed_ref, routes_ref, cos_ref, sin_ref, col_ref, row_ref) = refs[:10]
        (normed_out, c_out, w_v, proj_out, packed_out, routes_out) = refs[10:16]
        (raw_out, q_out, k_out, v_out, o_out, total_out) = refs[16:22]
        (x_v, normed_v, gains_v, sums_v, sums_got, local_sem, normed_sem) = refs[22:29]
        (part_send, part_recv, own_sem, qkv_send, qkv_recv, proj_send, proj_recv, proj_fwd) = refs[29:37]
        (small_send, small_recv, routes_send, routes_recv, sums_send, sums_recv) = refs[37:43]
        x_sems, c_sems = refs[43:47], refs[47:51]
        along, across, me, _ = seq_lines()
        x_line, core_line, dp, dp_flat = dp_lines()
        rank = dp * seq + me
        barrier = pltpu.get_barrier_semaphore()

        def device(peer):
            return (lax.div(peer, seq), lax.rem(peer, seq))

        def meet(step, carry):
            pl.semaphore_signal(
                barrier, 1, device_id=device(lax.rem(rank + step, devices)), device_id_type=MESH
            )
            return carry

        lax.fori_loop(1, devices, meet, 0)
        pl.semaphore_wait(barrier, devices - 1)

        def weight_rows(origin, h):
            return w_v.at[:, pl.ds(pl.multiple_of((origin * seq + h) * own_rows, own_rows), own_rows), :]

        own_x = pltpu.make_async_copy(x_ref, x_v.at[me], local_sem.at[0])
        own_c = pltpu.make_async_copy(c_ref, c_out.at[me], local_sem.at[2])
        own_qkv = pltpu.make_async_copy(qkv_ref.at[me], weight_rows(dp, me), own_sem)
        own_x.start()
        own_qkv.start()

        def part(peer, origin):
            return send_to(
                qkv_ref.at[peer], weight_rows(dp, origin), part_send.at[peer], part_recv.at[origin], (dp, peer)
            )

        for step in range(1, seq):
            part(lax.rem(me + step, seq), me).start()

        def small(peer, origin):
            return send_to(
                packed_ref, packed_out.at[origin], small_send.at[peer], small_recv.at[origin], device(peer)
            )

        def small_start(step, carry):
            small(lax.rem(rank + step, devices), rank).start()
            return carry

        lax.fori_loop(1, devices, small_start, 0)

        goal = lax.div(rank, ndp)
        place = lax.rem(rank, ndp)

        def proj_first(slot):
            return send_to(proj_ref, proj_out.at[slot], proj_send, proj_recv.at[slot], (dp, goal))

        stays = goal == me
        own_proj = pltpu.make_async_copy(proj_ref, proj_out.at[place], local_sem.at[1])
        pl.when(stays)(own_proj.start)
        pl.when(jnp.logical_not(stays))(lambda: proj_first(place).start())

        def route(peer, origin):
            return send_to(
                routes_ref, routes_out.at[origin], routes_send.at[peer], routes_recv.at[origin], (dp, peer)
            )

        for step in range(1, seq):
            route(lax.rem(me + step, seq), me).start()
        packed_out[rank] = packed_ref[...]
        routes_out[me] = routes_ref[...]

        gathers = seq_gathers(x_ref, x_v, x_sems)
        for program in gathers:
            program.start()

        def ready(h):
            @pl.when(h == me)
            def _():
                own_qkv.wait()

            @pl.when(h != me)
            def _():
                part(h, h).wait_recv()

        spread = Gather(
            x_line,
            core_line,
            dp,
            dp_flat,
            seq,
            lambda h: weight_rows(dp, h),
            weight_rows,
            qkv_send,
            qkv_recv,
            ready,
        )
        x_steps = sorted((s for p in gathers for s in p.steps()), key=lambda s: s[0])
        for hops, step in x_steps:
            if hops <= 1:
                step()
        spread.start()
        root = lax.div(me * ndp, seq)
        root_x, root_core = lax.div(root, 2), lax.rem(root, 2)
        on_line = core_line.place == root_core
        ways = [
            (on_line & (x_line.place >= root_x) & x_line.has(1), x_line.device(1), 0),
            (on_line & (x_line.place <= root_x) & x_line.has(-1), x_line.device(-1), 1),
            (on_line & core_line.has(1), core_line.device(1), 2),
            (on_line & core_line.has(-1), core_line.device(-1), 3),
        ]

        def onward(slot, way, target):
            return send_to(
                proj_out.at[slot], proj_out.at[slot], proj_fwd.at[slot, way], proj_recv.at[slot], target
            )

        rest = sorted(
            [s for s in x_steps if s[0] > 1] + [(hops + 0.75, step) for hops, step in spread.steps()],
            key=lambda s: s[0],
        )
        for _, step in rest:
            step()

        c_gathers = seq_gathers(c_ref, c_out, c_sems)
        own_c.start()
        for program in c_gathers:
            program.start()
        c_steps = sorted((s for p in c_gathers for s in p.steps()), key=lambda s: s[0])

        def move_cotangent(hops):
            while c_steps and c_steps[0][0] <= hops:
                c_steps.pop(0)[1]()

        for slot in range(ndp):
            held = (dp == root) & (lax.rem(me * ndp + slot, seq) == me)

            @pl.when(held)
            def _():
                own_proj.wait()

            @pl.when(jnp.logical_not(held))
            def _():
                onward(slot, 0, x_line.device(1)).wait_recv()

            for cond, target, way in ways:
                pl.when(cond)(lambda: onward(slot, way, target).start())

        def small_end(step, carry):
            source = lax.rem(rank + devices - step, devices)
            small(source, source).wait_recv()
            return carry

        lax.fori_loop(1, devices, small_end, 0)
        for block in range(width // 128):
            total = packed_out[block * per_block, n_router : n_router + 16, :].astype(F32)
            for i in range(1, per_block):
                total = total + packed_out[block * per_block + i, n_router : n_router + 16, :].astype(F32)
            gains_v[:, block * 128 : (block + 1) * 128] = total[0:8]
        own_x.wait()

        def normed_copy(src):
            return pltpu.make_async_copy(normed_v.at[src], normed_out.at[src], normed_sem.at[src])

        def project(src, carry):
            def strip(i, inner):
                at = pl.ds(pl.multiple_of(i * 16, 16), 16)
                values = x_v[src, at, :].astype(F32)
                factor = lax.rsqrt(jnp.mean(values * values, axis=-1, keepdims=True) + NORM_EPS)
                normed_v[src, at, :] = (values * factor * gains_v[0:1, :]).astype(BF)
                return inner

            lax.fori_loop(0, rows // 16, strip, 0, unroll=4)
            normed_copy(src).start()
            at = pl.ds(pl.multiple_of(src * rows, rows), rows)
            for j in range(2):
                raw = jnp.dot(normed_v[src], w_v[j], preferred_element_type=F32)
                raw_out[j, at, :] = raw
                sums_v[pl.ds(j * seq + src, 1), :] = as_row(jnp.sum(raw * raw, axis=1, keepdims=True))
            values = jnp.dot(normed_v[src], w_v[2], preferred_element_type=F32).astype(BF)
            for n in range(num_seqs):
                v_out[n, pl.ds(pl.multiple_of(src * local_len, local_len), local_len), :] = values[
                    n * local_len : (n + 1) * local_len
                ]
            return carry

        lax.fori_loop(0, seq // 2, project, 0)
        move_cotangent(1)
        lax.fori_loop(seq // 2, seq, project, 0)

        def square_sums(peer, origin):
            return send_to(sums_v, sums_got.at[origin], sums_send.at[peer], sums_recv.at[origin], (dp, peer))

        for step in range(1, seq):
            square_sums(lax.rem(me + step, seq), me).start()
        move_cotangent(2)
        total = sums_v[...]
        for step in range(1, seq):
            source = lax.rem(me + seq - step, seq)
            square_sums(source, source).wait_recv()
        sums_got[me] = sums_v[...]
        total = jnp.sum(sums_got[...], axis=0)
        for step in range(1, seq):
            square_sums(lax.rem(me + step, seq), me).wait_send()
        total_out[...] = total
        sums_v[...] = lax.rsqrt(total / width + NORM_EPS)

        def turn(src, carry):
            spots = pl.ds(pl.multiple_of(src * local_len, local_len), local_len)
            cosine, sine = cos_ref[spots, :], sin_ref[spots, :]
            for j, out in ((0, q_out), (1, k_out)):
                factor = as_columns(sums_v[pl.ds(j * seq + src, 1), :])
                for h in range(heads_here):
                    at = slice(h * HEAD_DIM, (h + 1) * HEAD_DIM)
                    gain = gains_v[
                        1 + j : 2 + j, pl.ds(pl.multiple_of(me * cols + h * HEAD_DIM, HEAD_DIM), HEAD_DIM)
                    ]
                    for n in range(num_seqs):
                        low, high = n * local_len, (n + 1) * local_len
                        values = raw_out[
                            j, pl.ds(pl.multiple_of(src * rows + low, local_len), local_len), at
                        ]
                        values = values * factor[low:high] * gain
                        out[n, spots, at] = turn_heads(values, cosine, sine).astype(BF)
            return carry

        lax.fori_loop(0, seq, turn, 0)
        move_cotangent(2.5)

        def attend(index, carry):
            n = lax.div(index, heads_here)
            head = pl.ds(pl.multiple_of(lax.rem(index, heads_here) * HEAD_DIM, HEAD_DIM), HEAD_DIM)
            for block in range(length // tile):
                low = block * tile
                limit = min(length, low + 2 * tile)
                scores = dot_rows(q_out[n, low : low + tile, head], k_out[n, 0:limit, head]) * HEAD_DIM**-0.5
                allowed = row_ref[n, 0:1, 0:limit] <= col_ref[n, low : low + tile, :]
                scores = jnp.where(allowed, scores, MASKED_SCORE)
                exps = jnp.exp(scores - jnp.max(scores, axis=-1, keepdims=True))
                probs = (exps / jnp.sum(exps, axis=-1, keepdims=True)).astype(BF)
                result = jnp.dot(probs, v_out[n, 0:limit, head], preferred_element_type=F32).astype(BF)
                for i in range(tile // local_len):
                    src = low // local_len + i
                    o_out[src, pl.ds(pl.multiple_of(n * local_len, local_len), local_len), head] = result[
                        i * local_len : (i + 1) * local_len
                    ]
            return carry

        lax.fori_loop(0, heads_here, attend, 0)
        move_cotangent(3)
        lax.fori_loop(heads_here, num_seqs * heads_here, attend, 0)
        move_cotangent(1000)

        for program in (*gathers, spread, *c_gathers):
            program.finish()
        for slot in range(ndp):
            for cond, target, way in ways:
                pl.when(cond)(lambda: onward(slot, way, target).wait_send())
        pl.when(jnp.logical_not(stays))(lambda: proj_first(place).wait_send())
        for step in range(1, seq):
            part(lax.rem(me + step, seq), me).wait_send()
            route(lax.rem(me + step, seq), me).wait_send()
            source = lax.rem(me + seq - step, seq)
            route(source, source).wait_recv()

        def small_sent(step, carry):
            small(lax.rem(rank + step, devices), rank).wait_send()
            return carry

        lax.fori_loop(1, devices, small_sent, 0)
        for src in range(seq):
            normed_copy(src).wait()
        own_c.wait()

    dma = pltpu.SemaphoreType.DMA
    hbm, vmem = pl.BlockSpec(memory_space=pl.ANY), pl.BlockSpec(memory_space=pltpu.VMEM)
    shaped = jax.ShapeDtypeStruct
    outs = [
        (shaped((seq, rows, width), BF), hbm),
        (shaped((seq, ahead, width), BF), hbm),
        (shaped((3, width, cols), BF), vmem),
        (shaped((ndp,) + proj_rows.shape, BF), hbm),
        (shaped((devices,) + packed.shape, BF), vmem),
        (shaped((seq,) + routes.shape, jnp.int32), vmem),
        (shaped((2, seq * rows, cols), F32), vmem),
        (shaped((num_seqs, length, cols), BF), vmem),
        (shaped((num_seqs, length, cols), BF), vmem),
        (shaped((num_seqs, length, cols), BF), vmem),
        (shaped((seq, rows, cols), BF), vmem),
        (shaped((2 * seq, rows), F32), vmem),
    ]
    return pl.pallas_call(
        kernel,
        out_shape=[shape for shape, _ in outs],
        in_specs=[hbm] * 4 + [vmem] * 6,
        out_specs=[spec for _, spec in outs],
        scratch_shapes=[
            pltpu.VMEM((seq, rows, width), BF),
            pltpu.VMEM((seq, rows, width), BF),
            pltpu.VMEM((8, width), F32),
            pltpu.VMEM((2 * seq, rows), F32),
            pltpu.VMEM((seq, 2 * seq, rows), F32),
            dma((3,)),
            dma((seq,)),
            dma((seq,)),
            dma((seq,)),
            dma,
            dma((ndp, seq, 4)),
            dma((ndp, seq)),
            dma,
            dma((ndp,)),
            dma((ndp, 4)),
            dma((devices,)),
            dma((devices,)),
            dma((seq,)),
            dma((seq,)),
            dma((seq,)),
            dma((seq,)),
        ]
        + gather_sems(seq, rows)
        + gather_sems(seq, ahead),
        compiler_params=pltpu.CompilerParams(
            collective_id=collective_id, has_side_effects=True, vmem_limit_bytes=VMEM_MOST
        ),
        name="attend_first",
        cost_estimate=cost_of(210),
    )(
        tokens,
        cotangent,
        qkv_rows,
        proj_rows,
        packed,
        routes,
        *tables,
        segments[:, :, None],
        segments[:, None, :],
    )


def small_exchange(arrays, axes, collective_id):
    sizes = [lax.axis_size(axis) for axis in axes]
    peers = math.prod(sizes)
    seq = lax.axis_size("seq")
    count = len(arrays)

    def kernel(*refs):
        ins, outs, (send_sem, recv_sem) = refs[:count], refs[count : 2 * count], refs[2 * count :]
        dp, sq = lax.axis_index("dp"), lax.axis_index("seq")
        me = sq if len(axes) == 1 else dp * seq + sq

        def device(peer):
            return (dp, peer) if len(axes) == 1 else (lax.div(peer, seq), lax.rem(peer, seq))

        barrier = pltpu.get_barrier_semaphore()
        for step in range(1, peers):
            pl.semaphore_signal(
                barrier, 1, device_id=device(lax.rem(me + step, peers)), device_id_type=MESH
            )
        pl.semaphore_wait(barrier, peers - 1)

        def copy(i, peer, src_slot):
            src = ins[i].at[0] if arrays[i].shape[0] == 1 else ins[i].at[peer]
            return pltpu.make_async_remote_copy(
                src_ref=src,
                dst_ref=outs[i].at[src_slot],
                send_sem=send_sem.at[i, peer],
                recv_sem=recv_sem.at[i, src_slot],
                device_id=device(peer),
                device_id_type=MESH,
            )

        for step in range(1, peers):
            for i in range(count):
                copy(i, lax.rem(me + step, peers), me).start()
        for i in range(count):
            outs[i][me] = ins[i][0] if arrays[i].shape[0] == 1 else ins[i][me]
        for step in range(1, peers):
            for i in range(count):
                copy(i, lax.rem(me + step, peers), me).wait_send()
                source = lax.rem(me + peers - step, peers)
                copy(i, source, source).wait_recv()

    return pl.pallas_call(
        kernel,
        out_shape=[jax.ShapeDtypeStruct((peers,) + a.shape[1:], a.dtype) for a in arrays],
        in_specs=[pl.BlockSpec(memory_space=pltpu.VMEM)] * count,
        out_specs=[pl.BlockSpec(memory_space=pltpu.VMEM)] * count,
        scratch_shapes=[
            pltpu.SemaphoreType.DMA((count, peers)),
            pltpu.SemaphoreType.DMA((count, peers)),
        ],
        compiler_params=pltpu.CompilerParams(collective_id=collective_id, has_side_effects=True),
        name="small_exchange",
        cost_estimate=cost_of(8),
    )(*arrays)


def middle_rows(o_head, proj_weight, tokens, gain, collective_id):
    seq, rows, cols = o_head.shape
    width = tokens.shape[1]
    nz, ny = grid_of(seq)
    n_seq = 10

    def kernel(*refs):
        o_ref, w_ref, x_ref, gain_ref, middle_out, ffn_out, all_out, terms_v, own_sem = refs[:9]
        scratch, sems = refs[9 : 9 + n_seq], refs[9 + n_seq :]
        along, across, me, _ = seq_lines()
        barrier = pltpu.get_barrier_semaphore()
        count = 0
        for line in (along, across):
            for turn in (1, -1):
                pl.when(line.has(turn))(
                    lambda: pl.semaphore_signal(
                        barrier, 1, device_id=line.device(turn), device_id_type=MESH
                    )
                )
                count = count + line.has(turn).astype(jnp.int32)

        def term(i, carry):
            dest = lax.rem(i, nz) * ny + lax.rem(across.place + 1 + lax.div(i, nz), ny)
            terms_v[dest] = jnp.dot(o_ref[dest], w_ref[...], preferred_element_type=F32).astype(BF)
            return carry

        lax.fori_loop(0, seq, term, 0)
        pl.semaphore_wait(barrier, count)
        reduces = seq_reduces(terms_v, middle_out, scratch)
        for step in woven(*[p.outward() for p in reduces]):
            step()
        for step in woven(*[p.inward() for p in reduces]):
            step()

        def strip(i, carry):
            at = pl.ds(pl.multiple_of(i * 16, 16), 16)
            values = middle_out[at, :] + x_ref[at, :].astype(F32)
            middle_out[at, :] = values
            factor = lax.rsqrt(jnp.mean(values * values, axis=-1, keepdims=True) + NORM_EPS)
            ffn_out[at, :] = (values * factor * gain_ref[...]).astype(BF)
            return carry

        lax.fori_loop(0, rows // 16, strip, 0, unroll=4)
        own = pltpu.make_async_copy(ffn_out, all_out.at[me], own_sem)
        own.start()
        gathers = seq_gathers(ffn_out, all_out, sems)
        for program in gathers:
            program.start()
        for program in reduces:
            program.finish()
        run_steps(*gathers)
        for program in gathers:
            program.finish()
        own.wait()

    vmem = pl.BlockSpec(memory_space=pltpu.VMEM)
    return pl.pallas_call(
        kernel,
        out_shape=[
            jax.ShapeDtypeStruct((rows, width), F32),
            jax.ShapeDtypeStruct((rows, width), BF),
            jax.ShapeDtypeStruct((seq, rows, width), BF),
        ],
        in_specs=[vmem] * 4,
        out_specs=[vmem, vmem, pl.BlockSpec(memory_space=pl.ANY)],
        scratch_shapes=[pltpu.VMEM((seq, rows, width), BF), pltpu.SemaphoreType.DMA]
        + reduce_scratch(seq, rows, width)
        + gather_sems(seq, rows),
        compiler_params=pltpu.CompilerParams(
            collective_id=collective_id, has_side_effects=True, vmem_limit_bytes=VMEM_MOST
        ),
        name="middle_rows",
        cost_estimate=cost_of(175),
    )(o_head, proj_weight, tokens, gain)


def attend_back(dz, proj_weight, o_head, query, key, value, raw, squares, gains, tables, segments, collective_id):
    seq = lax.axis_size("seq")
    rows, width = dz.shape
    num_seqs, length, cols = query.shape
    local_len = length // seq
    heads_here = cols // HEAD_DIM
    tile = 256
    scale = HEAD_DIM**-0.5

    def kernel(*refs):
        (dz_ref, w_ref, o_ref, q_ref, k_ref, v_ref, raw_ref, squares_ref, gains_ref) = refs[:9]
        (cos_ref, sin_ref, col_ref, row_ref) = refs[9:13]
        d_out, proj_out, gain_out = refs[13:16]
        (dz_v, do_v, turned, dk_acc, dv_acc, proj_acc, factor_v, inner_v, inner_got) = refs[16:25]
        own_sem, inner_send, inner_recv = refs[25:28]
        sems = refs[28:]
        dp = lax.axis_index("dp")
        along, across, me, _ = seq_lines()
        barrier = pltpu.get_barrier_semaphore()
        for step in range(1, seq):
            pl.semaphore_signal(
                barrier, 1, device_id=(dp, lax.rem(me + step, seq)), device_id_type=MESH
            )
        pl.semaphore_wait(barrier, seq - 1)
        own = pltpu.make_async_copy(dz_ref, dz_v.at[me], own_sem)
        own.start()
        programs = seq_gathers(dz_ref, dz_v, sems)
        for program in programs:
            program.start()
        factor_v[...] = lax.rsqrt(squares_ref[...] / width + NORM_EPS)
        proj_acc[...] = jnp.zeros_like(proj_acc)
        own.wait()
        run_steps(*programs)

        def project(src, carry):
            back = dot_rows(dz_v[src], w_ref[...]).astype(BF)
            for n in range(num_seqs):
                do_v[n, pl.ds(pl.multiple_of(src * local_len, local_len), local_len), :] = back[
                    n * local_len : (n + 1) * local_len
                ]
            proj_acc[...] += lax.dot_general(
                o_ref[src], dz_v[src], (((0,), (0,)), ((), ())), preferred_element_type=F32
            )
            return carry

        lax.fori_loop(0, seq, project, 0)
        proj_out[...] = proj_acc[...].astype(BF)

        def unturn(values, at):
            return values * cos_ref[at, :] - pltpu.roll(values, HEAD_DIM // 2, 1) * sin_ref[at, :]

        def attend(index, carry):
            n = lax.div(index, heads_here)
            head = pl.ds(pl.multiple_of(lax.rem(index, heads_here) * HEAD_DIM, HEAD_DIM), HEAD_DIM)
            dk_acc[...] = jnp.zeros_like(dk_acc)
            dv_acc[...] = jnp.zeros_like(dv_acc)
            for block in range(length // tile):
                low = block * tile
                limit = min(length, low + 2 * tile)
                spots = slice(low, low + tile)
                queries, keys, grads = q_ref[n, spots, head], k_ref[n, 0:limit, head], do_v[n, spots, head]
                scores = dot_rows(queries, keys) * scale
                allowed = row_ref[n, 0:1, 0:limit] <= col_ref[n, spots, :]
                scores = jnp.where(allowed, scores, MASKED_SCORE)
                exps = jnp.exp(scores - jnp.max(scores, axis=-1, keepdims=True))
                probs = exps / jnp.sum(exps, axis=-1, keepdims=True)
                grad_probs = dot_rows(grads, v_ref[n, 0:limit, head])
                inner = jnp.sum(probs * grad_probs, axis=-1, keepdims=True)
                grad_scores = (probs * (grad_probs - inner)).astype(BF)
                dq = jnp.dot(grad_scores, keys, preferred_element_type=F32) * scale
                turned[0, n, spots, head] = unturn(dq, spots)
                dk_acc[0:limit, :] += lax.dot_general(
                    grad_scores, queries, (((0,), (0,)), ((), ())), preferred_element_type=F32
                )
                dv_acc[0:limit, :] += lax.dot_general(
                    probs.astype(BF), grads, (((0,), (0,)), ((), ())), preferred_element_type=F32
                )
            for block in range(length // tile):
                spots = slice(block * tile, (block + 1) * tile)
                turned[1, n, spots, head] = unturn(dk_acc[spots, :] * scale, spots)
            for src in range(seq):
                d_out[2, src, pl.ds(pl.multiple_of(n * local_len, local_len), local_len), head] = dv_acc[
                    src * local_len : (src + 1) * local_len, :
                ].astype(BF)
            return carry

        lax.fori_loop(0, num_seqs * heads_here, attend, 0)

        def pieces(j, src):
            spots = pl.ds(pl.multiple_of(src * local_len, local_len), local_len)
            grads = jnp.concatenate([turned[j, n, spots, :] for n in range(num_seqs)], axis=0)
            return grads, raw_ref[j, pl.ds(pl.multiple_of(src * rows, rows), rows), :]

        def wide(row):
            return jnp.concatenate([as_columns(row)] * heads_here, axis=1)

        def measure(src, carry):
            sums = []
            for j in range(2):
                grads, values = pieces(j, src)
                scaled = grads * gains_ref[j : j + 1, :]
                inner_v[pl.ds(j * seq + src, 1), :] = as_row(
                    jnp.sum(scaled * values, axis=1, keepdims=True)
                )
                factor = wide(factor_v[pl.ds(j * seq + src, 1), :])
                sums.append(carry[j] + jnp.sum(grads * values * factor, axis=0, keepdims=True))
            return tuple(sums)

        zero = jnp.zeros((1, cols), F32)
        gain_q, gain_k = lax.fori_loop(0, seq, measure, (zero, zero))
        gain_out[0:1, :] = gain_q
        gain_out[1:2, :] = gain_k
        gain_out[2:8, :] = jnp.zeros((6, cols), F32)

        def inner_copy(peer, origin):
            return send_to(
                inner_v, inner_got.at[origin], inner_send.at[peer], inner_recv.at[origin], (dp, peer)
            )

        for step in range(1, seq):
            inner_copy(lax.rem(me + step, seq), me).start()
        inner_got[me] = inner_v[...]
        for program in programs:
            program.finish()
        for step in range(1, seq):
            source = lax.rem(me + seq - step, seq)
            inner_copy(source, source).wait_recv()
            inner_copy(lax.rem(me + step, seq), me).wait_send()
        inner_v[...] = jnp.sum(inner_got[...], axis=0) / width

        def normalize(src, carry):
            for j in range(2):
                grads, values = pieces(j, src)
                factor = wide(factor_v[pl.ds(j * seq + src, 1), :])
                inner = wide(inner_v[pl.ds(j * seq + src, 1), :])
                scaled = grads * gains_ref[j : j + 1, :]
                d_out[j, src] = (factor * (scaled - values * factor * factor * inner)).astype(BF)
            return carry

        lax.fori_loop(0, seq, normalize, 0)

    dma = pltpu.SemaphoreType.DMA
    hbm, vmem = pl.BlockSpec(memory_space=pl.ANY), pl.BlockSpec(memory_space=pltpu.VMEM)
    return pl.pallas_call(
        kernel,
        out_shape=[
            jax.ShapeDtypeStruct((3, seq, rows, cols), BF),
            jax.ShapeDtypeStruct((cols, width), BF),
            jax.ShapeDtypeStruct((8, cols), F32),
        ],
        in_specs=[hbm] + [vmem] * 12,
        out_specs=[vmem] * 3,
        scratch_shapes=[
            pltpu.VMEM((seq, rows, width), BF),
            pltpu.VMEM((num_seqs, length, cols), BF),
            pltpu.VMEM((2, num_seqs, length, cols), F32),
            pltpu.VMEM((length, HEAD_DIM), F32),
            pltpu.VMEM((length, HEAD_DIM), F32),
            pltpu.VMEM((cols, width), F32),
            pltpu.VMEM((2 * seq, rows), F32),
            pltpu.VMEM((2 * seq, rows), F32),
            pltpu.VMEM((seq, 2 * seq, rows), F32),
            dma,
            dma((seq,)),
            dma((seq,)),
        ]
        + gather_sems(seq, rows),
        compiler_params=pltpu.CompilerParams(
            collective_id=collective_id, has_side_effects=True, vmem_limit_bytes=VMEM_MOST
        ),
        name="attend_back",
        cost_estimate=cost_of(130),
    )(
        dz,
        proj_weight,
        o_head,
        query,
        key,
        value,
        raw,
        squares,
        gains,
        *tables,
        segments[:, :, None],
        segments[:, None, :],
    )


def dp_cuts(rows):
    pieces = max(n for n in (8, 4, 2, 1) if rows % (16 * n) == 0)
    return [(i * (rows // pieces), rows // pieces) for i in range(pieces)]


def last_sums(grads, normed, qkv_weight, proj_terms, router_terms, gain_heads, gain_ffn, gain_attn, collective_id):
    seq, ndp = lax.axis_size("seq"), lax.axis_size("dp")
    devices = seq * ndp
    _, _, rows, cols = grads.shape
    width = normed.shape[2]
    nz, ny = grid_of(seq)
    own_rows = proj_terms.shape[1]
    part_rows = 3 * own_rows
    n_router = router_terms.shape[1]
    per_block = 128 // own_rows
    n_seq = 10
    n_dp = 5
    block = 256

    def kernel(*refs):
        (d_ref, normed_ref, w_ref, proj_ref, router_ref, heads_ref, ffn_ref, gain_ref) = refs[:8]
        (o_ref, qkv_out, proj_out, sum_out) = refs[8:12]
        (terms_v, normed_v, qkv_v, qkv_sum, proj_v, proj_sum, packed_v, got, gains_v, normed_sem, proj_sem) = refs[12:23]
        rest = refs[23:]
        seq_scratch, rest = rest[:n_seq], rest[n_seq:]
        qkv_scratch, proj_scratch, rest = rest[:n_dp], rest[n_dp : 2 * n_dp], rest[2 * n_dp :]
        (part_send, part_recv, move_send, move_recv, small_send, small_recv, own_sem) = rest
        _, across, me, _ = seq_lines()
        x_line, core_line, dp, dp_flat = dp_lines()
        rank = dp * seq + me
        load_normed = pltpu.make_async_copy(normed_ref, normed_v, normed_sem)
        load_normed.start()
        load_proj = pltpu.make_async_copy(proj_ref, proj_v, proj_sem)
        load_proj.start()
        barrier = pltpu.get_barrier_semaphore()

        def device(peer):
            return (lax.div(peer, seq), lax.rem(peer, seq))

        def meet(step, carry):
            pl.semaphore_signal(
                barrier, 1, device_id=device(lax.rem(rank + step, devices)), device_id_type=MESH
            )
            return carry

        lax.fori_loop(1, devices, meet, 0)

        def normed_term(i, carry):
            dest = lax.rem(i, nz) * ny + lax.rem(across.place + 1 + lax.div(i, nz), ny)
            total = dot_rows(d_ref[0, dest], w_ref[0])
            for j in range(1, 3):
                total = total + dot_rows(d_ref[j, dest], w_ref[j])
            terms_v[dest] = total.astype(BF)
            return carry

        load_normed.wait()
        gains_v[...] = jnp.zeros_like(gains_v)
        for j in range(2):
            gains_v[1 + j : 2 + j, pl.ds(pl.multiple_of(me * cols, 128), cols)] = heads_ref[j : j + 1, :]
        gains_v[3:4, :] = ffn_ref[...]

        def weight_term(i, carry):
            at = pl.ds(pl.multiple_of(i * block, block), block)
            turned = normed_v[:, :, at].reshape(seq * rows, block).T
            gain = jnp.zeros((block, 1), F32)
            for j in range(3):
                term = jnp.dot(turned, d_ref[j].reshape(seq * rows, cols), preferred_element_type=F32)
                gain = gain + jnp.sum(term * w_ref[j, at, :].astype(F32), axis=1, keepdims=True)
                low = term.astype(BF)
                for piece in range(block // own_rows):
                    owner = i * (block // own_rows) + piece
                    spot = pl.multiple_of(lax.rem(owner, seq) * part_rows + j * own_rows, own_rows)
                    qkv_v[lax.div(owner, seq), pl.ds(spot, own_rows), :] = low[
                        piece * own_rows : (piece + 1) * own_rows
                    ]
            gains_v[0:1, at] = as_row(gain) / gain_ref[:, at]
            return carry

        blocks = width // block
        near = blocks // x_line.size

        def rotated(i, carry):
            return weight_term(lax.rem((x_line.place + 1) * near + i, blocks), carry)

        load_proj.wait()

        def over_dp(refs, out, buffers):
            return Reduce(
                core_line,
                x_line,
                dp,
                lambda core, x: dp_flat(x, core),
                dp_cuts(refs.shape[1]),
                refs,
                out,
                *buffers[0:2],
                buffers[2:5],
            )

        owners = [over_dp(qkv_v, qkv_sum, qkv_scratch), over_dp(proj_v, proj_sum, proj_scratch)]
        out_lists = [(list(owner.outward()), 2 * len(owner.cuts)) for owner in owners]
        in_lists = [(list(owner.inward()), len(owner.cuts)) for owner in owners]
        programs = seq_reduces(terms_v, o_ref, seq_scratch)

        lax.fori_loop(0, seq - nz, normed_term, 0)
        pl.semaphore_wait(barrier, devices - 1)
        for step in programs[0].outward():
            step()
        lax.fori_loop(0, blocks - near, rotated, 0)
        for steps, kept in out_lists:
            for step in steps[:-kept]:
                step()
        lax.fori_loop(seq - nz, seq, normed_term, 0)
        for step in programs[1].outward():
            step()
        for steps, kept in in_lists:
            for step in steps[:-kept]:
                step()
        inward = woven(*[p.inward() for p in programs])
        in_all = len(inward)

        def move_sums(share):
            while inward and in_all - len(inward) < share * in_all:
                inward.pop(0)()

        lax.fori_loop(blocks - near, blocks, rotated, 0)
        for steps, kept in out_lists:
            for step in steps[-kept:]:
                step()
        move_sums(0.25)
        packed_v[:, 0:n_router, :] = router_ref[...]
        for peer in range(devices):
            at = peer // per_block * 128
            packed_v[peer, n_router : n_router + 8, :] = gains_v[:, at : at + 128]

        def small(peer, origin):
            return send_to(
                packed_v.at[peer], got.at[origin], small_send.at[peer], small_recv.at[origin], device(peer)
            )

        def small_start(step, carry):
            small(lax.rem(rank + step, devices), rank).start()
            return carry

        lax.fori_loop(1, devices, small_start, 0)

        def part(peer, origin):
            return send_to(
                qkv_sum.at[pl.ds(pl.multiple_of(peer * part_rows, 16), part_rows)],
                qkv_out.at[origin],
                part_send.at[peer],
                part_recv.at[origin],
                (dp, peer),
            )

        own_part = pltpu.make_async_copy(
            qkv_sum.at[pl.ds(pl.multiple_of(me * part_rows, 16), part_rows)], qkv_out.at[me], own_sem.at[0]
        )
        goal = me * ndp + dp
        stays = goal == rank
        own_move = pltpu.make_async_copy(proj_sum, proj_out, own_sem.at[1])

        def move():
            return send_to(proj_sum, proj_out, move_send, move_recv, device(goal))

        move_sums(0.8)
        for steps, kept in in_lists:
            for step in steps[-kept:]:
                step()
        own_part.start()
        for step in range(1, seq):
            part(lax.rem(me + step, seq), me).start()
        pl.when(stays)(own_move.start)
        pl.when(jnp.logical_not(stays))(lambda: move().start())
        move_sums(1.0)

        got[rank] = packed_v[rank]

        def small_end(step, carry):
            small(lax.rem(rank + step, devices), rank).wait_send()
            source = lax.rem(rank + devices - step, devices)
            small(source, source).wait_recv()
            return carry

        lax.fori_loop(1, devices, small_end, 0)
        sum_out[...] = jnp.sum(got[...], axis=0)
        for program in (*programs, *owners):
            program.finish()
        for step in range(1, seq):
            part(lax.rem(me + step, seq), me).wait_send()
            source = lax.rem(me + seq - step, seq)
            part(source, source).wait_recv()
        own_part.wait()

        @pl.when(stays)
        def _():
            own_move.wait()

        @pl.when(jnp.logical_not(stays))
        def _():
            move().wait_send()
            move().wait_recv()

    dma = pltpu.SemaphoreType.DMA
    hbm, vmem = pl.BlockSpec(memory_space=pl.ANY), pl.BlockSpec(memory_space=pltpu.VMEM)
    return pl.pallas_call(
        kernel,
        out_shape=[
            jax.ShapeDtypeStruct((rows, width), F32),
            jax.ShapeDtypeStruct((seq, part_rows, cols), BF),
            jax.ShapeDtypeStruct((own_rows, width), BF),
            jax.ShapeDtypeStruct((n_router + 8, 128), F32),
        ],
        in_specs=[vmem, hbm, vmem, hbm] + [vmem] * 4,
        out_specs=[vmem] * 4,
        scratch_shapes=[
            pltpu.VMEM((seq, rows, width), BF),
            pltpu.VMEM((seq, rows, width), BF),
            pltpu.VMEM((ndp, seq * part_rows, cols), BF),
            pltpu.VMEM((seq * part_rows, cols), BF),
            pltpu.VMEM(proj_terms.shape, BF),
            pltpu.VMEM((own_rows, width), BF),
            pltpu.VMEM((devices, n_router + 8, 128), F32),
            pltpu.VMEM((devices, n_router + 8, 128), F32),
            pltpu.VMEM((8, width), F32),
            dma,
            dma,
        ]
        + reduce_scratch(seq, rows, width)
        + Reduce.scratch(dp_cuts(seq * part_rows), 2, ndp // 2, cols)
        + Reduce.scratch(dp_cuts(own_rows), 2, ndp // 2, width)
        + [dma((seq,)), dma((seq,)), dma, dma, dma((devices,)), dma((devices,)), dma((2,))],
        compiler_params=pltpu.CompilerParams(
            collective_id=collective_id, has_side_effects=True, vmem_limit_bytes=VMEM_MOST
        ),
        name="last_sums",
        cost_estimate=cost_of(110),
    )(grads, normed, qkv_weight, proj_terms, router_terms, gain_heads, gain_ffn, gain_attn)


def packed_rows(parts, sublanes):
    flat = jnp.concatenate(parts, axis=1)
    fill = -flat.shape[1] % (sublanes * 128)
    return jnp.pad(flat, ((0, 0), (0, fill))).reshape(flat.shape[0], -1, 128)


def slot_places(slots, capacity):
    rows, experts = slots.shape
    number = lax.broadcasted_iota(jnp.int32, (capacity, rows), 0).astype(F32)
    return [as_row(slots[:, e : e + 1]) == number for e in range(experts)]


def experts_dispatch(ffn_all, routes_all, router_full, me, experts, capacity):
    seq, rows, width = ffn_all.shape
    experts_all, top = router_full.shape[1], routes_all.shape[2]

    def kernel(me_ref, ffn_ref, routes_ref, router_ref, rows_out, gate_out, slot_out, col_out):
        first = me_ref[0] * experts
        logits = jnp.dot(ffn_ref[0], router_ref[...], preferred_element_type=F32)
        exps = jnp.exp(logits - jnp.max(logits, axis=-1, keepdims=True))
        probs = exps / jnp.sum(exps, axis=-1, keepdims=True)
        lane = lax.broadcasted_iota(jnp.int32, (rows, experts_all), 1)
        wide_lane = lax.broadcasted_iota(jnp.int32, (rows, 128), 1)
        hits, gates = jnp.zeros((rows, 128), F32), []
        for e in range(experts):
            hit = jnp.sum((routes_ref[0] == first + e).astype(F32), axis=1, keepdims=True)
            hits = jnp.where(wide_lane == e, hit, hits)
            gates.append(jnp.sum(jnp.where(lane == first + e, probs, 0.0), axis=1, keepdims=True))
        below = lax.broadcasted_iota(jnp.int32, (rows, rows), 0) > lax.broadcasted_iota(
            jnp.int32, (rows, rows), 1
        )
        earlier = jnp.dot(below.astype(BF), hits.astype(BF), preferred_element_type=F32)
        slots = jnp.where(hits > 0.0, earlier, float(rows + 1))[:, 0:experts]
        places = slot_places(slots, capacity)
        slot_out[0] = slots
        for e in range(experts):
            gate_out[e, 0] = jnp.sum(jnp.where(places[e], as_row(gates[e]), 0.0), axis=1, keepdims=True)
            col_out[0, :, e : e + 1] = gates[e]
        for e in range(experts):
            rows_out[e, 0] = jnp.dot(
                places[e].astype(BF), ffn_ref[0], preferred_element_type=F32
            ).astype(BF)

    def source(s, _):
        return (s, 0, 0)

    def slot(s, _):
        return (0, s, 0, 0)

    shaped = jax.ShapeDtypeStruct
    return pl.pallas_call(
        kernel,
        out_shape=[
            shaped((experts, seq, capacity, width), BF),
            shaped((experts, seq, capacity, 1), F32),
            shaped((seq, rows, experts), F32),
            shaped((seq, rows, experts), F32),
        ],
        grid_spec=pltpu.PrefetchScalarGridSpec(
            num_scalar_prefetch=1,
            grid=(seq,),
            in_specs=[
                pl.BlockSpec((1, rows, width), source),
                pl.BlockSpec((1, rows, top), source),
                pl.BlockSpec((width, experts_all), lambda s, _: (0, 0)),
            ],
            out_specs=[
                pl.BlockSpec((experts, 1, capacity, width), slot),
                pl.BlockSpec((experts, 1, capacity, 1), slot),
                pl.BlockSpec((1, rows, experts), source),
                pl.BlockSpec((1, rows, experts), source),
            ],
        ),
        compiler_params=pltpu.CompilerParams(vmem_limit_bytes=VMEM_MOST),
        name="experts_dispatch",
        cost_estimate=cost_of(12),
    )(me.reshape(1), ffn_all, routes_all, router_full)


EXPERT_STEP = 512


def server(now, places, thunks):
    per_step, steps = places
    spots = [min(per_step * steps - 1, int(per_step * steps * share)) for share, _ in thunks]

    def serve(point):
        for mark in sorted(set(spots)):
            if mark % per_step != point:
                continue
            group = [thunk for spot, (_, thunk) in zip(spots, thunks) if spot == mark]

            @pl.when(now == mark // per_step)
            def _():
                for thunk in group:
                    thunk()

    return serve


def experts_forward(rows, weight_in, weight_out, cot_rows, collective_id):
    experts, slots, width = rows.shape
    hidden_width = weight_out.shape[1]
    step = EXPERT_STEP
    steps = hidden_width // step
    seq = lax.axis_size("seq")
    part = cot_rows.shape[0]
    last = experts * steps - 1

    def kernel(rows_ref, in_ref, out_ref, c_ref, y_out, gate_out, up_out, hidden_out, c_out, acc, own_sem, *sems):
        f = pl.program_id(1)
        now = pl.program_id(0) * steps + f
        along, across, me, _ = seq_lines()
        gathers = seq_gathers(c_ref, c_out, sems)
        moves = sorted((s for p in gathers for s in p.steps()), key=lambda s: s[0])
        most = max(hops for hops, _ in moves)
        serve = server(now, (2, last + 1), [(0.1 + 0.85 * hops / most, thunk) for hops, thunk in moves])
        own = pltpu.make_async_copy(c_ref, c_out.at[me], own_sem)

        @pl.when(now == 0)
        def _():
            greet_lines(along, across)
            own.start()
            for program in gathers:
                program.start()

        gate = jnp.dot(rows_ref[0], in_ref[0, 0], preferred_element_type=F32)
        up = jnp.dot(rows_ref[0], in_ref[0, 1], preferred_element_type=F32)
        gate_out[0] = gate.astype(BF)
        up_out[0] = up.astype(BF)
        hidden = (gate / (1.0 + jnp.exp(-gate)) * up).astype(BF)
        hidden_out[0] = hidden
        serve(0)
        value = jnp.dot(hidden, out_ref[0], preferred_element_type=F32)

        @pl.when(f == 0)
        def _():
            acc[...] = value

        @pl.when(f > 0)
        def _():
            acc[...] += value

        @pl.when(f == steps - 1)
        def _():
            y_out[0] = acc[...].astype(BF)

        serve(1)

        @pl.when(now == last)
        def _():
            for program in gathers:
                program.finish()
            own.wait()

    shaped = jax.ShapeDtypeStruct
    hbm = pl.BlockSpec(memory_space=pl.ANY)
    by_expert = pl.BlockSpec((1, slots, width), lambda e, f: (e, 0, 0))
    hidden_block = pl.BlockSpec((1, slots, step), lambda e, f: (e, 0, f))
    return pl.pallas_call(
        kernel,
        grid=(experts, steps),
        out_shape=[
            shaped((experts, slots, width), BF),
            shaped((experts, slots, hidden_width), BF),
            shaped((experts, slots, hidden_width), BF),
            shaped((experts, slots, hidden_width), BF),
            shaped((seq, part, width), BF),
        ],
        in_specs=[
            by_expert,
            pl.BlockSpec((1, 2, width, step), lambda e, f: (e, 0, 0, f)),
            pl.BlockSpec((1, step, width), lambda e, f: (e, f, 0)),
            hbm,
        ],
        out_specs=[by_expert, hidden_block, hidden_block, hidden_block, hbm],
        scratch_shapes=[pltpu.VMEM((slots, width), F32), pltpu.SemaphoreType.DMA] + gather_sems(seq, part),
        compiler_params=pltpu.CompilerParams(
            collective_id=collective_id, has_side_effects=True, vmem_limit_bytes=VMEM_MOST
        ),
        name="experts_forward",
        cost_estimate=cost_of(65),
    )(rows, weight_in, weight_out, cot_rows)


def experts_mix(outputs, cot_first, cot_rest, gates, slot_cols, gate_cols):
    experts, slots, width = outputs.shape
    seq, rows, _ = slot_cols.shape
    capacity = slots // seq
    ahead = cot_first.shape[1]

    def kernel(y_ref, a_ref, b_ref, gate_ref, slot_ref, col_ref, mixed_out, dy_out, dprob_out, y_v, c_v):
        slot_cols = slot_ref[0]
        c_v[0:ahead, :] = a_ref[0]
        c_v[ahead:rows, :] = b_ref[0]
        number = lax.broadcasted_iota(jnp.int32, (rows, capacity), 1).astype(F32)
        places = slot_places(slot_cols, capacity)
        gated = []
        for e in range(experts):
            value = y_ref[e, 0]
            y_v[e * capacity : (e + 1) * capacity, :] = value
            gated.append(
                jnp.where(slot_cols[:, e : e + 1] == number, col_ref[0, :, e : e + 1], 0.0).astype(BF)
            )
            cot = jnp.dot(places[e].astype(BF), c_v[...], preferred_element_type=F32)
            dy_out[e, 0] = (cot * gate_ref[e, 0]).astype(BF)
            dgate = jnp.sum(cot * value.astype(F32), axis=1, keepdims=True)
            dprob_out[0, e : e + 1, :] = jnp.sum(jnp.where(places[e], dgate, 0.0), axis=0, keepdims=True)
        mixed_out[0] = jnp.dot(
            jnp.concatenate(gated, axis=1), y_v[...], preferred_element_type=F32
        ).astype(BF)

    def source(s):
        return (s, 0, 0)

    def slot(s):
        return (0, s, 0, 0)

    shaped = jax.ShapeDtypeStruct
    return pl.pallas_call(
        kernel,
        grid=(seq,),
        out_shape=[
            shaped((seq, rows, width), BF),
            shaped((experts, seq, capacity, width), BF),
            shaped((seq, experts, rows), F32),
        ],
        in_specs=[
            pl.BlockSpec((experts, 1, capacity, width), slot),
            pl.BlockSpec((1, ahead, width), source),
            pl.BlockSpec((1, rows - ahead, width), source),
            pl.BlockSpec((experts, 1, capacity, 1), slot),
            pl.BlockSpec((1, rows, experts), source),
            pl.BlockSpec((1, rows, experts), source),
        ],
        out_specs=[
            pl.BlockSpec((1, rows, width), source),
            pl.BlockSpec((experts, 1, capacity, width), slot),
            pl.BlockSpec((1, experts, rows), source),
        ],
        scratch_shapes=[pltpu.VMEM((experts * capacity, width), BF), pltpu.VMEM((rows, width), BF)],
        compiler_params=pltpu.CompilerParams(vmem_limit_bytes=VMEM_MOST),
        name="experts_mix",
        cost_estimate=cost_of(15),
    )(outputs.reshape(experts, seq, capacity, width), cot_first, cot_rest, gates, slot_cols, gate_cols)


def experts_out_terms(hidden, grads):
    experts, slots, width = grads.shape
    hidden_width = hidden.shape[2]
    step = hidden_width

    def kernel(hidden_ref, dy_ref, out_ref):
        out_ref[0] = lax.dot_general(
            hidden_ref[0], dy_ref[0], (((0,), (0,)), ((), ())), preferred_element_type=F32
        ).astype(BF)

    return pl.pallas_call(
        kernel,
        grid=(experts, hidden_width // step),
        out_shape=jax.ShapeDtypeStruct((experts, hidden_width, width), BF),
        in_specs=[
            pl.BlockSpec((1, slots, step), lambda e, f: (e, 0, f)),
            pl.BlockSpec((1, slots, width), lambda e, f: (e, 0, 0)),
        ],
        out_specs=pl.BlockSpec((1, step, width), lambda e, f: (e, f, 0)),
        compiler_params=pltpu.CompilerParams(vmem_limit_bytes=VMEM_MOST),
        name="experts_out_terms",
        cost_estimate=cost_of(15),
    )(hidden, grads)


def experts_back(rows, grads, gate_in, up_in, weight_in, weight_out, mixed_terms, collective_id):
    experts, slots, width = rows.shape
    hidden_width = weight_out.shape[1]
    step = EXPERT_STEP
    steps = hidden_width // step
    seq, tok, _ = mixed_terms.shape
    last = experts * steps - 1

    def kernel(
        rows_ref, dy_ref, gate_ref, up_ref, in_ref, out_ref, mixed_ref,
        drows_out, in_out, mixed_out,
        rows_t, mixed_v, load_sem, *scratch,
    ):
        f = pl.program_id(1)
        now = pl.program_id(0) * steps + f
        along, across, _, _ = seq_lines()
        reduces = seq_reduces(mixed_v, mixed_out, scratch)
        outward, late = (list(p.outward()) for p in reduces)
        early_in, late_in = (list(p.inward()) for p in reduces)
        nz = along.size
        rank = 2 * len(reduces[0].cuts)
        thunks = [(0.06 + 0.18 * i / len(late), thunk) for i, thunk in enumerate(late)]
        thunks += [(0.07 + (i // rank + 1) / nz, thunk) for i, thunk in enumerate(early_in)]
        thunks += [((i + 1.5) / (len(late_in) + 0.5), thunk) for i, thunk in enumerate(late_in)]
        serve = server(now, (4, last + 1), sorted(thunks, key=lambda t: t[0]))
        load = pltpu.make_async_copy(mixed_ref, mixed_v, load_sem)

        @pl.when(now == 0)
        def _():
            load.start()
            greet_lines(along, across)
            load.wait()
            for thunk in outward:
                thunk()

        @pl.when(f == 0)
        def _():
            rows_t[...] = rows_ref[0].T

        grad = dot_rows(dy_ref[0], out_ref[0])
        serve(0)
        gate, up = gate_ref[0].astype(F32), up_ref[0].astype(F32)
        sig = 1.0 / (1.0 + jnp.exp(-gate))
        silu = gate * sig
        dgate = (grad * up * sig * (1.0 + gate * (1.0 - sig))).astype(BF)
        dup = (grad * silu).astype(BF)
        in_out[0, 0] = jnp.dot(rows_t[...], dgate, preferred_element_type=F32).astype(BF)
        serve(1)
        in_out[0, 1] = jnp.dot(rows_t[...], dup, preferred_element_type=F32).astype(BF)
        serve(2)
        value = dot_rows(dgate, in_ref[0, 0]) + dot_rows(dup, in_ref[0, 1])

        @pl.when(f == 0)
        def _():
            drows_out[0] = value.astype(BF)

        @pl.when(f > 0)
        def _():
            drows_out[0] = (drows_out[0].astype(F32) + value).astype(BF)

        serve(3)

        @pl.when(now == last)
        def _():
            for program in reduces:
                program.finish()

    shaped = jax.ShapeDtypeStruct
    hbm = pl.BlockSpec(memory_space=pl.ANY)
    by_expert = pl.BlockSpec((1, slots, width), lambda e, f: (e, 0, 0))
    once = pl.BlockSpec((1, slots, width), lambda e, f: (e, 0, 0), pipeline_mode=pl.Buffered(1))
    hidden_block = pl.BlockSpec((1, slots, step), lambda e, f: (e, 0, f))
    in_block = pl.BlockSpec((1, 2, width, step), lambda e, f: (e, 0, 0, f))
    out_block = pl.BlockSpec((1, step, width), lambda e, f: (e, f, 0))
    return pl.pallas_call(
        kernel,
        grid=(experts, steps),
        out_shape=[
            shaped((experts, slots, width), BF),
            shaped((experts, 2, width, hidden_width), BF),
            shaped((tok, width), F32),
        ],
        in_specs=[once, once, hidden_block, hidden_block, in_block, out_block, hbm],
        out_specs=[by_expert, in_block, pl.BlockSpec(memory_space=pltpu.VMEM)],
        scratch_shapes=[
            pltpu.VMEM((width, slots), BF),
            pltpu.VMEM((seq, tok, width), BF),
            pltpu.SemaphoreType.DMA,
        ]
        + reduce_scratch(seq, tok, width),
        compiler_params=pltpu.CompilerParams(
            collective_id=collective_id, has_side_effects=True, vmem_limit_bytes=VMEM_MOST
        ),
        name="experts_back",
        cost_estimate=cost_of(95),
    )(rows, grads, gate_in, up_in, weight_in, weight_out, mixed_terms)


def rows_back(drows, slot_cols, prob_grads, collective_id):
    seq, rows, experts = slot_cols.shape
    width = drows.shape[-1]
    capacity = drows.shape[1] // seq
    nz, ny = grid_of(seq)

    def kernel(d_ref, slot_ref, prob_ref, o_ref, prob_out, terms_v, d_v, prob_send, prob_recv, *scratch):
        dp = lax.axis_index("dp")
        _, across, me, _ = seq_lines()
        barrier = pltpu.get_barrier_semaphore()
        for step in range(1, seq):
            pl.semaphore_signal(
                barrier, 1, device_id=(dp, lax.rem(me + step, seq)), device_id_type=MESH
            )
        number = lax.broadcasted_iota(jnp.int32, (rows, capacity), 1).astype(F32)

        def term(i, carry):
            dest = lax.rem(i, nz) * ny + lax.rem(across.place + 1 + lax.div(i, nz), ny)
            places = []
            for e in range(experts):
                d_v[e * capacity : (e + 1) * capacity, :] = d_ref[e, dest]
                places.append((slot_ref[dest, :, e : e + 1] == number).astype(BF))
            terms_v[dest] = jnp.dot(
                jnp.concatenate(places, axis=1), d_v[...], preferred_element_type=F32
            ).astype(BF)
            return carry

        def prob_copy(peer, origin):
            return send_to(
                prob_ref.at[peer], prob_out.at[origin], prob_send.at[peer], prob_recv.at[origin], (dp, peer)
            )

        reduces = seq_reduces(terms_v, o_ref, scratch)
        lax.fori_loop(0, seq - nz, term, 0)
        pl.semaphore_wait(barrier, seq - 1)
        for step in range(1, seq):
            prob_copy(lax.rem(me + step, seq), me).start()
        for thunk in reduces[0].outward():
            thunk()
        lax.fori_loop(seq - nz, seq, term, 0)
        for thunk in reduces[1].outward():
            thunk()
        prob_out[me] = prob_ref[me]
        for thunk in woven(*[p.inward() for p in reduces]):
            thunk()
        for program in reduces:
            program.finish()
        for step in range(1, seq):
            prob_copy(lax.rem(me + step, seq), me).wait_send()
            source = lax.rem(me + seq - step, seq)
            prob_copy(source, source).wait_recv()

    vmem = pl.BlockSpec(memory_space=pltpu.VMEM)
    dma = pltpu.SemaphoreType.DMA
    return pl.pallas_call(
        kernel,
        out_shape=[
            jax.ShapeDtypeStruct((rows, width), F32),
            jax.ShapeDtypeStruct(prob_grads.shape, F32),
        ],
        in_specs=[vmem] * 3,
        out_specs=[vmem] * 2,
        scratch_shapes=[
            pltpu.VMEM((seq, rows, width), BF),
            pltpu.VMEM((experts * capacity, width), BF),
            dma((seq,)),
            dma((seq,)),
        ]
        + reduce_scratch(seq, rows, width),
        compiler_params=pltpu.CompilerParams(
            collective_id=collective_id, has_side_effects=True, vmem_limit_bytes=VMEM_MOST
        ),
        name="rows_back",
        cost_estimate=cost_of(90),
    )(drows.reshape(experts, seq, capacity, width), slot_cols, prob_grads)


def rms_factor(values):
    return lax.rsqrt(jnp.mean(values * values, axis=-1, keepdims=True) + NORM_EPS)


def norm_back(values, factor, gain_row, incoming):
    scaled = incoming * gain_row
    gain_part = jnp.sum(incoming * values * factor, axis=0)
    inner = jnp.mean(scaled * values, axis=-1, keepdims=True)
    return (factor * (scaled - values * factor * factor * inner), gain_part)


def local(
    tokens,
    segments,
    routes,
    cotangent,
    attn_weight,
    router_weight,
    norm_gains,
    expert_in,
    expert_out,
):
    num_seqs, local_len, width = tokens.shape
    seq_length = segments.shape[1]
    seq, ndp = lax.axis_size("seq"), lax.axis_size("dp")
    me = lax.axis_index("seq")
    devices = seq * ndp
    cols = HEADS // seq * HEAD_DIM
    tok = num_seqs * local_len
    group = tok * seq
    own_rows = attn_weight.shape[0]
    experts_all = router_weight.shape[1]
    experts = experts_all // seq
    top = routes.shape[-1]
    capacity = (9 * tok * top + 8 * experts_all - 1) // (8 * experts_all)

    n_router = own_rows * experts_all
    token_rows, cot_low = tokens.reshape(tok, width), cotangent.reshape(tok, width)
    (router_rows,) = (packed_rows([router_weight.reshape(1, -1)], 16)[0],)
    rank = lax.axis_index("dp") * seq + me
    gain_rows_own = lax.dynamic_update_slice(
        jnp.zeros((16, 128), BF), norm_gains, (0, lax.rem(rank, 128 // own_rows) * own_rows)
    )
    tables = rotary_tables(seq_length)
    ahead = tok * 10 // 256 * 16
    normed_all, cot_all, qkv_weight, proj_got, small_all, routes_all, raw, query_head, key_head, value_head, o_head, sums = (
        attend_first(
            token_rows,
            cot_low[:ahead],
            attn_weight[:, :3].reshape(own_rows, 3, seq, cols).transpose(2, 1, 0, 3),
            attn_weight[:, 3],
            jnp.concatenate([router_rows, gain_rows_own], axis=0),
            routes.reshape(-1, 128),
            tables,
            segments,
            router_rows.shape[0],
            1,
        )
    )
    expert_in, sums = lax.optimization_barrier((expert_in, sums))
    in_full = lax.all_gather(expert_in, "dp", axis=1, tiled=True)
    out_full = lax.all_gather(expert_out, "dp", axis=2, tiled=True)
    router_full = (
        small_all[:, : router_rows.shape[0]].reshape(devices, -1)[:, :n_router].reshape(width, experts_all)
    )
    gain_rows = (
        jnp.sum(
            small_all[:, router_rows.shape[0] : router_rows.shape[0] + 4]
            .reshape(width // 128, 128 // own_rows, 4, 128)
            .astype(F32),
            axis=1,
        )
        .transpose(1, 0, 2)
        .reshape(4, width)
    )
    routes_all = routes_all.reshape(seq, tok, top)
    proj_weight = proj_got.reshape(cols, width)
    resid_in = token_rows.astype(F32)
    factor_attn = rms_factor(resid_in)
    middle, ffn_low, ffn_all = middle_rows(o_head, proj_weight, token_rows, gain_rows[3:4], 5)
    factor_ffn = rms_factor(middle)

    slots = seq * capacity
    in_weight = in_full.transpose(0, 2, 1, 3)
    rows, gates, slot_cols, gate_cols = experts_dispatch(
        ffn_all, routes_all, router_full, me, experts, capacity
    )
    rows = rows.reshape(experts, slots, width)
    outputs, gate_in, up_in, hidden, cot_rest = experts_forward(rows, in_weight, out_full, cot_low[ahead:], 7)
    mixed_terms, output_grads, prob_grads = experts_mix(
        outputs, cot_all, cot_rest, gates, slot_cols, gate_cols
    )
    output_grads = output_grads.reshape(experts, slots, width)
    out_term = experts_out_terms(hidden, output_grads)
    expert_out_grad = lax.psum_scatter(out_term, "dp", scatter_dimension=2, tiled=True).astype(F32)
    out_term, output_grads = lax.optimization_barrier((out_term, output_grads))
    drows, in_term, mixed = experts_back(
        rows,
        output_grads,
        gate_in,
        up_in,
        in_weight,
        out_full,
        mixed_terms,
        8,
    )
    block_out = (middle + mixed).astype(BF).reshape(num_seqs, local_len, width)
    expert_in_grad = lax.psum_scatter(
        in_term.transpose(0, 2, 1, 3), "dp", scatter_dimension=1, tiled=True
    ).astype(F32)
    grad_ffn, grad_prob = rows_back(drows, slot_cols, prob_grads, 9)
    grad_prob = grad_prob.reshape(experts_all, tok).T

    route_probs = jax.nn.softmax(
        jnp.dot(ffn_low, router_full, preferred_element_type=F32), axis=-1
    )
    grad_logits = (
        route_probs * (grad_prob - jnp.sum(route_probs * grad_prob, axis=-1, keepdims=True))
    ).astype(BF)
    router_term = jnp.einsum("td,te->de", ffn_low, grad_logits, preferred_element_type=F32)
    grad_ffn = grad_ffn + jnp.einsum(
        "te,de->td", grad_logits, router_full, preferred_element_type=F32
    )
    grad_middle, gain_ffn = norm_back(middle, factor_ffn, gain_rows[3], grad_ffn)
    grad_middle = grad_middle + cot_low.astype(F32)

    head_gains = jnp.pad(lax.dynamic_slice(gain_rows, (1, me * cols), (2, cols)), ((0, 6), (0, 0)))
    grad_heads, proj_term, gain_heads = attend_back(
        grad_middle.astype(BF),
        proj_weight,
        o_head,
        query_head,
        key_head,
        value_head,
        raw,
        sums,
        head_gains,
        tables,
        segments,
        11,
    )

    grad_normed, qkv_out, proj_grad, total = last_sums(
        grad_heads,
        normed_all,
        qkv_weight,
        proj_term.reshape(ndp, own_rows, width),
        packed_rows([router_term.reshape(devices, -1)], 8),
        gain_heads,
        gain_ffn[None],
        gain_rows[0:1],
        14,
    )
    grad_resid, _ = norm_back(resid_in, factor_attn, gain_rows[0], grad_normed)
    input_grad = (grad_resid + grad_middle).reshape(num_seqs, local_len, width)
    qkv_grad = qkv_out.reshape(seq, 3, own_rows, cols).transpose(2, 1, 0, 3).reshape(own_rows, 3, width)
    attn_grad = jnp.concatenate([qkv_grad, proj_grad[:, None, :]], axis=1).astype(F32)
    gain_at = total.shape[0] - 8
    router_grad = total[:gain_at].reshape(-1)[:n_router].reshape(own_rows, experts_all)
    gain_grad = lax.dynamic_slice(
        total, (gain_at, lax.rem(rank, 128 // own_rows) * own_rows), (4, own_rows)
    )
    return (
        block_out,
        input_grad,
        attn_grad,
        router_grad,
        gain_grad,
        expert_in_grad,
        expert_out_grad,
    )


def solution(mesh):
    in_specs = (
        P("dp", "seq", None),
        P("dp", None),
        P("dp", "seq", None),
        P("dp", "seq", None),
        P(("dp", "seq"), None, None),
        P(("dp", "seq"), None),
        P(None, ("dp", "seq")),
        P("seq", "dp", None, None),
        P("seq", None, "dp"),
    )
    out_specs = (
        P("dp", "seq", None),
        P("dp", "seq", None),
        P(("dp", "seq"), None, None),
        P(("dp", "seq"), None),
        P(None, ("dp", "seq")),
        P("seq", "dp", None, None),
        P("seq", None, "dp"),
    )
    return jax.shard_map(local, mesh=mesh, in_specs=in_specs, out_specs=out_specs, check_vma=False)
```
